32 devices in a mesh: row: 16 (over z, y, core), col: 2 (over x).
Axes of the slice: x: 2, y: 2, z: 4, core: 2. Of those that a mesh axis runs over, the one named last changes fastest.
Arguments:
- states: float32 [16384, 768], P(('row', 'col')), may hold values from -6 to 6
- upstream: float32 [16384, 768], P(('row', 'col')), may hold values from -6 to 6
- teacher: float32 [16384, 768], P(('row', 'col')), may hold values from -6 to 6
- validity: int32 [16384], P(('row', 'col')), may hold values from 0 to 1, as said below
- picture_start: int32 [32, 2], P(('row', 'col')), may hold values from 0 to 256, as said below
- first_gain: float32 [768], replicated, may hold values from 0.5 to 1.5
- query_weight: bfloat16 [768, 768], P('row', 'col'), may hold values from -0.21875 to 0.21875
- key_weight: bfloat16 [768, 768], P('row', 'col'), may hold values from -0.21875 to 0.21875
- value_weight: bfloat16 [768, 768], P('row', 'col'), may hold values from -0.21875 to 0.21875
- premix: float32 [12, 12], replicated, may hold values from -3 to 3
- postmix: float32 [12, 12], replicated, may hold values from -3 to 3
- output_weight: bfloat16 [768, 768], P('row', 'col'), may hold values from -0.875 to 0.875
- second_gain: float32 [768], replicated, may hold values from 0.5 to 1.5
- up_weight: bfloat16 [768, 3072], P('row', 'col'), may hold values from -0.21875 to 0.21875
- down_weight: bfloat16 [3072, 768], P('col', 'row'), may hold values from -0.109375 to 0.109375
Outputs:
- layer_out: float32 [16384, 768], P(('row', 'col'))
- distill_loss: float32 [], replicated
- task_loss: float32 [], replicated
- input_grad: float32 [16384, 768], P(('row', 'col'))
- first_grad: float32 [768], replicated
- query_grad: float32 [768, 768], P('row', 'col')
- key_grad: float32 [768, 768], P('row', 'col')
- value_grad: float32 [768, 768], P('row', 'col')
- premix_grad: float32 [12, 12], replicated
- postmix_grad: float32 [12, 12], replicated
- output_grad: float32 [768, 768], P('row', 'col')
- second_grad: float32 [768], replicated
- up_grad: float32 [768, 3072], P('row', 'col')
- down_grad: float32 [3072, 768], P('col', 'row')
The draws below stay inside these ranges and needn't reach their ends.
Inputs may be any that keep to these rules, and one draw needn't show every extreme that they name: `validity`: the first token of every sequence is valid. `picture_start`: row s holds the starts of sequence s's two picture spans of 256 positions; the first span lies within positions 0 to 255, the second within 256 to 511.
All inputs are finite; a program needn't handle non-finite values.
Results may differ from the reference program's by a relative error of at most 0.03.
The reference program's roundings to bfloat16 on the way count: a program that leaves them out, or rounds other values in their place, can miss the bound.
Values may be sent and summed in bfloat16 or wider, within the bound.
No kernel may reach another device: no remote copies, remote signals or barrier semaphores. Data moves between devices by JAX's collectives and lax.ppermute only.
A program may use at most 256 MiB of HBM per device.

```python
import jax
import jax.numpy as jnp
from jax import lax

HEADS = 12
HEAD_DIM = 64
FF = 3072
SEQ = 512
PIC = 256
D = 768
SEQS = 32
TOKENS = 16384


def draw_validity(key, part):
    positions = jnp.arange(TOKENS, dtype=jnp.int32)
    limits = 300 + 600 * positions // TOKENS
    random_rolls = jax.random.randint(key, (TOKENS,), 0, 1000, dtype=jnp.int32)
    valid_marks = (random_rolls < limits) | (positions % SEQ == 0)
    return valid_marks.astype(jnp.int32)


def draw_picture_start(key, part):
    halves = SEQ // 2
    sequence_index = jnp.arange(SEQS, dtype=jnp.int32)
    first_start = jax.random.randint(jax.random.fold_in(key, 1), (SEQS,), 0, halves - PIC + 1, dtype=jnp.int32)
    second_start = halves + jax.random.randint(jax.random.fold_in(key, 2), (SEQS,), 0, halves - PIC + 1, dtype=jnp.int32)
    first_start = jnp.where(sequence_index == 0, 0, first_start)
    second_start = jnp.where(sequence_index == SEQS - 1, SEQ - PIC, second_start)
    return jnp.stack([first_start, second_start], axis=1).astype(jnp.int32)


def block_scale(key, shape, cuts, smallest, top_value):
    loudness = 1.0
    for dim, blocks in cuts:
        draws = jax.random.uniform(jax.random.fold_in(jax.random.fold_in(key, 6), dim), (blocks,), jnp.float32, smallest / len(cuts), top_value / len(cuts))
        loudness = loudness * jnp.repeat(jnp.exp(draws), shape[dim] // blocks).reshape((-1,) + (1,) * (len(shape) - 1 - dim))
    return loudness


def gaussian(own_key, extent, width, limit, split=(), held_as=jnp.bfloat16):
    gain = block_scale(own_key, extent, split, -0.22, 0.18) if split else 1.0
    array = jax.random.normal(own_key, extent, jnp.float32) * width * gain
    return jnp.minimum(jnp.maximum(array, -limit), limit).astype(held_as)


def setup_inputs(seed: int = 0) -> dict:
    streams_of = jax.random.split(jax.random.key(seed), 16)
    return {
        "states": gaussian(streams_of[0], (TOKENS, D), 1.0, 6.0, ((0, 32),), jnp.float32),
        "upstream": gaussian(streams_of[1], (TOKENS, D), 1.0, 6.0, ((0, 32),), jnp.float32),
        "teacher": gaussian(streams_of[2], (TOKENS, D), 1.0, 6.0, ((0, 32),), jnp.float32),
        "validity": draw_validity(jax.random.fold_in(streams_of[15], 71), 0),
        "picture_start": draw_picture_start(jax.random.fold_in(streams_of[15], 71), 0),
        "first_gain": jnp.clip(1.0 + 0.1 * jax.random.normal(streams_of[5], (D,), jnp.float32), 0.5, 1.5),
        "query_weight": gaussian(streams_of[6], (D, D), D ** -0.5, 0.21875, ((0, 16), (1, 2))),
        "key_weight": gaussian(streams_of[7], (D, D), D ** -0.5, 0.21875, ((0, 16), (1, 2))),
        "value_weight": gaussian(streams_of[8], (D, D), D ** -0.5, 0.21875, ((0, 16), (1, 2))),
        "premix": gaussian(streams_of[9], (HEADS, HEADS), 0.5, 3.0, (), jnp.float32),
        "postmix": gaussian(streams_of[10], (HEADS, HEADS), 0.5, 3.0, (), jnp.float32),
        "output_weight": gaussian(streams_of[11], (D, D), (D // 16) ** -0.5, 0.875, ((0, 16), (1, 2))),
        "second_gain": jnp.clip(1.0 + 0.1 * jax.random.normal(streams_of[12], (D,), jnp.float32), 0.5, 1.5),
        "up_weight": gaussian(streams_of[13], (D, FF), D ** -0.5, 0.21875, ((0, 16), (1, 2))),
        "down_weight": gaussian(streams_of[14], (FF, D), FF ** -0.5, 0.109375, ((0, 2), (1, 16))),
    }


@jax.custom_vjp
def low(v):
    return lax.optimization_barrier(v.astype(jnp.bfloat16)).astype(jnp.float32)

@jax.custom_vjp
def low_back(v):
    return v

def low_keep(v):
    return (low(v), None)

def low_pass(kept, grad):
    return (grad,)

def back_keep(v):
    return (v, None)

def back_low(kept, grad):
    return (low(grad),)
low.defvjp(low_keep, low_pass)
low_back.defvjp(back_keep, back_low)
EPSILON = 1e-06
HIGHEST = lax.Precision.HIGHEST

def permitted(positions, columns, starts):
    causal = columns[None, :] <= positions[:, None]
    first_rows = (positions >= starts[0]) & (positions < starts[0] + PIC)
    first_cols = (columns >= starts[0]) & (columns < starts[0] + PIC)
    second_rows = (positions >= starts[1]) & (positions < starts[1] + PIC)
    second_cols = (columns >= starts[1]) & (columns < starts[1] + PIC)
    return causal | first_rows[:, None] & first_cols[None, :] | second_rows[:, None] & second_cols[None, :]

def inverse_rms(values):
    return lax.rsqrt(lax.optimization_barrier(jnp.mean(values * values, axis=-1, keepdims=True)) + EPSILON)

def matmul(left_side, other_side):
    return jnp.dot(left_side, other_side, preferred_element_type=jnp.float32, precision=HIGHEST)

def attention(queries, keys_all, values_all, premix, postmix, starts):
    seq_len = queries.shape[0]
    block_rows = min(512, seq_len)
    block_total = seq_len // block_rows
    factor_scale = HEAD_DIM ** (-0.5)
    columns = jnp.arange(seq_len, dtype=jnp.int32)

    def one_block(scan_item):
        query_block, offset = scan_item
        positions = offset + jnp.arange(block_rows, dtype=jnp.int32)
        scores = low_back(jnp.einsum('qgd,kgd->gqk', query_block, keys_all, precision=HIGHEST) * factor_scale)
        mixed_scores = jnp.einsum('gh,gqk->hqk', premix, scores, precision=HIGHEST)
        mixed_scores = jnp.where(permitted(positions, columns, starts)[None], mixed_scores, -1e+30)
        highest = lax.optimization_barrier(jnp.max(mixed_scores, axis=-1, keepdims=True))
        exp_terms = jnp.exp(mixed_scores - highest)
        softmax_probs = exp_terms / lax.optimization_barrier(jnp.sum(exp_terms, axis=-1, keepdims=True))
        weights = low(jnp.einsum('hg,hqk->gqk', postmix, softmax_probs, precision=HIGHEST))
        return jnp.einsum('gqk,kgd->qgd', weights, values_all, precision=HIGHEST)
    blocks = queries.reshape(block_total, block_rows, HEADS, HEAD_DIM)
    offsets = jnp.arange(block_total, dtype=jnp.int32) * block_rows
    result = lax.map(jax.checkpoint(one_block), (blocks, offsets))
    return result.reshape(seq_len, HEADS * HEAD_DIM)

def layer(params, states, starts):
    first_gain, query_weight, key_weight, value_weight, premix, postmix, output_weight, second_gain, up_weight, down_weight = params
    seq_len = states.shape[0]
    normed = low(states * inverse_rms(states) * first_gain)
    queries = low_back(low(matmul(normed, query_weight))).reshape(seq_len, HEADS, HEAD_DIM)
    keys_all = low_back(low(matmul(normed, key_weight))).reshape(seq_len, HEADS, HEAD_DIM)
    values_all = low_back(low(matmul(normed, value_weight))).reshape(seq_len, HEADS, HEAD_DIM)
    attended = low_back(low(attention(queries, keys_all, values_all, premix, postmix, starts)))
    middle = states + low_back(matmul(attended, output_weight))
    normed_two = low(middle * inverse_rms(middle) * second_gain)
    hidden_pre = low_back(matmul(normed_two, up_weight))
    hidden = low(jnp.maximum(hidden_pre, 0.0))
    return middle + low_back(matmul(hidden, down_weight))

def reference(states, upstream, teacher, validity, picture_start, first_gain, query_weight, key_weight, value_weight, premix, postmix, output_weight, second_gain, up_weight, down_weight):
    params = (first_gain, query_weight.astype(jnp.float32), key_weight.astype(jnp.float32), value_weight.astype(jnp.float32), premix, postmix, output_weight.astype(jnp.float32), second_gain, up_weight.astype(jnp.float32), down_weight.astype(jnp.float32))
    valid_marks = validity.astype(jnp.float32)
    total_valid = jnp.sum(valid_marks)
    factor = TOKENS / total_valid
    scan_items = (states.reshape(SEQS, SEQ, D), upstream.reshape(SEQS, SEQ, D), teacher.reshape(SEQS, SEQ, D), valid_marks.reshape(SEQS, SEQ), picture_start)
    zero_grads = jax.tree.map(jnp.zeros_like, params)
    zero_value = jnp.zeros((), jnp.float32)

    def step(carried, scan_item):
        totals, distance, linear = carried
        seq_states, seq_upstream, seq_teacher, seq_valid, starts = scan_item
        outputs, pullback = jax.vjp(lambda weights_tuple, inputs: layer(weights_tuple, inputs, starts), params, seq_states)
        differ = outputs - seq_teacher
        distance = distance + jnp.sum(seq_valid * lax.optimization_barrier(jnp.sum(differ * differ, axis=1)))
        linear = linear + jnp.sum(seq_valid * lax.optimization_barrier(jnp.sum(seq_upstream * outputs, axis=1)))
        grad_out = factor * seq_valid[:, None] * (seq_upstream + differ)
        param_grads, input_grads = pullback(grad_out)
        totals = jax.tree.map(lambda first_term, other_term: first_term + other_term, totals, param_grads)
        return ((totals, distance, linear), (outputs, input_grads))
    (totals, distance, linear), (outputs, input_grads) = lax.scan(step, (zero_grads, zero_value, zero_value), scan_items)
    return (outputs.reshape(TOKENS, D), distance / (total_valid * D), linear / total_valid, input_grads.reshape(TOKENS, D), totals[0], totals[1], totals[2], totals[3], totals[4], totals[5], totals[6], totals[7], totals[8], totals[9])
```

```python
import functools

import jax
import jax.numpy as jnp
from jax import lax
from jax.experimental import pallas as pl
from jax.experimental.pallas import tpu as pltpu
from jax.sharding import PartitionSpec as P

HEADS = 12
HEAD_DIM = 64
PIC = 256
EPSILON = 1e-06
F32 = jnp.float32
BF16 = jnp.bfloat16
AXES = ("row", "col")
X_BIT, CORE_BIT, Y_BIT, Z_BIT = 1, 2, 4, 8
PLANE = (X_BIT, Y_BIT, X_BIT | Y_BIT)
LINE = (Z_BIT, 2 * Z_BIT, 3 * Z_BIT)
EXTRA = 128
PARAMS = pltpu.CompilerParams(vmem_limit_bytes=60000 * 1024)
SMEM = pl.BlockSpec(memory_space=pltpu.SMEM)
ANY = pl.BlockSpec(memory_space=pl.ANY)
VMEM = pl.BlockSpec(memory_space=pltpu.VMEM)


def dot(a, b):
    return lax.dot_general(a, b, (((1,), (0,)), ((), ())), preferred_element_type=F32)


def dot_nt(a, b):
    return lax.dot_general(a, b, (((1,), (1,)), ((), ())), preferred_element_type=F32)


def place_copies(spot, pieces, wholes, rows_at, cols_at, widths, sems):
    if len(pieces) == len(wholes):
        return [
            pltpu.make_async_copy(piece, whole, sems.at[n])
            for n, (piece, whole) in enumerate(zip(pieces, wholes))
        ]
    copies = []
    for k, piece in enumerate(pieces):
        core, y, x = k // 4, (k // 2) % 2, k % 2
        for z in range(4):
            r = ((spot[0] ^ z) * 2 + (spot[1] ^ y)) * 2 + (spot[2] ^ core)
            c = spot[3] ^ x
            for whole, row, col, width in zip(wholes, rows_at, cols_at, widths):
                depth = whole.shape[0] // 16
                copies.append(
                    pltpu.make_async_copy(
                        piece.at[z, pl.ds(row, depth), pl.ds(col, width)],
                        whole.at[
                            pl.ds(pl.multiple_of(r * depth, 16), depth),
                            pl.ds(pl.multiple_of(c * width, 128), width),
                        ],
                        sems.at[len(copies)],
                    )
                )
    return copies


def send_copies(spot, source, keep, send, row, half, col, width, sems):
    depth = source.shape[0] // 16
    copies = []
    for j in range(8):
        z, y = j // 2, j % 2
        plane = (spot[1] ^ y) * 2 + (spot[3] ^ half)
        for n, (target, core) in enumerate(((keep, spot[2]), (send, 1 - spot[2]))):
            start = pl.multiple_of((2 * j + core) * depth, 16)
            copies.append(
                pltpu.make_async_copy(
                    source.at[pl.ds(start, depth), pl.ds(0, width)],
                    target.at[plane, spot[0] ^ z, pl.ds(row, depth), pl.ds(col, width)],
                    sems.at[2 * j + n],
                )
            )
    return copies


def attend_kernel(blocks, spot, starts, normed_ref, *rest):
    pieces, rest = rest[:blocks], rest[blocks:]
    pm_ref, po_ref, q_ref, k_ref, v_ref, out_ref, p_ref, wq, wk, wv, kt, bias, acc, sems = rest
    step = pl.program_id(0)
    half = normed_ref.shape[0] // 2

    @pl.when(step == 0)
    def _():
        width = wq.shape[1] // 2
        depth = wq.shape[0] // 16
        copies = place_copies(
            spot, pieces, (wq, wk, wv), (0, depth, 2 * depth), (0, 0, 0), (width,) * 3, sems
        )
        for copy in copies:
            copy.start()
        rows = lax.broadcasted_iota(jnp.int32, (half, half), 0)
        cols = lax.broadcasted_iota(jnp.int32, (half, half), 1)
        for b in range(2):
            i, j = rows + b * half, cols + b * half
            ok = j <= i
            for s in range(2):
                p = starts[0, s]
                ok = ok | ((i >= p) & (i < p + PIC) & (j >= p) & (j < p + PIC))
            bias[b] = jnp.where(ok, 0.0, -1e30)
        acc[...] = jnp.zeros_like(acc)
        for copy in copies:
            copy.wait()
        k_ref[...] = dot(normed_ref[...], wk[...]).astype(BF16)
        kt[...] = k_ref[...].T
        q_ref[...] = dot(normed_ref[...], wq[...]).astype(BF16)
        v_ref[...] = dot(normed_ref[...], wv[...]).astype(BF16)

    pm = pm_ref[0]
    po = po_ref[0]
    vs = (v_ref[...].astype(F32) * po).astype(BF16)
    top = (q_ref[:half].astype(F32) * pm).astype(BF16)
    low = (q_ref[half:].astype(F32) * pm).astype(BF16)
    s0 = dot(top, kt[:, :half]) + bias[0]
    s1 = dot(low, kt[:, :half])
    s2 = dot(low, kt[:, half:]) + bias[1]
    m0 = jnp.max(s0, axis=1, keepdims=True)
    e0 = jnp.exp(s0 - m0)
    p0 = (e0 / jnp.sum(e0, axis=1, keepdims=True)).astype(BF16)
    m1 = jnp.maximum(jnp.max(s1, axis=1, keepdims=True), jnp.max(s2, axis=1, keepdims=True))
    e1 = jnp.exp(s1 - m1)
    e2 = jnp.exp(s2 - m1)
    inv = 1.0 / (jnp.sum(e1, axis=1, keepdims=True) + jnp.sum(e2, axis=1, keepdims=True))
    p1 = (e1 * inv).astype(BF16)
    p2 = (e2 * inv).astype(BF16)
    p_ref[0, :, :half] = p0
    p_ref[0, :, half : 2 * half] = p1
    p_ref[0, :, 2 * half :] = p2
    acc[:half] += dot(p0, vs[:half])
    acc[half:] += dot(p1, vs[:half]) + dot(p2, vs[half:])

    @pl.when(step == HEADS - 1)
    def _():
        out_ref[...] = acc[...].astype(BF16)


def attend(spot, starts, normed, pieces, pm, po):
    seq, width = normed.shape
    half = seq // 2
    whole = pl.BlockSpec((seq, width), lambda h: (0, 0))
    row = pl.BlockSpec((1, 1, width), lambda h: (h, 0, 0))
    low = jax.ShapeDtypeStruct((seq, width), BF16)
    return pl.pallas_call(
        functools.partial(attend_kernel, len(pieces)),
        grid=(HEADS,),
        in_specs=[SMEM, SMEM, whole] + [ANY] * len(pieces) + [row, row],
        out_specs=[whole] * 4 + [pl.BlockSpec((1, half, 3 * half), lambda h: (h, 0, 0))],
        out_shape=[low] * 4 + [jax.ShapeDtypeStruct((HEADS, half, 3 * half), BF16)],
        scratch_shapes=[pltpu.VMEM((width, width), BF16)] * 3
        + [
            pltpu.VMEM((width, seq), BF16),
            pltpu.VMEM((2, half, half), F32),
            pltpu.VMEM((seq, width), F32),
            pltpu.SemaphoreType.DMA((96,)),
        ],
        compiler_params=PARAMS,
        name="attend",
    )(spot, starts, normed, *pieces, pm, po)


def middle_kernel(blocks, outs, spot, factor, *rest):
    pieces, rest = rest[:blocks], rest[blocks:]
    att_ref, states_ref, up_ref, teach_ref, valid_ref, gain_ref = rest[:6]
    layer_ref, mid_ref, agrad_ref, sums_ref = rest[6:10]
    grads, rest = rest[10 : 10 + outs], rest[10 + outs :]
    wo, wu, wd, hidden, pre, n2t, olt, slots, sems, out_sems = rest
    seq, width = att_ref.shape
    units = wu.shape[1]
    blocked = blocks == 8
    copies = place_copies(
        spot,
        pieces,
        (wo, wu, wd),
        (0, 0, 0),
        (units, 0, units // 2),
        (width // 2, units // 2, units // 2),
        sems,
    )
    for copy in copies:
        copy.start()
    for n, copy in enumerate(copies):
        if n % 3 == 0:
            copy.wait()
    mid_ref[...] = states_ref[...] + dot(att_ref[...], wo[...])
    middle = mid_ref[...]
    scale = lax.rsqrt(jnp.mean(middle * middle, axis=1, keepdims=True) + EPSILON)
    n2 = (middle * scale * gain_ref[...]).astype(BF16)
    n2t[...] = n2.T
    for n, copy in enumerate(copies):
        if n % 3 != 0:
            copy.wait()

    chunk = 512
    steps = units // chunk

    def up_step(j, _):
        at = pl.ds(pl.multiple_of(j * chunk, chunk), chunk)
        hidden[:, at] = jnp.maximum(dot(n2, wu[:, at]), 0.0).astype(BF16)
        return 0

    lax.fori_loop(0, steps, up_step, 0)
    layer_ref[...] = mid_ref[...] + dot_nt(hidden[...], wd[...])
    layer = layer_ref[...]
    valid = valid_ref[...].astype(F32)
    upstream = up_ref[...]
    differ = layer - teach_ref[...]
    sums_ref[1:2, :] = jnp.sum(valid * (differ * differ), axis=0, keepdims=True)
    sums_ref[2:3, :] = jnp.sum(valid * (upstream * layer), axis=0, keepdims=True)
    out_grad = (factor[0, 0] * valid) * (upstream + differ)
    out_low = out_grad.astype(BF16)
    olt[...] = out_low.T

    def down_step(j, _):
        at = pl.ds(pl.multiple_of(j * chunk, chunk), chunk)
        part = hidden[:, at]
        back = jnp.where(part > 0, dot(out_low, wd[:, at]), 0.0).astype(BF16)
        pre[:, at] = back
        for which, (left, right) in enumerate(((n2t, back), (olt, part))):
            slot = slots.at[which]

            @pl.when(j > 0)
            def _():
                for copy in grad_copies(which, j - 1):
                    copy.wait()

            slot[...] = dot(left[...], right).astype(BF16)
            for copy in grad_copies(which, j):
                copy.start()
        return 0

    def grad_copies(which, j):
        if not blocked:
            at = pl.ds(pl.multiple_of(j * chunk, chunk), chunk)
            return [pltpu.make_async_copy(slots.at[which], grads[which].at[:, at], out_sems.at[which, 0])]
        per = steps // 2
        return send_copies(
            spot,
            slots.at[which],
            grads[0],
            grads[1],
            0,
            j // per,
            pl.multiple_of(which * (units // 2) + (j % per) * chunk, 128),
            chunk,
            out_sems.at[which],
        )

    lax.fori_loop(0, steps, down_step, 0)
    grad = dot_nt(pre[...], wu[...])
    middle = mid_ref[...]
    scale = lax.rsqrt(jnp.mean(middle * middle, axis=1, keepdims=True) + EPSILON)
    sums_ref[0:1, :] = jnp.sum(grad * middle * scale, axis=0, keepdims=True)
    term = gain_ref[...] * grad
    inner = jnp.mean(term * middle, axis=1, keepdims=True)
    layer = layer_ref[...]
    out_grad = (factor[0, 0] * valid_ref[...].astype(F32)) * (
        up_ref[...] + (layer - teach_ref[...])
    )
    mid_grad = out_grad + scale * term - middle * (scale * scale * scale) * inner
    mid_ref[...] = mid_grad
    branch = mid_grad.astype(BF16)
    agrad_ref[...] = dot_nt(branch, wo[...]).astype(BF16)
    n2t[...] = att_ref[...].T
    for which in range(2):
        for copy in grad_copies(which, steps - 1):
            copy.wait()
    half = width // 2
    last = []
    for c in range(2):
        slots[c, :, :half] = dot(n2t[...], branch[:, c * half : (c + 1) * half]).astype(BF16)
        if blocked:
            made = send_copies(
                spot, slots.at[c], grads[0], grads[1], 0, c, units, half, out_sems.at[c]
            )
        else:
            made = [
                pltpu.make_async_copy(
                    slots.at[c, :, pl.ds(0, half)],
                    grads[2].at[:, pl.ds(c * half, half)],
                    out_sems.at[c, 0],
                )
            ]
        for copy in made:
            copy.start()
        last += made
    for copy in last:
        copy.wait()


def middle_block(spot, factor, pieces, attended, states, upstream, teacher, valid, gain, units):
    seq, width = attended.shape
    full = jax.ShapeDtypeStruct((seq, width), F32)
    if len(pieces) == 8:
        depth = width // 16
        grads = [jax.ShapeDtypeStruct((4, 4, depth, units + width // 2), BF16)] * 2
    else:
        grads = [
            jax.ShapeDtypeStruct((width, units), BF16),
            jax.ShapeDtypeStruct((width, units), BF16),
            jax.ShapeDtypeStruct((width, width), BF16),
        ]
    return pl.pallas_call(
        functools.partial(middle_kernel, len(pieces), len(grads)),
        in_specs=[SMEM, SMEM] + [ANY] * len(pieces) + [VMEM] * 6,
        out_specs=[VMEM] * 4 + [ANY] * len(grads),
        out_shape=[
            full,
            full,
            jax.ShapeDtypeStruct((seq, width), BF16),
            jax.ShapeDtypeStruct((8, width), F32),
        ]
        + grads,
        scratch_shapes=[
            pltpu.VMEM((width, width), BF16),
            pltpu.VMEM((width, units), BF16),
            pltpu.VMEM((width, units), BF16),
            pltpu.VMEM((seq, units), BF16),
            pltpu.VMEM((seq, units), BF16),
            pltpu.VMEM((width, seq), BF16),
            pltpu.VMEM((width, seq), BF16),
            pltpu.VMEM((2, width, 512), BF16),
            pltpu.SemaphoreType.DMA((96,)),
            pltpu.SemaphoreType.DMA((2, 16)),
        ],
        compiler_params=PARAMS,
        name="middle",
    )(spot, factor, *pieces, attended, states, upstream, teacher, valid, gain)


def attend_back_kernel(
    blocked, spot, pms, pos, nt_ref, q_ref, k_ref, v_ref, g_ref, p_ref, pm_ref, po_ref,
    dq_ref, dk_ref, dv_ref, pre_ref, post_ref, *rest,
):
    outs = 2 if blocked else 3
    grads = rest[:outs]
    vt, qt, gt, dq, dkt, dvt, slots, sems = rest[outs:]
    step = pl.program_id(0)
    seq, width = q_ref.shape
    half = seq // 2

    @pl.when(step == 0)
    def _():
        vt[...] = v_ref[...].T
        qt[...] = q_ref[...].T
        gt[...] = g_ref[...].T
        dq[...] = jnp.zeros_like(dq)
        dkt[...] = jnp.zeros_like(dkt)
        dvt[...] = jnp.zeros_like(dvt)

    pm = pm_ref[0]
    po = po_ref[0]
    p0, p1, p2 = (p_ref[0, :, b * half : (b + 1) * half] for b in range(3))
    top = (g_ref[:half].astype(F32) * po).astype(BF16)
    low = (g_ref[half:].astype(F32) * po).astype(BF16)
    g0 = dot(top, vt[:, :half])
    g1 = dot(low, vt[:, :half])
    g2 = dot(low, vt[:, half:])
    u0 = dot(gt[:, :half], p0) + dot(gt[:, half:], p1)
    u1 = dot(gt[:, half:], p2)
    f0, f1, f2 = p0.astype(F32), p1.astype(F32), p2.astype(F32)
    t0 = f0 * g0
    d0 = (t0 - f0 * jnp.sum(t0, axis=1, keepdims=True)).astype(BF16)
    t1, t2 = f1 * g1, f2 * g2
    r1 = jnp.sum(t1, axis=1, keepdims=True) + jnp.sum(t2, axis=1, keepdims=True)
    d1 = (t1 - f1 * r1).astype(BF16)
    d2 = (t2 - f2 * r1).astype(BF16)
    w0 = dot(d0, k_ref[:half])
    w1 = dot(d1, k_ref[:half]) + dot(d2, k_ref[half:])
    dq[:half] += pm * w0
    dq[half:] += pm * w1
    pre_ref[0] = jnp.sum(q_ref[:half].astype(F32) * w0, axis=0, keepdims=True) + jnp.sum(
        q_ref[half:].astype(F32) * w1, axis=0, keepdims=True
    )
    for g in range(HEADS):
        at = slice(g * HEAD_DIM, (g + 1) * HEAD_DIM)
        b = pos[step, g]
        u0g, u1g = u0[at], u1[at]
        dvt[at, :half] += b * u0g
        dvt[at, half:] += b * u1g
        both = u0g * vt[at, :half].astype(F32) + u1g * vt[at, half:].astype(F32)
        post_ref[0, g : g + 1, :] = jnp.sum(both, axis=0, keepdims=True)
    qs = jnp.concatenate(
        [
            (qt[g * HEAD_DIM : (g + 1) * HEAD_DIM].astype(F32) * pms[step, g]).astype(BF16)
            for g in range(HEADS)
        ],
        axis=0,
    )
    dkt[:, :half] += dot(qs[:, :half], d0) + dot(qs[:, half:], d1)
    dkt[:, half:] += dot(qs[:, half:], d2)

    @pl.when(step == HEADS - 1)
    def _():
        dq_ref[...] = dq[...].astype(BF16)
        dk_ref[...] = dkt[...].astype(BF16).T
        dv_ref[...] = dvt[...].astype(BF16).T
        made = []
        for n, ref in enumerate((dq_ref, dk_ref, dv_ref)):
            slots[n] = dot(nt_ref[...], ref[...]).astype(BF16)
            if blocked:
                part = width // 2
                for c in range(2):
                    made += send_copies(
                        spot,
                        slots.at[n, :, pl.ds(c * part, part)],
                        grads[0],
                        grads[1],
                        n * (width // 16),
                        c,
                        0,
                        part,
                        sems.at[2 * n + c],
                    )
            else:
                made.append(pltpu.make_async_copy(slots.at[n], grads[n], sems.at[n, 0]))
            for copy in made[-32 if blocked else -1 :]:
                copy.start()
        for copy in made:
            copy.wait()


def attend_back(spot, blocked, nt, q, k, v, g, p, pm, po, pms, pos):
    seq, width = q.shape
    half = seq // 2
    whole = pl.BlockSpec((seq, width), lambda h: (0, 0))
    row = pl.BlockSpec((1, 1, width), lambda h: (h, 0, 0))
    low = jax.ShapeDtypeStruct((seq, width), BF16)
    if blocked:
        grads = [jax.ShapeDtypeStruct((4, 4, 3 * (width // 16), width // 2), BF16)] * 2
    else:
        grads = [jax.ShapeDtypeStruct((width, width), BF16)] * 3
    return pl.pallas_call(
        functools.partial(attend_back_kernel, blocked),
        grid=(HEADS,),
        in_specs=[SMEM, SMEM, SMEM, pl.BlockSpec((width, seq), lambda h: (0, 0))]
        + [whole] * 4
        + [pl.BlockSpec((1, half, 3 * half), lambda h: (h, 0, 0)), row, row],
        out_specs=[whole] * 3
        + [row, pl.BlockSpec((1, HEADS, half), lambda h: (h, 0, 0))]
        + [ANY] * len(grads),
        out_shape=[low] * 3
        + [
            jax.ShapeDtypeStruct((HEADS, 1, width), F32),
            jax.ShapeDtypeStruct((HEADS, HEADS, half), F32),
        ]
        + grads,
        scratch_shapes=[pltpu.VMEM((width, seq), BF16)] * 3
        + [
            pltpu.VMEM((seq, width), F32),
            pltpu.VMEM((width, seq), F32),
            pltpu.VMEM((width, seq), F32),
            pltpu.VMEM((3, width, width), BF16),
            pltpu.SemaphoreType.DMA((6, 16)),
        ],
        compiler_params=PARAMS,
        name="attend_back",
    )(spot, pms, pos, nt, q, k, v, g, p, pm, po)


def input_kernel(blocks, spot, *rest):
    pieces, rest = rest[:blocks], rest[blocks:]
    dq_ref, dk_ref, dv_ref, states_ref, mid_ref, gain_ref, out_ref, first_ref = rest[:8]
    wq, wk, wv, sems = rest[8:]
    width = wq.shape[1] // 2
    depth = wq.shape[0] // 16
    copies = place_copies(
        spot, pieces, (wq, wk, wv), (0, depth, 2 * depth), (0, 0, 0), (width,) * 3, sems
    )
    for copy in copies:
        copy.start()
    states = states_ref[...]
    scale = lax.rsqrt(jnp.mean(states * states, axis=1, keepdims=True) + EPSILON)
    for copy in copies:
        copy.wait()
    grad = (
        dot_nt(dq_ref[...], wq[...]) + dot_nt(dk_ref[...], wk[...]) + dot_nt(dv_ref[...], wv[...])
    )
    first_ref[...] = jnp.broadcast_to(
        jnp.sum(grad * states * scale, axis=0, keepdims=True), first_ref.shape
    )
    term = gain_ref[...] * grad
    inner = jnp.mean(term * states, axis=1, keepdims=True)
    out_ref[...] = mid_ref[...] + scale * term - states * (scale * scale * scale) * inner


def input_block(spot, pieces, dq, dk, dv, states, mid_grad, gain):
    seq, width = dq.shape
    return pl.pallas_call(
        functools.partial(input_kernel, len(pieces)),
        in_specs=[SMEM] + [ANY] * len(pieces) + [VMEM] * 6,
        out_specs=[VMEM] * 2,
        out_shape=[
            jax.ShapeDtypeStruct((seq, width), F32),
            jax.ShapeDtypeStruct((8, width), F32),
        ],
        scratch_shapes=[pltpu.VMEM((width, width), BF16)] * 3 + [pltpu.SemaphoreType.DMA((96,))],
        compiler_params=PARAMS,
        name="input_grad",
    )(spot, *pieces, dq, dk, dv, states, mid_grad, gain)


def exchange(value, mask, total):
    return lax.ppermute(value, AXES, [(i, i ^ mask) for i in range(total)])


def gather_blocks(packet, total):
    line = jnp.stack([packet] + [exchange(packet, m, total) for m in LINE])
    plane = [line] + [exchange(line, m, total) for m in PLANE]
    return plane + [exchange(part, CORE_BIT, total) for part in plane]


def add_low(*terms):
    return functools.reduce(jnp.add, [t.astype(F32) for t in terms])


def reduce_blocks(keep, send, total):
    other = exchange(send, CORE_BIT, total)
    away = [
        exchange(add_low(keep[k], other[k]).astype(BF16), m, total) for k, m in enumerate(PLANE, 1)
    ]
    line = add_low(keep[0], other[0], *away)
    far = [exchange(line[k].astype(BF16), m, total) for k, m in enumerate(LINE, 1)]
    return add_low(line[0], *far)


def reduce_small(value, total):
    value = value + exchange(value, CORE_BIT, total)
    value = add_low(value, *[exchange(value, m, total) for m in PLANE])
    return add_low(value, *[exchange(value, m, total) for m in LINE])


def gather_whole(block):
    rows, cols = lax.axis_size("row"), lax.axis_size("col")
    depth, width = block.shape
    every = lax.all_gather(block[None], AXES, axis=0, tiled=True)
    every = every.reshape(rows, cols, depth, width).transpose(0, 2, 1, 3)
    return every.reshape(rows * depth, cols * width)


def scatter_whole(grad):
    rows, cols = lax.axis_size("row"), lax.axis_size("col")
    depth, width = grad.shape[0] // rows, grad.shape[1] // cols
    parts = grad.reshape(rows, depth, cols, width).transpose(0, 2, 1, 3)
    parts = parts.reshape(rows * cols, depth, width).astype(F32)
    return lax.psum_scatter(parts, AXES, scatter_dimension=0, tiled=True)[0]


def shards(
    states,
    upstream,
    teacher,
    validity,
    picture_start,
    first_gain,
    query_weight,
    key_weight,
    value_weight,
    premix,
    postmix,
    output_weight,
    second_gain,
    up_weight,
    down_weight,
):
    row_total = lax.axis_size("row")
    col_total = lax.axis_size("col")
    total = row_total * col_total
    seq_len, features = states.shape
    depth, width = query_weight.shape
    units = up_weight.shape[1] * col_total
    blocked = (row_total, col_total) == (16, 2)
    row = lax.axis_index("row")
    spot = jnp.stack([row // 4, (row // 2) % 2, row % 2, lax.axis_index("col")]).astype(jnp.int32)
    count = jnp.sum(validity)
    down_turned = down_weight.T
    if blocked:
        packet = jnp.concatenate([query_weight, key_weight, value_weight], axis=0)
        qkv = gather_blocks(packet, total)
        lanes = lax.broadcasted_iota(jnp.int32, (depth, EXTRA), 1)
        digits = jnp.where(lanes == 0, count // 256, jnp.where(lanes == 1, count % 256, 0))
        packet = jnp.concatenate(
            [up_weight, down_turned, output_weight, digits.astype(BF16)], axis=1
        )
        rest = gather_blocks(packet, total)
        at = 2 * up_weight.shape[1] + width
        marks = sum(jnp.sum(part[:, 0, at : at + 2].astype(F32), axis=0) for part in rest)
        total_valid = marks[0] * 256.0 + marks[1]
    else:
        qkv = [gather_whole(w) for w in (query_weight, key_weight, value_weight)]
        rest = [gather_whole(w) for w in (output_weight, up_weight, down_turned)]
        total_valid = lax.psum(count.astype(F32), AXES)
    first_scale = lax.rsqrt(jnp.mean(states * states, axis=-1, keepdims=True) + EPSILON)
    normed = (states * first_scale * first_gain).astype(BF16)
    pms = premix.T * (HEAD_DIM**-0.5)
    pos = postmix
    pm = jnp.repeat(pms, HEAD_DIM, axis=1)[:, None]
    po = jnp.repeat(pos, HEAD_DIM, axis=1)[:, None]
    queries, keys, values, attended, probs = attend(spot, picture_start, normed, qkv, pm, po)
    factor = (seq_len * total) / total_valid
    layer_out, mid_grad, attended_grad, sums, *grads = middle_block(
        spot,
        factor.reshape(1, 1),
        rest,
        attended,
        states,
        upstream,
        teacher,
        validity[:, None],
        second_gain[None],
        units,
    )
    if blocked:
        ffn = reduce_blocks(grads[0], grads[1], total)
        half = up_weight.shape[1]
        up_grad, down_grad, output_grad = ffn[:, :half], ffn[:, half : 2 * half].T, ffn[:, 2 * half :]
    else:
        up_grad, down_grad, output_grad = (scatter_whole(g) for g in grads)
        down_grad = down_grad.T
    dq, dk, dv, pre, post, *grads = attend_back(
        spot, blocked, normed.T, queries, keys, values, attended_grad, probs, pm, po, pms, pos
    )
    if blocked:
        attn = reduce_blocks(grads[0], grads[1], total)
        query_grad, key_grad, value_grad = (attn[n * depth : (n + 1) * depth] for n in range(3))
    else:
        query_grad, key_grad, value_grad = (scatter_whole(g) for g in grads)
    input_grad, first_rows = input_block(
        spot, qkv, dq, dk, dv, states, mid_grad, first_gain[None]
    )
    pre = jnp.sum(pre.reshape(HEADS, HEADS, HEAD_DIM), axis=2).T * (HEAD_DIM**-0.5)
    post = jnp.sum(post, axis=2)
    small = jnp.concatenate(
        [
            first_rows[0],
            sums[0],
            pre.reshape(-1),
            post.reshape(-1),
            jnp.sum(sums[1:3], axis=1),
        ]
    )
    if blocked:
        size = small.shape[0]
        small = jnp.pad(small, (0, -size % 1024)).reshape(-1, 128)
        small = reduce_small(small, total).reshape(-1)[:size]
    else:
        small = lax.psum(small, AXES)
    mixes = HEADS * HEADS
    first_grad, second_grad, premix_grad, postmix_grad, losses = jnp.split(
        small, [features, 2 * features, 2 * features + mixes, 2 * features + 2 * mixes]
    )
    return (
        layer_out,
        losses[0] / (total_valid * features),
        losses[1] / total_valid,
        input_grad,
        first_grad,
        query_grad,
        key_grad,
        value_grad,
        premix_grad.reshape(HEADS, HEADS),
        postmix_grad.reshape(HEADS, HEADS),
        output_grad,
        second_grad,
        up_grad,
        down_grad,
    )


def solution(mesh):
    tokens, block = P(AXES, None), P("row", "col")
    return jax.shard_map(
        shards,
        mesh=mesh,
        in_specs=(
            tokens, tokens, tokens, P(AXES), tokens, P(), block, block, block, P(), P(), block,
            P(), block, P("col", "row"),
        ),
        out_specs=(
            tokens, P(), P(), tokens, P(), block, block, block, P(), P(), block, P(), block,
            P("col", "row"),
        ),
        check_vma=False,
    )
```

```python
import functools

import jax
import jax.numpy as jnp
from jax import lax
from jax.experimental import pallas as pl
from jax.experimental.pallas import tpu as pltpu
from jax.sharding import PartitionSpec as P

HEADS = 12
HEAD_DIM = 64
PIC = 256
EPSILON = 1e-06
F32 = jnp.float32
BF16 = jnp.bfloat16
AXES = ("row", "col")
X_BIT, CORE_BIT, Y_BIT, Z_BIT = 1, 2, 4, 8
LINES = [[at + Z_BIT // 2 * z for z in range(4)] for at in range(4)]
EXTRA = 128
SIDES = ((0, 0), (0, 1), (1, 0))
PARAMS = pltpu.CompilerParams(vmem_limit_bytes=60000 * 1024)
SMEM = pl.BlockSpec(memory_space=pltpu.SMEM)
ANY = pl.BlockSpec(memory_space=pl.ANY)
VMEM = pl.BlockSpec(memory_space=pltpu.VMEM)


def dot(a, b):
    return lax.dot_general(a, b, (((1,), (0,)), ((), ())), preferred_element_type=F32)


def dot_nt(a, b):
    return lax.dot_general(a, b, (((1,), (1,)), ((), ())), preferred_element_type=F32)


def cost(micros):
    return pl.CostEstimate(flops=micros * 10**9, bytes_accessed=10**6, transcendentals=0)


def placed(pieces):
    for core in range(2):
        lines, halves = pieces[2 * core : 2 * core + 2]
        for n, (y, x) in enumerate(SIDES):
            for z in range(4):
                yield lines, (n, z), core, y, x, z
        for z in range(4):
            yield halves, (z // 2, z % 2), core, 1, 1, z


def place_copies(spot, pieces, wholes, rows_at, cols_at, widths, sems):
    if len(pieces) == len(wholes):
        return [
            pltpu.make_async_copy(piece, whole, sems.at[n])
            for n, (piece, whole) in enumerate(zip(pieces, wholes))
        ]
    copies = []
    for piece, index, core, y, x, z in placed(pieces):
        r = (z * 2 + (spot[1] ^ y)) * 2 + (spot[2] ^ core)
        c = spot[3] ^ x
        for whole, row, col, width in zip(wholes, rows_at, cols_at, widths):
            depth = whole.shape[0] // 16
            copies.append(
                pltpu.make_async_copy(
                    piece.at[(*index, pl.ds(row, depth), pl.ds(col, width))],
                    whole.at[
                        pl.ds(pl.multiple_of(r * depth, 16), depth),
                        pl.ds(pl.multiple_of(c * width, 128), width),
                    ],
                    sems.at[len(copies)],
                )
            )
    return copies


def send_copies(spot, source, keep, send, row, half, col, width, sems):
    depth = source.shape[0] // 16
    copies = []
    for j in range(8):
        z, y = j // 2, j % 2
        plane = (spot[1] ^ y) * 2 + (spot[3] ^ half)
        for n, (target, core) in enumerate(((keep, spot[2]), (send, 1 - spot[2]))):
            start = pl.multiple_of((2 * j + core) * depth, 16)
            copies.append(
                pltpu.make_async_copy(
                    source.at[pl.ds(start, depth), pl.ds(0, width)],
                    target.at[plane, z, pl.ds(row, depth), pl.ds(col, width)],
                    sems.at[2 * j + n],
                )
            )
    return copies


def attend_kernel(blocks, spot, starts, normed_ref, *rest):
    pieces, rest = rest[:blocks], rest[blocks:]
    pm_ref, po_ref, q_ref, k_ref, v_ref, out_ref, p_ref, wq, wk, wv, kt, bias, acc, sems = rest
    step = pl.program_id(0)
    half = normed_ref.shape[0] // 2

    @pl.when(step == 0)
    def _():
        width = wq.shape[1] // 2
        depth = wq.shape[0] // 16
        copies = place_copies(
            spot, pieces, (wq, wk, wv), (0, depth, 2 * depth), (0, 0, 0), (width,) * 3, sems
        )
        for copy in copies:
            copy.start()
        rows = lax.broadcasted_iota(jnp.int32, (half, half), 0)
        cols = lax.broadcasted_iota(jnp.int32, (half, half), 1)
        for b in range(2):
            i, j = rows + b * half, cols + b * half
            ok = j <= i
            for s in range(2):
                p = starts[0, s]
                ok = ok | ((i >= p) & (i < p + PIC) & (j >= p) & (j < p + PIC))
            bias[b] = jnp.where(ok, 0.0, -1e30)
        acc[...] = jnp.zeros_like(acc)
        for copy in copies:
            copy.wait()
        k_ref[...] = dot(normed_ref[...], wk[...]).astype(BF16)
        kt[...] = k_ref[...].T
        q_ref[...] = dot(normed_ref[...], wq[...]).astype(BF16)
        v_ref[...] = dot(normed_ref[...], wv[...]).astype(BF16)

    pm = pm_ref[0]
    po = po_ref[0]
    vs = (v_ref[...].astype(F32) * po).astype(BF16)
    top = (q_ref[:half].astype(F32) * pm).astype(BF16)
    low = (q_ref[half:].astype(F32) * pm).astype(BF16)
    s0 = dot(top, kt[:, :half]) + bias[0]
    s1 = dot(low, kt[:, :half])
    s2 = dot(low, kt[:, half:]) + bias[1]
    m0 = jnp.max(s0, axis=1, keepdims=True)
    e0 = jnp.exp(s0 - m0)
    p0 = (e0 / jnp.sum(e0, axis=1, keepdims=True)).astype(BF16)
    m1 = jnp.maximum(jnp.max(s1, axis=1, keepdims=True), jnp.max(s2, axis=1, keepdims=True))
    e1 = jnp.exp(s1 - m1)
    e2 = jnp.exp(s2 - m1)
    inv = 1.0 / (jnp.sum(e1, axis=1, keepdims=True) + jnp.sum(e2, axis=1, keepdims=True))
    p1 = (e1 * inv).astype(BF16)
    p2 = (e2 * inv).astype(BF16)
    p_ref[0, :, :half] = p0
    p_ref[0, :, half : 2 * half] = p1
    p_ref[0, :, 2 * half :] = p2
    acc[:half] += dot(p0, vs[:half])
    acc[half:] += dot(p1, vs[:half]) + dot(p2, vs[half:])

    @pl.when(step == HEADS - 1)
    def _():
        out_ref[...] = acc[...].astype(BF16)


def attend(spot, starts, normed, pieces, pm, po):
    seq, width = normed.shape
    half = seq // 2
    whole = pl.BlockSpec((seq, width), lambda h: (0, 0))
    row = pl.BlockSpec((1, 1, width), lambda h: (h, 0, 0))
    low = jax.ShapeDtypeStruct((seq, width), BF16)
    return pl.pallas_call(
        functools.partial(attend_kernel, len(pieces)),
        grid=(HEADS,),
        in_specs=[SMEM, SMEM, whole] + [ANY] * len(pieces) + [row, row],
        out_specs=[whole] * 4 + [pl.BlockSpec((1, half, 3 * half), lambda h: (h, 0, 0))],
        out_shape=[low] * 4 + [jax.ShapeDtypeStruct((HEADS, half, 3 * half), BF16)],
        scratch_shapes=[pltpu.VMEM((width, width), BF16)] * 3
        + [
            pltpu.VMEM((width, seq), BF16),
            pltpu.VMEM((2, half, half), F32),
            pltpu.VMEM((seq, width), F32),
            pltpu.SemaphoreType.DMA((96,)),
        ],
        compiler_params=PARAMS,
        name="attend",
        cost_estimate=cost(20),
    )(spot, starts, normed, *pieces, pm, po)


def middle_kernel(blocks, outs, tokens, spot, count, *rest):
    pieces, rest = rest[:blocks], rest[blocks:]
    att_ref, states_ref, up_ref, teach_ref, valid_ref, gain_ref = rest[:6]
    layer_ref, mid_ref, agrad_ref, sums_ref = rest[6:10]
    grads, rest = rest[10 : 10 + outs], rest[10 + outs :]
    wo, wu, wd, hidden, pre, n2t, olt, slots, marks, sems, out_sems, mark_sems = rest
    seq, width = att_ref.shape
    units = wu.shape[1]
    blocked = outs == 4
    mark_copies = []
    if blocked:
        for n, (piece, index, *_) in enumerate(placed(pieces)):
            mark_copies.append(
                pltpu.make_async_copy(
                    piece.at[(*index, pl.ds(0, 16), pl.ds((units + width) // 2, EXTRA))],
                    marks.at[n],
                    mark_sems.at[n],
                )
            )
    copies = place_copies(
        spot,
        pieces,
        (wo, wu, wd),
        (0, 0, 0),
        (units // 2, 0, (units + width) // 2 + EXTRA),
        (width // 2, units // 2, units // 2),
        sems,
    )
    for copy in mark_copies + copies[::3] + copies[1::3] + copies[2::3]:
        copy.start()
    for copy in mark_copies:
        copy.wait()
    total_valid = jnp.full((1, 1), count[0, 0], F32)
    if blocked:
        digits = jnp.sum(marks[...].astype(F32), axis=0)[:1]
        lanes = lax.broadcasted_iota(jnp.int32, digits.shape, 1)
        digits = jnp.where(lanes == 0, digits * 256.0, jnp.where(lanes == 1, digits, 0.0))
        total_valid += jnp.sum(digits, axis=1, keepdims=True)
    factor = tokens / total_valid
    sums_ref[...] = jnp.broadcast_to(total_valid, sums_ref.shape)
    for copy in copies[::3]:
        copy.wait()
    mid_ref[...] = states_ref[...] + dot(att_ref[...], wo[...])
    middle = mid_ref[...]
    scale = lax.rsqrt(jnp.mean(middle * middle, axis=1, keepdims=True) + EPSILON)
    n2 = (middle * scale * gain_ref[...]).astype(BF16)
    n2t[...] = n2.T
    for copy in copies[1::3]:
        copy.wait()

    chunk = 512
    steps = units // chunk

    def up_step(j, _):
        at = pl.ds(pl.multiple_of(j * chunk, chunk), chunk)
        hidden[:, at] = jnp.maximum(dot(n2, wu[:, at]), 0.0).astype(BF16)
        return 0

    lax.fori_loop(0, steps, up_step, 0)
    for copy in copies[2::3]:
        copy.wait()
    layer_ref[...] = mid_ref[...] + dot_nt(hidden[...], wd[...])
    layer = layer_ref[...]
    valid = valid_ref[...].astype(F32)
    upstream = up_ref[...]
    differ = layer - teach_ref[...]
    sums_ref[1:2, :] = jnp.sum(valid * (differ * differ), axis=0, keepdims=True)
    sums_ref[2:3, :] = jnp.sum(valid * (upstream * layer), axis=0, keepdims=True)
    out_grad = (factor * valid) * (upstream + differ)
    out_low = out_grad.astype(BF16)
    olt[...] = out_low.T

    def down_step(j, _):
        at = pl.ds(pl.multiple_of(j * chunk, chunk), chunk)
        part = hidden[:, at]
        back = jnp.where(part > 0, dot(out_low, wd[:, at]), 0.0).astype(BF16)
        pre[:, at] = back
        for which, (left, right) in enumerate(((n2t, back), (olt, part))):
            slot = slots.at[which]

            @pl.when(j > 0)
            def _():
                for copy in grad_copies(which, j - 1):
                    copy.wait()

            slot[...] = dot(left[...], right).astype(BF16)
            for copy in grad_copies(which, j):
                copy.start()
        return 0

    def grad_copies(which, j):
        if not blocked:
            at = pl.ds(pl.multiple_of(j * chunk, chunk), chunk)
            return [pltpu.make_async_copy(slots.at[which], grads[which].at[:, at], out_sems.at[which, 0])]
        per = steps // 2
        return send_copies(
            spot,
            slots.at[which],
            grads[2 * which],
            grads[2 * which + 1],
            0,
            j // per,
            pl.multiple_of((j % per) * chunk, 128),
            chunk,
            out_sems.at[which],
        )

    lax.fori_loop(0, steps, down_step, 0)
    grad = dot_nt(pre[...], wu[...])
    middle = mid_ref[...]
    scale = lax.rsqrt(jnp.mean(middle * middle, axis=1, keepdims=True) + EPSILON)
    sums_ref[0:1, :] = jnp.sum(grad * middle * scale, axis=0, keepdims=True)
    term = gain_ref[...] * grad
    inner = jnp.mean(term * middle, axis=1, keepdims=True)
    layer = layer_ref[...]
    out_grad = (factor * valid_ref[...].astype(F32)) * (
        up_ref[...] + (layer - teach_ref[...])
    )
    mid_grad = out_grad + scale * term - middle * (scale * scale * scale) * inner
    mid_ref[...] = mid_grad
    branch = mid_grad.astype(BF16)
    agrad_ref[...] = dot_nt(branch, wo[...]).astype(BF16)
    n2t[...] = att_ref[...].T
    for which in range(2):
        for copy in grad_copies(which, steps - 1):
            copy.wait()
    half = width // 2
    last = []
    for c in range(2):
        slots[c, :, :half] = dot(n2t[...], branch[:, c * half : (c + 1) * half]).astype(BF16)
        if blocked:
            made = send_copies(
                spot, slots.at[c], grads[0], grads[1], 0, c, units // 2, half, out_sems.at[c]
            )
        else:
            made = [
                pltpu.make_async_copy(
                    slots.at[c, :, pl.ds(0, half)],
                    grads[2].at[:, pl.ds(c * half, half)],
                    out_sems.at[c, 0],
                )
            ]
        for copy in made:
            copy.start()
        last += made
    for copy in last:
        copy.wait()


def middle_block(blocked, spot, count, tokens, pieces, attended, states, upstream, teacher, valid, gain, units):
    seq, width = attended.shape
    full = jax.ShapeDtypeStruct((seq, width), F32)
    if blocked:
        depth = width // 16
        grads = [jax.ShapeDtypeStruct((4, 4, depth, (units + width) // 2), BF16)] * 2
        grads += [jax.ShapeDtypeStruct((4, 4, depth, units // 2), BF16)] * 2
    else:
        grads = [
            jax.ShapeDtypeStruct((width, units), BF16),
            jax.ShapeDtypeStruct((width, units), BF16),
            jax.ShapeDtypeStruct((width, width), BF16),
        ]
    return pl.pallas_call(
        functools.partial(middle_kernel, len(pieces), len(grads), tokens),
        in_specs=[SMEM, SMEM] + [ANY] * len(pieces) + [VMEM] * 6,
        out_specs=[VMEM] * 4 + [ANY] * len(grads),
        out_shape=[
            full,
            full,
            jax.ShapeDtypeStruct((seq, width), BF16),
            jax.ShapeDtypeStruct((8, width), F32),
        ]
        + grads,
        scratch_shapes=[
            pltpu.VMEM((width, width), BF16),
            pltpu.VMEM((width, units), BF16),
            pltpu.VMEM((width, units), BF16),
            pltpu.VMEM((seq, units), BF16),
            pltpu.VMEM((seq, units), BF16),
            pltpu.VMEM((width, seq), BF16),
            pltpu.VMEM((width, seq), BF16),
            pltpu.VMEM((2, width, 512), BF16),
            pltpu.VMEM((32, 16, EXTRA), BF16),
            pltpu.SemaphoreType.DMA((96,)),
            pltpu.SemaphoreType.DMA((2, 16)),
            pltpu.SemaphoreType.DMA((32,)),
        ],
        compiler_params=PARAMS,
        name="middle",
        cost_estimate=cost(35),
    )(spot, count, *pieces, attended, states, upstream, teacher, valid, gain)


def attend_back_kernel(first, blocked, spot, pms, pos, *refs):
    turned, refs = (None, refs) if first else (refs[:7], refs[7:])
    q_ref, k_ref, v_ref, g_ref, p_ref, pm_ref, po_ref = refs[:7]
    pre_ref, post_ref, *rest = refs[7:]
    if first:
        vt, qt, gt, dq, dkt, dvt = rest
    else:
        nt_ref, vt, qt, gt, dq_in, dkt_in, dvt_in = turned
        dq_ref, dk_ref, dv_ref, *rest = rest
        outs = 2 if blocked else 3
        grads = rest[:outs]
        dq, dkt, dvt, slots, sems = rest[outs:]
    step = pl.program_id(0)
    head = step if first else step + HEADS // 2
    seq, width = q_ref.shape
    half = seq // 2

    @pl.when(step == 0)
    def _():
        if first:
            vt[...] = v_ref[...].T
            qt[...] = q_ref[...].T
            gt[...] = g_ref[...].T
            dq[...] = jnp.zeros_like(dq)
            dkt[...] = jnp.zeros_like(dkt)
            dvt[...] = jnp.zeros_like(dvt)
        else:
            dq[...] = dq_in[...]
            dkt[...] = dkt_in[...]
            dvt[...] = dvt_in[...]

    pm = pm_ref[0]
    po = po_ref[0]
    p0, p1, p2 = (p_ref[0, :, b * half : (b + 1) * half] for b in range(3))
    top = (g_ref[:half].astype(F32) * po).astype(BF16)
    low = (g_ref[half:].astype(F32) * po).astype(BF16)
    g0 = dot(top, vt[:, :half])
    g1 = dot(low, vt[:, :half])
    g2 = dot(low, vt[:, half:])
    u0 = dot(gt[:, :half], p0) + dot(gt[:, half:], p1)
    u1 = dot(gt[:, half:], p2)
    f0, f1, f2 = p0.astype(F32), p1.astype(F32), p2.astype(F32)
    t0 = f0 * g0
    d0 = (t0 - f0 * jnp.sum(t0, axis=1, keepdims=True)).astype(BF16)
    t1, t2 = f1 * g1, f2 * g2
    r1 = jnp.sum(t1, axis=1, keepdims=True) + jnp.sum(t2, axis=1, keepdims=True)
    d1 = (t1 - f1 * r1).astype(BF16)
    d2 = (t2 - f2 * r1).astype(BF16)
    w0 = dot(d0, k_ref[:half])
    w1 = dot(d1, k_ref[:half]) + dot(d2, k_ref[half:])
    dq[:half] += pm * w0
    dq[half:] += pm * w1
    pre_ref[0] = jnp.sum(q_ref[:half].astype(F32) * w0, axis=0, keepdims=True) + jnp.sum(
        q_ref[half:].astype(F32) * w1, axis=0, keepdims=True
    )
    for g in range(HEADS):
        at = slice(g * HEAD_DIM, (g + 1) * HEAD_DIM)
        b = pos[head, g]
        u0g, u1g = u0[at], u1[at]
        dvt[at, :half] += b * u0g
        dvt[at, half:] += b * u1g
        both = u0g * vt[at, :half].astype(F32) + u1g * vt[at, half:].astype(F32)
        post_ref[0, g : g + 1, :] = jnp.sum(both, axis=0, keepdims=True)
    qs = jnp.concatenate(
        [
            (qt[g * HEAD_DIM : (g + 1) * HEAD_DIM].astype(F32) * pms[head, g]).astype(BF16)
            for g in range(HEADS)
        ],
        axis=0,
    )
    dkt[:, :half] += dot(qs[:, :half], d0) + dot(qs[:, half:], d1)
    dkt[:, half:] += dot(qs[:, half:], d2)

    if first:
        return

    @pl.when(step == HEADS // 2 - 1)
    def _():
        dq_ref[...] = dq[...].astype(BF16)
        dk_ref[...] = dkt[...].astype(BF16).T
        dv_ref[...] = dvt[...].astype(BF16).T
        made = []
        for n, ref in enumerate((dq_ref, dk_ref, dv_ref)):
            slots[n] = dot(nt_ref[...], ref[...]).astype(BF16)
            if blocked:
                part = width // 2
                for c in range(2):
                    made += send_copies(
                        spot,
                        slots.at[n, :, pl.ds(c * part, part)],
                        grads[0],
                        grads[1],
                        n * (width // 16),
                        c,
                        0,
                        part,
                        sems.at[2 * n + c],
                    )
            else:
                made.append(pltpu.make_async_copy(slots.at[n], grads[n], sems.at[n, 0]))
            for copy in made[-32 if blocked else -1 :]:
                copy.start()
        for copy in made:
            copy.wait()


def attend_back(spot, blocked, turned, q, k, v, g, p, pm, po, pms, pos):
    seq, width = q.shape
    half = seq // 2
    first = turned is None
    base = 0 if first else HEADS // 2
    whole = pl.BlockSpec((seq, width), lambda h: (0, 0))
    across = pl.BlockSpec((width, seq), lambda h: (0, 0))
    row = pl.BlockSpec((1, 1, width), lambda h: (h + base, 0, 0))
    low = jax.ShapeDtypeStruct((seq, width), BF16)
    low_across = jax.ShapeDtypeStruct((width, seq), BF16)
    out_specs = [
        pl.BlockSpec((1, 1, width), lambda h: (h, 0, 0)),
        pl.BlockSpec((1, HEADS, half), lambda h: (h, 0, 0)),
    ]
    out_shape = [
        jax.ShapeDtypeStruct((HEADS // 2, 1, width), F32),
        jax.ShapeDtypeStruct((HEADS // 2, HEADS, half), F32),
    ]
    if first:
        in_specs, scratch = [], []
        out_specs += [across] * 3 + [whole] + [across] * 2
        out_shape += [low_across] * 3 + [jax.ShapeDtypeStruct((seq, width), F32)]
        out_shape += [jax.ShapeDtypeStruct((width, seq), F32)] * 2
    else:
        in_specs = [across] * 4 + [whole] + [across] * 2
        if blocked:
            grads = [jax.ShapeDtypeStruct((4, 4, 3 * (width // 16), width // 2), BF16)] * 2
        else:
            grads = [jax.ShapeDtypeStruct((width, width), BF16)] * 3
        out_specs += [whole] * 3 + [ANY] * len(grads)
        out_shape += [low] * 3 + grads
        scratch = [
            pltpu.VMEM((seq, width), F32),
            pltpu.VMEM((width, seq), F32),
            pltpu.VMEM((width, seq), F32),
            pltpu.VMEM((3, width, width), BF16),
            pltpu.SemaphoreType.DMA((6, 16)),
        ]
    return pl.pallas_call(
        functools.partial(attend_back_kernel, first, blocked),
        grid=(HEADS // 2,),
        in_specs=[SMEM, SMEM, SMEM]
        + in_specs
        + [whole] * 4
        + [pl.BlockSpec((1, half, 3 * half), lambda h: (h + base, 0, 0)), row, row],
        out_specs=out_specs,
        out_shape=out_shape,
        scratch_shapes=scratch,
        compiler_params=PARAMS,
        name="attend_back_first" if first else "attend_back",
        cost_estimate=cost(14),
    )(spot, pms, pos, *(() if first else turned), q, k, v, g, p, pm, po)


def input_kernel(blocks, spot, *rest):
    pieces, rest = rest[:blocks], rest[blocks:]
    dq_ref, dk_ref, dv_ref, states_ref, mid_ref, gain_ref, out_ref, first_ref = rest[:8]
    wq, wk, wv, sems = rest[8:]
    width = wq.shape[1] // 2
    depth = wq.shape[0] // 16
    copies = place_copies(
        spot, pieces, (wq, wk, wv), (0, depth, 2 * depth), (0, 0, 0), (width,) * 3, sems
    )
    for copy in copies:
        copy.start()
    states = states_ref[...]
    scale = lax.rsqrt(jnp.mean(states * states, axis=1, keepdims=True) + EPSILON)
    for copy in copies:
        copy.wait()
    grad = (
        dot_nt(dq_ref[...], wq[...]) + dot_nt(dk_ref[...], wk[...]) + dot_nt(dv_ref[...], wv[...])
    )
    first_ref[...] = jnp.broadcast_to(
        jnp.sum(grad * states * scale, axis=0, keepdims=True), first_ref.shape
    )
    term = gain_ref[...] * grad
    inner = jnp.mean(term * states, axis=1, keepdims=True)
    out_ref[...] = mid_ref[...] + scale * term - states * (scale * scale * scale) * inner


def input_block(spot, pieces, dq, dk, dv, states, mid_grad, gain):
    seq, width = dq.shape
    return pl.pallas_call(
        functools.partial(input_kernel, len(pieces)),
        in_specs=[SMEM] + [ANY] * len(pieces) + [VMEM] * 6,
        out_specs=[VMEM] * 2,
        out_shape=[
            jax.ShapeDtypeStruct((seq, width), F32),
            jax.ShapeDtypeStruct((8, width), F32),
        ],
        scratch_shapes=[pltpu.VMEM((width, width), BF16)] * 3 + [pltpu.SemaphoreType.DMA((96,))],
        compiler_params=PARAMS,
        name="input_grad",
        cost_estimate=cost(9),
    )(spot, *pieces, dq, dk, dv, states, mid_grad, gain)


def exchange(value, mask, total):
    return lax.ppermute(value, AXES, [(i, i ^ mask) for i in range(total)])


def after(value, *others):
    return lax.optimization_barrier((value, *others))[0]


def over_lines(blocks):
    return lax.all_to_all(blocks, "row", 0, 0, axis_index_groups=LINES, tiled=True)


def gather_line(packet):
    return over_lines(jnp.broadcast_to(packet, (4, *packet.shape)))


def gather_sides(line, total):
    return exchange(line, X_BIT, total), exchange(line, Y_BIT, total)


def gather_halves(over_x, over_y, total):
    return exchange(over_x[:2], Y_BIT, total), exchange(over_y[2:], X_BIT, total)


def add_low(*terms):
    return functools.reduce(jnp.add, [t.astype(F32) for t in terms])


def reduce_core(keep, other):
    mine = add_low(keep, other).astype(BF16)
    return mine, mine[2:, :2], mine[1::2, 2:]


def reduce_first(over_y, over_x, total):
    return exchange(over_y, Y_BIT, total), exchange(over_x, X_BIT, total)


def reduce_sides(mine, over_y, over_x):
    return add_low(mine[1, :2], over_y[1]).astype(BF16), add_low(mine[2, 2:], over_x[1]).astype(BF16)


def reduce_second(side_x, side_y, total):
    return exchange(side_x, X_BIT, total), exchange(side_y, Y_BIT, total)


def reduce_own(mine, over_y, over_x):
    return add_low(mine[0, :2], over_y[0]), add_low(mine[0, 2:], over_x[0])


def reduce_line(head, tail, side_x, side_y):
    return over_lines(jnp.concatenate([add_low(head, side_x), add_low(tail, side_y)]).astype(BF16))


def pack_small(first_rows, sums, pre, post):
    pre = jnp.sum(pre.reshape(HEADS, HEADS, HEAD_DIM), axis=2).T * (HEAD_DIM**-0.5)
    losses = jnp.sum(sums[1:3], axis=1)
    small = [first_rows[0], sums[0], pre.reshape(-1), jnp.sum(post, axis=2).reshape(-1), losses]
    small = jnp.concatenate(small)
    return jnp.pad(small, (0, -small.shape[0] % 1024)).reshape(-1, 128)


def gather_whole(block):
    rows, cols = lax.axis_size("row"), lax.axis_size("col")
    depth, width = block.shape
    every = lax.all_gather(block[None], AXES, axis=0, tiled=True)
    every = every.reshape(rows, cols, depth, width).transpose(0, 2, 1, 3)
    return every.reshape(rows * depth, cols * width)


def scatter_whole(grad):
    rows, cols = lax.axis_size("row"), lax.axis_size("col")
    depth, width = grad.shape[0] // rows, grad.shape[1] // cols
    parts = grad.reshape(rows, depth, cols, width).transpose(0, 2, 1, 3)
    parts = parts.reshape(rows * cols, depth, width).astype(F32)
    return lax.psum_scatter(parts, AXES, scatter_dimension=0, tiled=True)[0]


def shards(
    states,
    upstream,
    teacher,
    validity,
    picture_start,
    first_gain,
    query_weight,
    key_weight,
    value_weight,
    premix,
    postmix,
    output_weight,
    second_gain,
    up_weight,
    down_weight,
):
    row_total = lax.axis_size("row")
    col_total = lax.axis_size("col")
    total = row_total * col_total
    seq_len, features = states.shape
    depth, width = query_weight.shape
    units = up_weight.shape[1] * col_total
    blocked = (row_total, col_total) == (16, 2)
    row = lax.axis_index("row")
    spot = jnp.stack([row // 4, (row // 2) % 2, row % 2, lax.axis_index("col")]).astype(jnp.int32)
    count = jnp.sum(validity)
    down_turned = down_weight.T
    if blocked:
        packet = jnp.concatenate([query_weight, key_weight, value_weight], axis=0)
        qkv_line = gather_line(packet)
        qkv_sides = gather_sides(qkv_line, total)
        lanes = lax.broadcasted_iota(jnp.int32, (depth, EXTRA), 1)
        digits = jnp.where(lanes == 0, count // 256, jnp.where(lanes == 1, count % 256, 0))
        packet = jnp.concatenate(
            [up_weight, output_weight, digits.astype(BF16), down_turned], axis=1
        )
        line = gather_line(after(packet, qkv_line))
        qkv_halves = jnp.stack(gather_halves(*qkv_sides, total))
        qkv_lines = jnp.stack([qkv_line, *qkv_sides])
        qkv = [qkv_lines, qkv_halves]
        qkv += [exchange(part, CORE_BIT, total) for part in qkv]
        line, *qkv = lax.optimization_barrier((line, *qkv))
        sides = gather_sides(line, total)
        total_valid = jnp.zeros((), F32)
    else:
        qkv = [gather_whole(w) for w in (query_weight, key_weight, value_weight)]
        rest = [gather_whole(w) for w in (output_weight, up_weight, down_turned)]
        total_valid = lax.psum(count.astype(F32), AXES)
    first_scale = lax.rsqrt(jnp.mean(states * states, axis=-1, keepdims=True) + EPSILON)
    normed = (states * first_scale * first_gain).astype(BF16)
    pms = premix.T * (HEAD_DIM**-0.5)
    pos = postmix
    pm = jnp.repeat(pms, HEAD_DIM, axis=1)[:, None]
    po = jnp.repeat(pos, HEAD_DIM, axis=1)[:, None]
    queries, keys, values, attended, probs = attend(spot, picture_start, normed, qkv, pm, po)
    if blocked:
        *sides, attended = lax.optimization_barrier((*sides, attended))
        rest = [jnp.stack([line, *sides]), jnp.stack(gather_halves(*sides, total))]
        rest += [exchange(part, CORE_BIT, total) for part in rest]
    layer_out, mid_grad, attended_grad, sums, *grads = middle_block(
        blocked,
        spot,
        total_valid.reshape(1, 1),
        seq_len * total,
        rest,
        attended,
        states,
        upstream,
        teacher,
        validity[:, None],
        second_gain[None],
        units,
    )
    total_valid = sums[3, 0]
    heads = queries, keys, values, attended_grad, probs, pm, po, pms, pos
    if blocked:
        down_mine, *first, attended_grad = lax.optimization_barrier(
            (*reduce_core(grads[2], exchange(grads[3], CORE_BIT, total)), attended_grad)
        )
        down_first = reduce_first(*first, total)
        heads = queries, keys, values, attended_grad, probs, pm, po, pms, pos
        up_other = exchange(grads[1], CORE_BIT, total)
        part = attend_back(spot, blocked, None, *heads)
        up_keep, up_other, *rest = lax.optimization_barrier((grads[0], up_other, *down_first, *part))
        down_first, part = rest[:2], rest[2:]
        up_mine, *first = reduce_core(up_keep, up_other)
        down_sides = reduce_sides(down_mine, *down_first)
        *rest, up_mine, down_head, down_tail = lax.optimization_barrier(
            (*first, *down_sides, *part, up_mine, *reduce_own(down_mine, *down_first))
        )
        first, down_sides, part = rest[:2], rest[2:4], rest[4:]
        up_first = reduce_first(*first, total)
        down_sides = reduce_second(*down_sides, total)
    else:
        up_grad, output_grad, down_grad = (scatter_whole(g) for g in (grads[0], grads[2], grads[1]))
        down_grad = down_grad.T
        part = attend_back(spot, blocked, None, *heads)
    pre, post, *turned = part
    pre_last, post_last, dq, dk, dv, *grads = attend_back(spot, blocked, (normed.T, *turned), *heads)
    pre = jnp.concatenate([pre, pre_last])
    post = jnp.concatenate([post, post_last])
    if blocked:
        dq, dk, dv, *rest = lax.optimization_barrier((dq, dk, dv, *grads, *up_first, *down_sides))
        grads, up_first, down_sides = rest[:2], rest[2:4], rest[4:]
        up_sides = reduce_second(*reduce_sides(up_mine, *up_first), total)
        down_line = reduce_line(down_head, down_tail, *down_sides)
        mine, *first, dq, dk, dv = lax.optimization_barrier(
            (*reduce_core(grads[0], exchange(grads[1], CORE_BIT, total)), dq, dk, dv)
        )
        first = reduce_first(*first, total)
        input_grad, first_rows = input_block(
            spot, qkv, dq, dk, dv, states, mid_grad, first_gain[None]
        )
        input_grad, first_rows, *up_sides = lax.optimization_barrier(
            (input_grad, first_rows, *up_sides)
        )
        up_line = reduce_line(*reduce_own(up_mine, *up_first), *up_sides)
        sides = reduce_sides(mine, *first)
        small = pack_small(first_rows, sums, pre, post)
        small += exchange(small, CORE_BIT, total)
        small = after(small, *sides)
        sides = reduce_second(*sides, total)
        for bit in (X_BIT, Y_BIT):
            small += exchange(small, bit, total)
        *sides, down_line, small = lax.optimization_barrier((*sides, down_line, small))
        for bit in (Z_BIT, 2 * Z_BIT):
            small += exchange(small, bit, total)
        line = reduce_line(*reduce_own(mine, *first), *sides)
        down_grad, ffn, attn = (jnp.sum(w.astype(F32), axis=0) for w in (down_line, up_line, line))
        down_grad = down_grad.T
        up_grad, output_grad = ffn[:, : units // col_total], ffn[:, units // col_total :]
        query_grad, key_grad, value_grad = (attn[n * depth : (n + 1) * depth] for n in range(3))
    else:
        query_grad, key_grad, value_grad = (scatter_whole(g) for g in grads)
        input_grad, first_rows = input_block(
            spot, qkv, dq, dk, dv, states, mid_grad, first_gain[None]
        )
        small = lax.psum(pack_small(first_rows, sums, pre, post), AXES)
    small = small.reshape(-1)
    mixes = HEADS * HEADS
    first_grad, second_grad, premix_grad, postmix_grad, losses = jnp.split(
        small, [features, 2 * features, 2 * features + mixes, 2 * features + 2 * mixes]
    )
    return (
        layer_out,
        losses[0] / (total_valid * features),
        losses[1] / total_valid,
        input_grad,
        first_grad,
        query_grad,
        key_grad,
        value_grad,
        premix_grad.reshape(HEADS, HEADS),
        postmix_grad.reshape(HEADS, HEADS),
        output_grad,
        second_grad,
        up_grad,
        down_grad,
    )


def solution(mesh):
    tokens, block = P(AXES, None), P("row", "col")
    return jax.shard_map(
        shards,
        mesh=mesh,
        in_specs=(
            tokens, tokens, tokens, P(AXES), tokens, P(), block, block, block, P(), P(), block,
            P(), block, P("col", "row"),
        ),
        out_specs=(
            tokens, P(), P(), tokens, P(), block, block, block, P(), P(), block, P(), block,
            P("col", "row"),
        ),
        check_vma=False,
    )
```

```python
import functools

import jax
import jax.numpy as jnp
from jax import lax
from jax.experimental import pallas as pl
from jax.experimental.pallas import tpu as pltpu
from jax.sharding import PartitionSpec as P

HEADS = 12
HEAD_DIM = 64
PIC = 256
EPSILON = 1e-06
F32 = jnp.float32
BF16 = jnp.bfloat16
AXES = ("row", "col")
X_BIT, CORE_BIT, Y_BIT, Z_BIT = 1, 2, 4, 8
LINES = [[at + Z_BIT // 2 * z for z in range(4)] for at in range(4)]
EXTRA = 128
SIDES = ((0, 0), (0, 1), (1, 0))
PARAMS = pltpu.CompilerParams(vmem_limit_bytes=60000 * 1024)
SMEM = pl.BlockSpec(memory_space=pltpu.SMEM)
ANY = pl.BlockSpec(memory_space=pl.ANY)
VMEM = pl.BlockSpec(memory_space=pltpu.VMEM)


def dot(a, b):
    return lax.dot_general(a, b, (((1,), (0,)), ((), ())), preferred_element_type=F32)


def dot_nt(a, b):
    return lax.dot_general(a, b, (((1,), (1,)), ((), ())), preferred_element_type=F32)


def cost(micros):
    return pl.CostEstimate(flops=micros * 10**9, bytes_accessed=10**6, transcendentals=0)


def placed(pieces):
    for core in range(2):
        lines, halves = pieces[2 * core : 2 * core + 2]
        for n, (y, x) in enumerate(SIDES):
            for z in range(4):
                yield lines, (n, z), core, y, x, z
        for z in range(4):
            yield halves, (z // 2, z % 2), core, 1, 1, z


def place_copies(spot, pieces, wholes, rows_at, cols_at, widths, sems, near=False):
    if len(pieces) == len(wholes):
        return [
            pltpu.make_async_copy(piece, whole, sems.at[n])
            for n, (piece, whole) in enumerate(zip(pieces, wholes))
        ]
    copies = []
    for piece, index, core, y, x, z in placed(pieces):
        r = ((spot[0] ^ z if near else z) * 2 + (spot[1] ^ y)) * 2 + (spot[2] ^ core)
        c = spot[3] ^ x
        for whole, row, col, width in zip(wholes, rows_at, cols_at, widths):
            depth = whole.shape[0] // 16
            copies.append(
                pltpu.make_async_copy(
                    piece.at[(*index, pl.ds(row, depth), pl.ds(col, width))],
                    whole.at[
                        pl.ds(pl.multiple_of(r * depth, 16), depth),
                        pl.ds(pl.multiple_of(c * width, 128), width),
                    ],
                    sems.at[len(copies)],
                )
            )
    return copies


def send_copies(spot, source, keep, send, row, half, col, width, sems, near=False):
    depth = source.shape[0] // 16
    copies = []
    for j in range(8):
        z, y = j // 2, j % 2
        plane = (spot[1] ^ y) * 2 + (spot[3] ^ half)
        for n, (target, core) in enumerate(((keep, spot[2]), (send, 1 - spot[2]))):
            start = pl.multiple_of((2 * j + core) * depth, 16)
            copies.append(
                pltpu.make_async_copy(
                    source.at[pl.ds(start, depth), pl.ds(0, width)],
                    target.at[plane, spot[0] ^ z if near else z, pl.ds(row, depth), pl.ds(col, width)],
                    sems.at[2 * j + n],
                )
            )
    return copies


def attend_kernel(blocks, spot, starts, normed_ref, *rest):
    pieces, rest = rest[:blocks], rest[blocks:]
    pm_ref, po_ref, q_ref, k_ref, v_ref, out_ref, p_ref, wq, wk, wv, kt, bias, acc, sems = rest
    step = pl.program_id(0)
    half = normed_ref.shape[0] // 2

    @pl.when(step == 0)
    def _():
        width = wq.shape[1] // 2
        depth = wq.shape[0] // 16
        copies = place_copies(
            spot, pieces, (wq, wk, wv), (0, depth, 2 * depth), (0, 0, 0), (width,) * 3, sems, True
        )
        for copy in copies:
            copy.start()
        rows = lax.broadcasted_iota(jnp.int32, (half, half), 0)
        cols = lax.broadcasted_iota(jnp.int32, (half, half), 1)
        for b in range(2):
            i, j = rows + b * half, cols + b * half
            ok = j <= i
            for s in range(2):
                p = starts[0, s]
                ok = ok | ((i >= p) & (i < p + PIC) & (j >= p) & (j < p + PIC))
            bias[b] = jnp.where(ok, 0.0, -1e30)
        acc[...] = jnp.zeros_like(acc)
        for copy in copies:
            copy.wait()
        k_ref[...] = dot(normed_ref[...], wk[...]).astype(BF16)
        kt[...] = k_ref[...].T
        q_ref[...] = dot(normed_ref[...], wq[...]).astype(BF16)
        v_ref[...] = dot(normed_ref[...], wv[...]).astype(BF16)

    pm = pm_ref[0]
    po = po_ref[0]
    vs = (v_ref[...].astype(F32) * po).astype(BF16)
    top = (q_ref[:half].astype(F32) * pm).astype(BF16)
    low = (q_ref[half:].astype(F32) * pm).astype(BF16)
    s0 = dot(top, kt[:, :half]) + bias[0]
    s1 = dot(low, kt[:, :half])
    s2 = dot(low, kt[:, half:]) + bias[1]
    m0 = jnp.max(s0, axis=1, keepdims=True)
    e0 = jnp.exp(s0 - m0)
    p0 = (e0 / jnp.sum(e0, axis=1, keepdims=True)).astype(BF16)
    m1 = jnp.maximum(jnp.max(s1, axis=1, keepdims=True), jnp.max(s2, axis=1, keepdims=True))
    e1 = jnp.exp(s1 - m1)
    e2 = jnp.exp(s2 - m1)
    inv = 1.0 / (jnp.sum(e1, axis=1, keepdims=True) + jnp.sum(e2, axis=1, keepdims=True))
    p1 = (e1 * inv).astype(BF16)
    p2 = (e2 * inv).astype(BF16)
    p_ref[0, :, :half] = p0
    p_ref[0, :, half : 2 * half] = p1
    p_ref[0, :, 2 * half :] = p2
    acc[:half] += dot(p0, vs[:half])
    acc[half:] += dot(p1, vs[:half]) + dot(p2, vs[half:])

    @pl.when(step == HEADS - 1)
    def _():
        out_ref[...] = acc[...].astype(BF16)


def attend(spot, starts, normed, pieces, pm, po):
    seq, width = normed.shape
    half = seq // 2
    whole = pl.BlockSpec((seq, width), lambda h: (0, 0))
    row = pl.BlockSpec((1, 1, width), lambda h: (h, 0, 0))
    low = jax.ShapeDtypeStruct((seq, width), BF16)
    return pl.pallas_call(
        functools.partial(attend_kernel, len(pieces)),
        grid=(HEADS,),
        in_specs=[SMEM, SMEM, whole] + [ANY] * len(pieces) + [row, row],
        out_specs=[whole] * 4 + [pl.BlockSpec((1, half, 3 * half), lambda h: (h, 0, 0))],
        out_shape=[low] * 4 + [jax.ShapeDtypeStruct((HEADS, half, 3 * half), BF16)],
        scratch_shapes=[pltpu.VMEM((width, width), BF16)] * 3
        + [
            pltpu.VMEM((width, seq), BF16),
            pltpu.VMEM((2, half, half), F32),
            pltpu.VMEM((seq, width), F32),
            pltpu.SemaphoreType.DMA((96,)),
        ],
        compiler_params=PARAMS,
        name="attend",
        cost_estimate=cost(20),
    )(spot, starts, normed, *pieces, pm, po)


def up_copies(spot, slots, grads, sems, j, chunk, steps):
    slot = lax.rem(j, 2)
    if len(grads) == 1:
        at = pl.ds(pl.multiple_of(j * chunk, chunk), chunk)
        return [pltpu.make_async_copy(slots.at[slot], grads[0].at[:, at], sems.at[slot, 0])]
    per = steps // 2
    col = pl.multiple_of(lax.rem(j, per) * chunk, 128)
    return send_copies(
        spot, slots.at[slot], *grads, 0, lax.div(j, per), col, chunk, sems.at[slot]
    )


def forward_kernel(blocks, outs, tokens, spot, count, *rest):
    pieces, rest = rest[:blocks], rest[blocks:]
    att_ref, states_ref, up_ref, teach_ref, valid_ref, gain_ref = rest[:6]
    layer_ref, mid_ref, hidden, n2t, og_ref, sums_ref = rest[6:12]
    grads, rest = rest[12 : 12 + outs], rest[12 + outs :]
    wo, wu, wd, olt, slots, marks, sems, out_sems, mark_sems = rest
    seq, width = att_ref.shape
    units = wu.shape[1]
    blocked = outs == 2
    mark_copies = []
    if blocked:
        for n, (piece, index, *_) in enumerate(placed(pieces)):
            mark_copies.append(
                pltpu.make_async_copy(
                    piece.at[(*index, pl.ds(0, 16), pl.ds((units + width) // 2, EXTRA))],
                    marks.at[n],
                    mark_sems.at[n],
                )
            )
    copies = weight_copies(spot, pieces, wo, wu, wd, sems)
    for copy in mark_copies + copies[0] + copies[1] + copies[2]:
        copy.start()
    for copy in mark_copies:
        copy.wait()
    total_valid = jnp.full((1, 1), count[0, 0], F32)
    if blocked:
        digits = jnp.sum(marks[...].astype(F32), axis=0)[:1]
        lanes = lax.broadcasted_iota(jnp.int32, digits.shape, 1)
        digits = jnp.where(lanes == 0, digits * 256.0, jnp.where(lanes == 1, digits, 0.0))
        total_valid += jnp.sum(digits, axis=1, keepdims=True)
    factor = tokens / total_valid
    sums_ref[...] = jnp.broadcast_to(total_valid, sums_ref.shape)
    for copy in copies[0]:
        copy.wait()
    mid_ref[...] = states_ref[...] + dot(att_ref[...], wo[...])
    middle = mid_ref[...]
    scale = lax.rsqrt(jnp.mean(middle * middle, axis=1, keepdims=True) + EPSILON)
    n2 = (middle * scale * gain_ref[...]).astype(BF16)
    n2t[...] = n2.T
    for copy in copies[1]:
        copy.wait()

    chunk = 512
    steps = units // chunk

    def up_step(j, _):
        at = pl.ds(pl.multiple_of(j * chunk, chunk), chunk)
        hidden[:, at] = jnp.maximum(dot(n2, wu[:, at]), 0.0).astype(BF16)
        return 0

    lax.fori_loop(0, steps, up_step, 0)
    for copy in copies[2]:
        copy.wait()
    layer_ref[...] = mid_ref[...] + dot_nt(hidden[...], wd[...])
    layer = layer_ref[...]
    valid = valid_ref[...].astype(F32)
    upstream = up_ref[...]
    differ = layer - teach_ref[...]
    sums_ref[1:2, :] = jnp.sum(valid * (differ * differ), axis=0, keepdims=True)
    sums_ref[2:3, :] = jnp.sum(valid * (upstream * layer), axis=0, keepdims=True)
    out_grad = (factor * valid) * (upstream + differ)
    og_ref[...] = out_grad
    olt[...] = out_grad.astype(BF16).T

    def down_step(j, _):
        made = up_copies(spot, slots, grads, out_sems, j, chunk, steps)

        @pl.when(j >= 2)
        def _():
            for copy in up_copies(spot, slots, grads, out_sems, j - 2, chunk, steps):
                copy.wait()

        at = pl.ds(pl.multiple_of(j * chunk, chunk), chunk)
        slots[lax.rem(j, 2)] = dot(olt[...], hidden[:, at]).astype(BF16)
        for copy in made:
            copy.start()
        return 0

    lax.fori_loop(0, steps, down_step, 0)
    for j in (steps - 2, steps - 1):
        for copy in up_copies(spot, slots, grads, out_sems, j, chunk, steps):
            copy.wait()


def weight_copies(spot, pieces, wo, wu, wd, sems):
    units, width = wu.shape[1], wo.shape[1]
    copies = place_copies(
        spot,
        pieces,
        (wo, wu, wd),
        (0, 0, 0),
        (units // 2, 0, (units + width) // 2 + EXTRA),
        (width // 2, units // 2, units // 2),
        sems,
    )
    return copies[::3], copies[1::3], copies[2::3]


def forward_block(blocked, spot, count, tokens, pieces, attended, states, upstream, teacher, valid, gain, units):
    seq, width = attended.shape
    full = jax.ShapeDtypeStruct((seq, width), F32)
    if blocked:
        grads = [jax.ShapeDtypeStruct((4, 4, width // 16, units // 2), BF16)] * 2
    else:
        grads = [jax.ShapeDtypeStruct((width, units), BF16)]
    return pl.pallas_call(
        functools.partial(forward_kernel, len(pieces), len(grads), tokens),
        in_specs=[SMEM, SMEM] + [ANY] * len(pieces) + [VMEM] * 6,
        out_specs=[VMEM] * 6 + [ANY] * len(grads),
        out_shape=[
            full,
            full,
            jax.ShapeDtypeStruct((seq, units), BF16),
            jax.ShapeDtypeStruct((width, seq), BF16),
            full,
            jax.ShapeDtypeStruct((8, width), F32),
        ]
        + grads,
        scratch_shapes=[
            pltpu.VMEM((width, width), BF16),
            pltpu.VMEM((width, units), BF16),
            pltpu.VMEM((width, units), BF16),
            pltpu.VMEM((width, seq), BF16),
            pltpu.VMEM((2, width, 512), BF16),
            pltpu.VMEM((32, 16, EXTRA), BF16),
            pltpu.SemaphoreType.DMA((96,)),
            pltpu.SemaphoreType.DMA((2, 16)),
            pltpu.SemaphoreType.DMA((32,)),
        ],
        compiler_params=PARAMS,
        name="forward",
        cost_estimate=cost(20),
    )(spot, count, *pieces, attended, states, upstream, teacher, valid, gain)


def back_kernel(blocks, blocked, spot, *rest):
    pieces, rest = rest[:blocks], rest[blocks:]
    sources, gain_ref, outs_and_scratch = rest[:5], rest[5], rest[6:]
    mg_ref, agrad_ref, sum_ref = outs_and_scratch[:3]
    grads, rest = outs_and_scratch[3:5], outs_and_scratch[5:]
    wo, wu, wd, hidden, n2t, out_grad, mid_ref, att_ref, pre, attt, slots, sems, in_sems, out_sems = rest
    seq, width = att_ref.shape
    units = wu.shape[1]
    wide = grads if blocked else grads[:1]
    loads = [
        pltpu.make_async_copy(source, target, in_sems.at[n])
        for n, (source, target) in enumerate(zip(sources, (out_grad, hidden, n2t, mid_ref, att_ref)))
    ]
    copies = weight_copies(spot, pieces, wo, wu, wd, sems)
    for copy in [loads[0], *copies[2], *loads[1:3], *copies[1], *loads[3:], *copies[0]]:
        copy.start()
    loads[0].wait()
    out_low = out_grad[...].astype(BF16)
    for copy in [*copies[2], *loads[1:3]]:
        copy.wait()

    chunk = 512
    steps = units // chunk

    def up_step(j, _):
        made = up_copies(spot, slots, wide, out_sems, j, chunk, steps)

        @pl.when(j >= 2)
        def _():
            for copy in up_copies(spot, slots, wide, out_sems, j - 2, chunk, steps):
                copy.wait()

        at = pl.ds(pl.multiple_of(j * chunk, chunk), chunk)
        back = jnp.where(hidden[:, at] > 0, dot(out_low, wd[:, at]), 0.0).astype(BF16)
        pre[:, at] = back
        slots[lax.rem(j, 2)] = dot(n2t[...], back).astype(BF16)
        for copy in made:
            copy.start()
        return 0

    lax.fori_loop(0, steps, up_step, 0)
    for copy in [*copies[1], *loads[3:], *copies[0]]:
        copy.wait()
    grad = dot_nt(pre[...], wu[...])
    middle = mid_ref[...]
    scale = lax.rsqrt(jnp.mean(middle * middle, axis=1, keepdims=True) + EPSILON)
    sum_ref[...] = jnp.broadcast_to(
        jnp.sum(grad * middle * scale, axis=0, keepdims=True), sum_ref.shape
    )
    term = gain_ref[...] * grad
    inner = jnp.mean(term * middle, axis=1, keepdims=True)
    mid_grad = out_grad[...] + scale * term - middle * (scale * scale * scale) * inner
    mg_ref[...] = mid_grad
    branch = mid_grad.astype(BF16)
    agrad_ref[...] = dot_nt(branch, wo[...]).astype(BF16)
    attt[...] = att_ref[...].T
    for j in (steps - 2, steps - 1):
        for copy in up_copies(spot, slots, wide, out_sems, j, chunk, steps):
            copy.wait()
    half = width // 2
    last = []
    for c in range(2):
        slots[c, :, :half] = dot(attt[...], branch[:, c * half : (c + 1) * half]).astype(BF16)
        if blocked:
            made = send_copies(
                spot, slots.at[c], *grads, 0, c, units // 2, half, out_sems.at[c]
            )
        else:
            made = [
                pltpu.make_async_copy(
                    slots.at[c, :, pl.ds(0, half)],
                    grads[1].at[:, pl.ds(c * half, half)],
                    out_sems.at[c, 0],
                )
            ]
        for copy in made:
            copy.start()
        last += made
    for copy in last:
        copy.wait()


def back_block(blocked, spot, pieces, out_grad, hidden, n2t, middle, attended, gain):
    seq, units = hidden.shape
    width = attended.shape[1]
    full = jax.ShapeDtypeStruct((seq, width), F32)
    if blocked:
        grads = [jax.ShapeDtypeStruct((4, 4, width // 16, (units + width) // 2), BF16)] * 2
    else:
        grads = [
            jax.ShapeDtypeStruct((width, units), BF16),
            jax.ShapeDtypeStruct((width, width), BF16),
        ]
    return pl.pallas_call(
        functools.partial(back_kernel, len(pieces), blocked),
        in_specs=[SMEM] + [ANY] * (len(pieces) + 5) + [VMEM],
        out_specs=[VMEM] * 3 + [ANY] * len(grads),
        out_shape=[
            full,
            jax.ShapeDtypeStruct((seq, width), BF16),
            jax.ShapeDtypeStruct((8, width), F32),
        ]
        + grads,
        scratch_shapes=[
            pltpu.VMEM((width, width), BF16),
            pltpu.VMEM((width, units), BF16),
            pltpu.VMEM((width, units), BF16),
            pltpu.VMEM((seq, units), BF16),
            pltpu.VMEM((width, seq), BF16),
            pltpu.VMEM((seq, width), F32),
            pltpu.VMEM((seq, width), F32),
            pltpu.VMEM((seq, width), BF16),
            pltpu.VMEM((seq, units), BF16),
            pltpu.VMEM((width, seq), BF16),
            pltpu.VMEM((2, width, 512), BF16),
            pltpu.SemaphoreType.DMA((96,)),
            pltpu.SemaphoreType.DMA((5,)),
            pltpu.SemaphoreType.DMA((2, 16)),
        ],
        compiler_params=PARAMS,
        name="back",
        cost_estimate=cost(20),
    )(spot, *pieces, out_grad, hidden, n2t, middle, attended, gain)


def attend_back_kernel(
    blocked, spot, pms, pos, nt_ref, q_ref, k_ref, v_ref, g_ref, p_ref, pm_ref, po_ref,
    dq_ref, dk_ref, dv_ref, pre_ref, post_ref, *rest,
):
    outs = 2 if blocked else 3
    grads = rest[:outs]
    vt, qt, gt, dq, dkt, dvt, slots, sems = rest[outs:]
    step = pl.program_id(0)
    seq, width = q_ref.shape
    half = seq // 2

    @pl.when(step == 0)
    def _():
        vt[...] = v_ref[...].T
        qt[...] = q_ref[...].T
        gt[...] = g_ref[...].T
        dq[...] = jnp.zeros_like(dq)
        dkt[...] = jnp.zeros_like(dkt)
        dvt[...] = jnp.zeros_like(dvt)

    pm = pm_ref[0]
    po = po_ref[0]
    p0, p1, p2 = (p_ref[0, :, b * half : (b + 1) * half] for b in range(3))
    top = (g_ref[:half].astype(F32) * po).astype(BF16)
    low = (g_ref[half:].astype(F32) * po).astype(BF16)
    g0 = dot(top, vt[:, :half])
    g1 = dot(low, vt[:, :half])
    g2 = dot(low, vt[:, half:])
    u0 = dot(gt[:, :half], p0) + dot(gt[:, half:], p1)
    u1 = dot(gt[:, half:], p2)
    f0, f1, f2 = p0.astype(F32), p1.astype(F32), p2.astype(F32)
    t0 = f0 * g0
    d0 = (t0 - f0 * jnp.sum(t0, axis=1, keepdims=True)).astype(BF16)
    t1, t2 = f1 * g1, f2 * g2
    r1 = jnp.sum(t1, axis=1, keepdims=True) + jnp.sum(t2, axis=1, keepdims=True)
    d1 = (t1 - f1 * r1).astype(BF16)
    d2 = (t2 - f2 * r1).astype(BF16)
    w0 = dot(d0, k_ref[:half])
    w1 = dot(d1, k_ref[:half]) + dot(d2, k_ref[half:])
    dq[:half] += pm * w0
    dq[half:] += pm * w1
    pre_ref[0] = jnp.sum(q_ref[:half].astype(F32) * w0, axis=0, keepdims=True) + jnp.sum(
        q_ref[half:].astype(F32) * w1, axis=0, keepdims=True
    )
    for g in range(HEADS):
        at = slice(g * HEAD_DIM, (g + 1) * HEAD_DIM)
        b = pos[step, g]
        u0g, u1g = u0[at], u1[at]
        dvt[at, :half] += b * u0g
        dvt[at, half:] += b * u1g
        both = u0g * vt[at, :half].astype(F32) + u1g * vt[at, half:].astype(F32)
        post_ref[0, g : g + 1, :] = jnp.sum(both, axis=0, keepdims=True)
    qs = jnp.concatenate(
        [
            (qt[g * HEAD_DIM : (g + 1) * HEAD_DIM].astype(F32) * pms[step, g]).astype(BF16)
            for g in range(HEADS)
        ],
        axis=0,
    )
    dkt[:, :half] += dot(qs[:, :half], d0) + dot(qs[:, half:], d1)
    dkt[:, half:] += dot(qs[:, half:], d2)

    @pl.when(step == HEADS - 1)
    def _():
        dq_ref[...] = dq[...].astype(BF16)
        dk_ref[...] = dkt[...].astype(BF16).T
        dv_ref[...] = dvt[...].astype(BF16).T
        made = []
        for n, ref in enumerate((dq_ref, dk_ref, dv_ref)):
            slots[n] = dot(nt_ref[...], ref[...]).astype(BF16)
            if blocked:
                part = width // 2
                for c in range(2):
                    made += send_copies(
                        spot,
                        slots.at[n, :, pl.ds(c * part, part)],
                        grads[0],
                        grads[1],
                        n * (width // 16),
                        c,
                        0,
                        part,
                        sems.at[2 * n + c],
                        True,
                    )
            else:
                made.append(pltpu.make_async_copy(slots.at[n], grads[n], sems.at[n, 0]))
            for copy in made[-32 if blocked else -1 :]:
                copy.start()
        for copy in made:
            copy.wait()


def attend_back(spot, blocked, nt, q, k, v, g, p, pm, po, pms, pos):
    seq, width = q.shape
    half = seq // 2
    whole = pl.BlockSpec((seq, width), lambda h: (0, 0))
    row = pl.BlockSpec((1, 1, width), lambda h: (h, 0, 0))
    low = jax.ShapeDtypeStruct((seq, width), BF16)
    if blocked:
        grads = [jax.ShapeDtypeStruct((4, 4, 3 * (width // 16), width // 2), BF16)] * 2
    else:
        grads = [jax.ShapeDtypeStruct((width, width), BF16)] * 3
    return pl.pallas_call(
        functools.partial(attend_back_kernel, blocked),
        grid=(HEADS,),
        in_specs=[SMEM, SMEM, SMEM, pl.BlockSpec((width, seq), lambda h: (0, 0))]
        + [whole] * 4
        + [pl.BlockSpec((1, half, 3 * half), lambda h: (h, 0, 0)), row, row],
        out_specs=[whole] * 3
        + [row, pl.BlockSpec((1, HEADS, half), lambda h: (h, 0, 0))]
        + [ANY] * len(grads),
        out_shape=[low] * 3
        + [
            jax.ShapeDtypeStruct((HEADS, 1, width), F32),
            jax.ShapeDtypeStruct((HEADS, HEADS, half), F32),
        ]
        + grads,
        scratch_shapes=[pltpu.VMEM((width, seq), BF16)] * 3
        + [
            pltpu.VMEM((seq, width), F32),
            pltpu.VMEM((width, seq), F32),
            pltpu.VMEM((width, seq), F32),
            pltpu.VMEM((3, width, width), BF16),
            pltpu.SemaphoreType.DMA((6, 16)),
        ],
        compiler_params=PARAMS,
        name="attend_back",
        cost_estimate=cost(28),
    )(spot, pms, pos, nt, q, k, v, g, p, pm, po)


def input_kernel(blocks, spot, *rest):
    pieces, rest = rest[:blocks], rest[blocks:]
    dq_ref, dk_ref, dv_ref, states_ref, mid_ref, gain_ref, out_ref, first_ref = rest[:8]
    wq, wk, wv, sems = rest[8:]
    width = wq.shape[1] // 2
    depth = wq.shape[0] // 16
    copies = place_copies(
        spot, pieces, (wq, wk, wv), (0, depth, 2 * depth), (0, 0, 0), (width,) * 3, sems, True
    )
    for copy in copies:
        copy.start()
    states = states_ref[...]
    scale = lax.rsqrt(jnp.mean(states * states, axis=1, keepdims=True) + EPSILON)
    for copy in copies:
        copy.wait()
    grad = (
        dot_nt(dq_ref[...], wq[...]) + dot_nt(dk_ref[...], wk[...]) + dot_nt(dv_ref[...], wv[...])
    )
    first_ref[...] = jnp.broadcast_to(
        jnp.sum(grad * states * scale, axis=0, keepdims=True), first_ref.shape
    )
    term = gain_ref[...] * grad
    inner = jnp.mean(term * states, axis=1, keepdims=True)
    out_ref[...] = mid_ref[...] + scale * term - states * (scale * scale * scale) * inner


def input_block(spot, pieces, dq, dk, dv, states, mid_grad, gain):
    seq, width = dq.shape
    return pl.pallas_call(
        functools.partial(input_kernel, len(pieces)),
        in_specs=[SMEM] + [ANY] * len(pieces) + [VMEM] * 6,
        out_specs=[VMEM] * 2,
        out_shape=[
            jax.ShapeDtypeStruct((seq, width), F32),
            jax.ShapeDtypeStruct((8, width), F32),
        ],
        scratch_shapes=[pltpu.VMEM((width, width), BF16)] * 3 + [pltpu.SemaphoreType.DMA((96,))],
        compiler_params=PARAMS,
        name="input_grad",
        cost_estimate=cost(9),
    )(spot, *pieces, dq, dk, dv, states, mid_grad, gain)


def exchange(value, mask, total):
    return lax.ppermute(value, AXES, [(i, i ^ mask) for i in range(total)])


def after(value, *others):
    return lax.optimization_barrier((value, *others))[0]


def over_lines(blocks):
    return lax.all_to_all(blocks, "row", 0, 0, axis_index_groups=LINES, tiled=True)


def gather_line(packet):
    return over_lines(jnp.broadcast_to(packet, (4, *packet.shape)))


def gather_near(packet, total):
    return jnp.stack([packet, *[exchange(packet, m * Z_BIT, total) for m in (1, 2, 3)]])


def gather_sides(line, total):
    return exchange(line, X_BIT, total), exchange(line, Y_BIT, total)


def gather_halves(over_x, over_y, total):
    return exchange(over_x[:2], Y_BIT, total), exchange(over_y[2:], X_BIT, total)


def add_low(*terms):
    return functools.reduce(jnp.add, [t.astype(F32) for t in terms])


def reduce_core(keep, other):
    mine = add_low(keep, other).astype(BF16)
    return mine, mine[2:, :2], mine[1::2, 2:]


def reduce_first(over_y, over_x, total):
    return exchange(over_y, Y_BIT, total), exchange(over_x, X_BIT, total)


def reduce_sides(mine, over_y, over_x):
    return add_low(mine[1, :2], over_y[1]).astype(BF16), add_low(mine[2, 2:], over_x[1]).astype(BF16)


def reduce_second(side_x, side_y, total):
    return exchange(side_x, X_BIT, total), exchange(side_y, Y_BIT, total)


def reduce_own(mine, over_y, over_x):
    return add_low(mine[0, :2], over_y[0]), add_low(mine[0, 2:], over_x[0])


def reduce_line(head, tail, side_x, side_y):
    return over_lines(jnp.concatenate([add_low(head, side_x), add_low(tail, side_y)]).astype(BF16))


def reduce_near(head, tail, side_x, side_y, total):
    line = jnp.concatenate([add_low(head, side_x), add_low(tail, side_y)])
    return add_low(line[0], *[exchange(line[m].astype(BF16), m * Z_BIT, total) for m in (1, 2, 3)])


def pack_small(first_rows, second_rows, sums, pre, post):
    pre = jnp.sum(pre.reshape(HEADS, HEADS, HEAD_DIM), axis=2).T * (HEAD_DIM**-0.5)
    losses = jnp.sum(sums[1:3], axis=1)
    small = [first_rows[0], second_rows[0], pre.reshape(-1), jnp.sum(post, axis=2).reshape(-1), losses]
    small = jnp.concatenate(small)
    return jnp.pad(small, (0, -small.shape[0] % 1024)).reshape(-1, 128)


def gather_whole(block):
    rows, cols = lax.axis_size("row"), lax.axis_size("col")
    depth, width = block.shape
    every = lax.all_gather(block[None], AXES, axis=0, tiled=True)
    every = every.reshape(rows, cols, depth, width).transpose(0, 2, 1, 3)
    return every.reshape(rows * depth, cols * width)


def scatter_whole(grad):
    rows, cols = lax.axis_size("row"), lax.axis_size("col")
    depth, width = grad.shape[0] // rows, grad.shape[1] // cols
    parts = grad.reshape(rows, depth, cols, width).transpose(0, 2, 1, 3)
    parts = parts.reshape(rows * cols, depth, width).astype(F32)
    return lax.psum_scatter(parts, AXES, scatter_dimension=0, tiled=True)[0]


def shards(
    states,
    upstream,
    teacher,
    validity,
    picture_start,
    first_gain,
    query_weight,
    key_weight,
    value_weight,
    premix,
    postmix,
    output_weight,
    second_gain,
    up_weight,
    down_weight,
):
    row_total = lax.axis_size("row")
    col_total = lax.axis_size("col")
    total = row_total * col_total
    seq_len, features = states.shape
    depth, width = query_weight.shape
    units = up_weight.shape[1] * col_total
    blocked = (row_total, col_total) == (16, 2)
    row = lax.axis_index("row")
    spot = jnp.stack([row // 4, (row // 2) % 2, row % 2, lax.axis_index("col")]).astype(jnp.int32)
    count = jnp.sum(validity)
    down_turned = down_weight.T
    if blocked:
        packet = jnp.concatenate([query_weight, key_weight, value_weight], axis=0)
        qkv_line = gather_near(packet, total)
        qkv_sides = gather_sides(qkv_line, total)
        lanes = lax.broadcasted_iota(jnp.int32, (depth, EXTRA), 1)
        digits = jnp.where(lanes == 0, count // 256, jnp.where(lanes == 1, count % 256, 0))
        packet = jnp.concatenate(
            [up_weight, output_weight, digits.astype(BF16), down_turned], axis=1
        )
        line = gather_line(packet)
        qkv_halves = jnp.stack(gather_halves(*qkv_sides, total))
        qkv_lines = jnp.stack([qkv_line, *qkv_sides])
        qkv = [qkv_lines, qkv_halves]
        qkv += [exchange(part, CORE_BIT, total) for part in qkv]
        line, *qkv = lax.optimization_barrier((line, *qkv))
        sides = gather_sides(line, total)
        total_valid = jnp.zeros((), F32)
    else:
        qkv = [gather_whole(w) for w in (query_weight, key_weight, value_weight)]
        rest = [gather_whole(w) for w in (output_weight, up_weight, down_turned)]
        total_valid = lax.psum(count.astype(F32), AXES)
    first_scale = lax.rsqrt(jnp.mean(states * states, axis=-1, keepdims=True) + EPSILON)
    normed = (states * first_scale * first_gain).astype(BF16)
    pms = premix.T * (HEAD_DIM**-0.5)
    pos = postmix
    pm = jnp.repeat(pms, HEAD_DIM, axis=1)[:, None]
    po = jnp.repeat(pos, HEAD_DIM, axis=1)[:, None]
    queries, keys, values, attended, probs = attend(spot, picture_start, normed, qkv, pm, po)
    if blocked:
        *sides, attended = lax.optimization_barrier((*sides, attended))
        rest = [jnp.stack([line, *sides]), jnp.stack(gather_halves(*sides, total))]
        rest += [exchange(part, CORE_BIT, total) for part in rest]
    layer_out, middle, hidden, n2t, out_grad, sums, *grads = forward_block(
        blocked,
        spot,
        total_valid.reshape(1, 1),
        seq_len * total,
        rest,
        attended,
        states,
        upstream,
        teacher,
        validity[:, None],
        second_gain[None],
        units,
    )
    total_valid = sums[3, 0]
    if blocked:
        *mine, out_grad = lax.optimization_barrier(
            (*reduce_core(grads[0], exchange(grads[1], CORE_BIT, total)), out_grad)
        )
        down_mine, down_first = mine[0], reduce_first(*mine[1:], total)
    else:
        down_grad = scatter_whole(grads[0]).T
    mid_grad, attended_grad, second_rows, *grads = back_block(
        blocked, spot, rest, out_grad, hidden, n2t, middle, attended, second_gain[None]
    )
    nt = normed.T
    if blocked:
        over_y, over_x, attended_grad, *grads = lax.optimization_barrier(
            (*down_first, attended_grad, *grads)
        )
        down_sides = reduce_sides(down_mine, over_y, over_x)
        down_own = reduce_own(down_mine, over_y, over_x)
        *mine, side_x, side_y, attended_grad = lax.optimization_barrier(
            (*reduce_core(grads[0], exchange(grads[1], CORE_BIT, total)), *down_sides, attended_grad)
        )
        up_mine, up_first = mine[0], reduce_first(*mine[1:], total)
        down_sides = reduce_second(side_x, side_y, total)
    else:
        up_grad, output_grad = (scatter_whole(g) for g in grads)
    dq, dk, dv, pre, post, *grads = attend_back(
        spot, blocked, nt, queries, keys, values, attended_grad, probs, pm, po, pms, pos
    )
    if blocked:
        rest = lax.optimization_barrier((dq, dk, dv, *grads, *up_first, *down_sides, pre, post))
        dq, dk, dv, *rest, pre, post = rest
        grads, up_first, down_sides = rest[:2], rest[2:4], rest[4:]
        *mine, dq, dk, dv = lax.optimization_barrier(
            (*reduce_core(grads[0], exchange(grads[1], CORE_BIT, total)), dq, dk, dv)
        )
        mine, first = mine[0], reduce_first(*mine[1:], total)
        up_sides = reduce_second(*reduce_sides(up_mine, *up_first), total)
        down_line = reduce_line(*down_own, *down_sides)
        input_grad, first_rows = input_block(
            spot, qkv, dq, dk, dv, states, mid_grad, first_gain[None]
        )
        *rest, first_rows, second_rows, pre, post = lax.optimization_barrier(
            (*first, *up_sides, first_rows, second_rows, pre, post)
        )
        first, up_sides = rest[:2], rest[2:]
        sides = reduce_sides(mine, *first)
        small = pack_small(first_rows, second_rows, sums, pre, post)
        small += exchange(small, CORE_BIT, total)
        small = after(small, *sides)
        sides = reduce_second(*sides, total)
        for bit in (X_BIT, Y_BIT):
            small += exchange(small, bit, total)
        up_line = reduce_line(*reduce_own(up_mine, *up_first), *up_sides)
        *sides, down_line, small = lax.optimization_barrier((*sides, down_line, small))
        line = reduce_near(*reduce_own(mine, *first), *sides, total)
        for bit in (Z_BIT, 2 * Z_BIT):
            small += exchange(small, bit, total)
        down_grad, ffn = (jnp.sum(w.astype(F32), axis=0) for w in (down_line, up_line))
        down_grad = down_grad.T
        up_grad, output_grad = ffn[:, : units // col_total], ffn[:, units // col_total :]
        query_grad, key_grad, value_grad = (line[n * depth : (n + 1) * depth] for n in range(3))
    else:
        query_grad, key_grad, value_grad = (scatter_whole(g) for g in grads)
        input_grad, first_rows = input_block(
            spot, qkv, dq, dk, dv, states, mid_grad, first_gain[None]
        )
        small = lax.psum(pack_small(first_rows, second_rows, sums, pre, post), AXES)
    small = small.reshape(-1)
    mixes = HEADS * HEADS
    first_grad, second_grad, premix_grad, postmix_grad, losses = jnp.split(
        small, [features, 2 * features, 2 * features + mixes, 2 * features + 2 * mixes]
    )
    return (
        layer_out,
        losses[0] / (total_valid * features),
        losses[1] / total_valid,
        input_grad,
        first_grad,
        query_grad,
        key_grad,
        value_grad,
        premix_grad.reshape(HEADS, HEADS),
        postmix_grad.reshape(HEADS, HEADS),
        output_grad,
        second_grad,
        up_grad,
        down_grad,
    )


def solution(mesh):
    tokens, block = P(AXES, None), P("row", "col")
    return jax.shard_map(
        shards,
        mesh=mesh,
        in_specs=(
            tokens, tokens, tokens, P(AXES), tokens, P(), block, block, block, P(), P(), block,
            P(), block, P("col", "row"),
        ),
        out_specs=(
            tokens, P(), P(), tokens, P(), block, block, block, P(), P(), block, P(), block,
            P("col", "row"),
        ),
        check_vma=False,
    )
```

```python
import functools

import jax
import jax.numpy as jnp
from jax import lax
from jax.experimental import pallas as pl
from jax.experimental.layout import Layout, with_layout_constraint
from jax.experimental.pallas import tpu as pltpu
from jax.sharding import PartitionSpec as P

HEADS = 12
HEAD_DIM = 64
PIC = 256
EPSILON = 1e-06
F32 = jnp.float32
BF16 = jnp.bfloat16
AXES = ("row", "col")
X_BIT, CORE_BIT, Y_BIT, Z_BIT = 1, 2, 4, 8
LINES = [[at + Z_BIT // 2 * z for z in range(4)] for at in range(4)]
EXTRA = 128
SIDES = ((0, 0), (0, 1), (1, 0))
PARAMS = pltpu.CompilerParams(vmem_limit_bytes=60000 * 1024)
SMEM = pl.BlockSpec(memory_space=pltpu.SMEM)
ANY = pl.BlockSpec(memory_space=pl.ANY)
VMEM = pl.BlockSpec(memory_space=pltpu.VMEM)


def dot(a, b):
    return lax.dot_general(a, b, (((1,), (0,)), ((), ())), preferred_element_type=F32)


def dot_nt(a, b):
    return lax.dot_general(a, b, (((1,), (1,)), ((), ())), preferred_element_type=F32)


def cost(micros):
    return pl.CostEstimate(flops=micros * 10**9, bytes_accessed=10**6, transcendentals=0)


def placed(pieces):
    for core in range(2):
        lines, halves = pieces[2 * core : 2 * core + 2]
        for n, (y, x) in enumerate(SIDES):
            for z in range(4):
                yield lines, (n, z), core, y, x, z
        for z in range(4):
            yield halves, (z // 2, z % 2), core, 1, 1, z


def place_copies(spot, pieces, wholes, rows_at, cols_at, widths, sems, near=False):
    if len(pieces) == len(wholes):
        return [
            pltpu.make_async_copy(piece, whole, sems.at[n])
            for n, (piece, whole) in enumerate(zip(pieces, wholes))
        ]
    copies = []
    for piece, index, core, y, x, z in placed(pieces):
        r = ((spot[0] ^ z if near else z) * 2 + (spot[1] ^ y)) * 2 + (spot[2] ^ core)
        c = spot[3] ^ x
        for whole, row, col, width in zip(wholes, rows_at, cols_at, widths):
            depth = whole.shape[0] // 16
            copies.append(
                pltpu.make_async_copy(
                    piece.at[(*index, pl.ds(row, depth), pl.ds(col, width))],
                    whole.at[
                        pl.ds(pl.multiple_of(r * depth, 16), depth),
                        pl.ds(pl.multiple_of(c * width, 128), width),
                    ],
                    sems.at[len(copies)],
                )
            )
    return copies


def send_copies(spot, source, keep, send, row, half, col, width, sems, near=False):
    depth = source.shape[0] // 16
    copies = []
    for j in range(8):
        z, y = j // 2, j % 2
        plane = (spot[1] ^ y) * 2 + (spot[3] ^ half)
        for n, (target, core) in enumerate(((keep, spot[2]), (send, 1 - spot[2]))):
            start = pl.multiple_of((2 * j + core) * depth, 16)
            copies.append(
                pltpu.make_async_copy(
                    source.at[pl.ds(start, depth), pl.ds(0, width)],
                    target.at[plane, spot[0] ^ z if near else z, pl.ds(row, depth), pl.ds(col, width)],
                    sems.at[2 * j + n],
                )
            )
    return copies


def attend_kernel(blocks, spot, starts, normed_ref, *rest):
    pieces, rest = rest[:blocks], rest[blocks:]
    pm_ref, po_ref, q_ref, k_ref, v_ref, out_ref, p_ref, wq, wk, wv, kt, bias, acc, sems = rest
    step = pl.program_id(0)
    half = normed_ref.shape[0] // 2

    @pl.when(step == 0)
    def _():
        width = wq.shape[1] // 2
        depth = wq.shape[0] // 16
        copies = place_copies(
            spot, pieces, (wq, wk, wv), (0, depth, 2 * depth), (0, 0, 0), (width,) * 3, sems, True
        )
        for copy in copies:
            copy.start()
        rows = lax.broadcasted_iota(jnp.int32, (half, half), 0)
        cols = lax.broadcasted_iota(jnp.int32, (half, half), 1)
        for b in range(2):
            i, j = rows + b * half, cols + b * half
            ok = j <= i
            for s in range(2):
                p = starts[0, s]
                ok = ok | ((i >= p) & (i < p + PIC) & (j >= p) & (j < p + PIC))
            bias[b] = jnp.where(ok, 0.0, -1e30)
        acc[...] = jnp.zeros_like(acc)
        for copy in copies:
            copy.wait()
        k_ref[...] = dot(normed_ref[...], wk[...]).astype(BF16)
        kt[...] = k_ref[...].T
        q_ref[...] = dot(normed_ref[...], wq[...]).astype(BF16)
        v_ref[...] = dot(normed_ref[...], wv[...]).astype(BF16)

    pm = pm_ref[0]
    po = po_ref[0]
    vs = (v_ref[...].astype(F32) * po).astype(BF16)
    top = (q_ref[:half].astype(F32) * pm).astype(BF16)
    low = (q_ref[half:].astype(F32) * pm).astype(BF16)
    s0 = dot(top, kt[:, :half]) + bias[0]
    s1 = dot(low, kt[:, :half])
    s2 = dot(low, kt[:, half:]) + bias[1]
    m0 = jnp.max(s0, axis=1, keepdims=True)
    e0 = jnp.exp(s0 - m0)
    p0 = (e0 / jnp.sum(e0, axis=1, keepdims=True)).astype(BF16)
    m1 = jnp.maximum(jnp.max(s1, axis=1, keepdims=True), jnp.max(s2, axis=1, keepdims=True))
    e1 = jnp.exp(s1 - m1)
    e2 = jnp.exp(s2 - m1)
    inv = 1.0 / (jnp.sum(e1, axis=1, keepdims=True) + jnp.sum(e2, axis=1, keepdims=True))
    p1 = (e1 * inv).astype(BF16)
    p2 = (e2 * inv).astype(BF16)
    p_ref[0, :, :half] = p0
    p_ref[0, :, half : 2 * half] = p1
    p_ref[0, :, 2 * half :] = p2
    acc[:half] += dot(p0, vs[:half])
    acc[half:] += dot(p1, vs[:half]) + dot(p2, vs[half:])

    @pl.when(step == HEADS - 1)
    def _():
        out_ref[...] = acc[...].astype(BF16)


def attend(spot, starts, normed, pieces, pm, po):
    seq, width = normed.shape
    half = seq // 2
    whole = pl.BlockSpec((seq, width), lambda h: (0, 0))
    row = pl.BlockSpec((1, 1, width), lambda h: (h, 0, 0))
    low = jax.ShapeDtypeStruct((seq, width), BF16)
    return pl.pallas_call(
        functools.partial(attend_kernel, len(pieces)),
        grid=(HEADS,),
        in_specs=[SMEM, SMEM, whole] + [ANY] * len(pieces) + [row, row],
        out_specs=[whole] * 4 + [pl.BlockSpec((1, half, 3 * half), lambda h: (h, 0, 0))],
        out_shape=[low] * 4 + [jax.ShapeDtypeStruct((HEADS, half, 3 * half), BF16)],
        scratch_shapes=[pltpu.VMEM((width, width), BF16)] * 3
        + [
            pltpu.VMEM((width, seq), BF16),
            pltpu.VMEM((2, half, half), F32),
            pltpu.VMEM((seq, width), F32),
            pltpu.SemaphoreType.DMA((96,)),
        ],
        compiler_params=PARAMS,
        name="attend",
        cost_estimate=cost(20),
    )(spot, starts, normed, *pieces, pm, po)


def middle_kernel(blocks, outs, tokens, spot, count, *rest):
    pieces, rest = rest[:blocks], rest[blocks:]
    att_ref, states_ref, up_ref, teach_ref, valid_ref, gain_ref = rest[:6]
    layer_ref, mid_ref, agrad_ref, sums_ref = rest[6:10]
    grads, rest = rest[10 : 10 + outs], rest[10 + outs :]
    wo, wu, wd, hidden, pre, n2t, olt, slots, marks, sems, out_sems, mark_sems = rest
    seq, width = att_ref.shape
    units = wu.shape[1]
    blocked = outs == 2
    mark_copies = []
    if blocked:
        for n, (piece, index, *_) in enumerate(placed(pieces)):
            mark_copies.append(
                pltpu.make_async_copy(
                    piece.at[(*index, pl.ds(0, 16), pl.ds((units + width) // 2, EXTRA))],
                    marks.at[n],
                    mark_sems.at[n],
                )
            )
    copies = place_copies(
        spot,
        pieces,
        (wo, wu, wd),
        (0, 0, 0),
        (units // 2, 0, (units + width) // 2 + EXTRA),
        (width // 2, units // 2, units // 2),
        sems,
    )
    for copy in mark_copies + copies[::3] + copies[1::3] + copies[2::3]:
        copy.start()
    for copy in mark_copies:
        copy.wait()
    total_valid = jnp.full((1, 1), count[0, 0], F32)
    if blocked:
        by_lane = jnp.sum(marks[...].astype(F32), axis=0)[:1]
        total_valid += jnp.sum(by_lane, axis=1, keepdims=True)
    factor = tokens / total_valid
    sums_ref[...] = jnp.broadcast_to(total_valid, sums_ref.shape)
    for copy in copies[::3]:
        copy.wait()
    mid_ref[...] = states_ref[...] + dot(att_ref[...], wo[...])
    middle = mid_ref[...]
    scale = lax.rsqrt(jnp.mean(middle * middle, axis=1, keepdims=True) + EPSILON)
    n2 = (middle * scale * gain_ref[...]).astype(BF16)
    n2t[...] = n2.T
    for copy in copies[1::3]:
        copy.wait()

    chunk = 512
    steps = units // chunk

    def up_step(j, _):
        at = pl.ds(pl.multiple_of(j * chunk, chunk), chunk)
        hidden[:, at] = jnp.maximum(dot(n2, wu[:, at]), 0.0).astype(BF16)
        return 0

    lax.fori_loop(0, steps, up_step, 0)
    for copy in copies[2::3]:
        copy.wait()
    layer_ref[...] = mid_ref[...] + dot_nt(hidden[...], wd[...])
    layer = layer_ref[...]
    valid = valid_ref[...].astype(F32)
    upstream = up_ref[...]
    differ = layer - teach_ref[...]
    sums_ref[1:2, :] = jnp.sum(valid * (differ * differ), axis=0, keepdims=True)
    sums_ref[2:3, :] = jnp.sum(valid * (upstream * layer), axis=0, keepdims=True)
    out_grad = (factor * valid) * (upstream + differ)
    out_low = out_grad.astype(BF16)
    olt[...] = out_low.T

    def down_step(j, _):
        at = pl.ds(pl.multiple_of(j * chunk, chunk), chunk)
        part = hidden[:, at]
        back = jnp.where(part > 0, dot(out_low, wd[:, at]), 0.0).astype(BF16)
        pre[:, at] = back
        for which, (left, right) in enumerate(((n2t, back), (olt, part))):
            slot = slots.at[which]

            @pl.when(j > 0)
            def _():
                for copy in grad_copies(which, j - 1):
                    copy.wait()

            slot[...] = dot(left[...], right).astype(BF16)
            for copy in grad_copies(which, j):
                copy.start()
        return 0

    def grad_copies(which, j):
        if not blocked:
            at = pl.ds(pl.multiple_of(j * chunk, chunk), chunk)
            return [pltpu.make_async_copy(slots.at[which], grads[which].at[:, at], out_sems.at[which, 0])]
        per = steps // 2
        return send_copies(
            spot,
            slots.at[which],
            grads[0],
            grads[1],
            0,
            j // per,
            pl.multiple_of(which * ((units + width) // 2) + (j % per) * chunk, 128),
            chunk,
            out_sems.at[which],
            True,
        )

    lax.fori_loop(0, steps, down_step, 0)
    grad = dot_nt(pre[...], wu[...])
    middle = mid_ref[...]
    scale = lax.rsqrt(jnp.mean(middle * middle, axis=1, keepdims=True) + EPSILON)
    sums_ref[0:1, :] = jnp.sum(grad * middle * scale, axis=0, keepdims=True)
    term = gain_ref[...] * grad
    inner = jnp.mean(term * middle, axis=1, keepdims=True)
    layer = layer_ref[...]
    out_grad = (factor * valid_ref[...].astype(F32)) * (
        up_ref[...] + (layer - teach_ref[...])
    )
    mid_grad = out_grad + scale * term - middle * (scale * scale * scale) * inner
    mid_ref[...] = mid_grad
    branch = mid_grad.astype(BF16)
    agrad_ref[...] = dot_nt(branch, wo[...]).astype(BF16)
    n2t[...] = att_ref[...].T
    for which in range(2):
        for copy in grad_copies(which, steps - 1):
            copy.wait()
    half = width // 2
    last = []
    for c in range(2):
        slots[c, :, :half] = dot(n2t[...], branch[:, c * half : (c + 1) * half]).astype(BF16)
        if blocked:
            made = send_copies(
                spot, slots.at[c], grads[0], grads[1], 0, c, units // 2, half, out_sems.at[c], True
            )
        else:
            made = [
                pltpu.make_async_copy(
                    slots.at[c, :, pl.ds(0, half)],
                    grads[2].at[:, pl.ds(c * half, half)],
                    out_sems.at[c, 0],
                )
            ]
        for copy in made:
            copy.start()
        last += made
    for copy in last:
        copy.wait()


def middle_block(blocked, spot, count, tokens, pieces, attended, states, upstream, teacher, valid, gain, units):
    seq, width = attended.shape
    full = jax.ShapeDtypeStruct((seq, width), F32)
    if blocked:
        depth = width // 16
        grads = [jax.ShapeDtypeStruct((4, 4, depth, units + width // 2), BF16)] * 2
    else:
        grads = [
            jax.ShapeDtypeStruct((width, units), BF16),
            jax.ShapeDtypeStruct((width, units), BF16),
            jax.ShapeDtypeStruct((width, width), BF16),
        ]
    return pl.pallas_call(
        functools.partial(middle_kernel, len(pieces), len(grads), tokens),
        in_specs=[SMEM, SMEM] + [ANY] * len(pieces) + [VMEM] * 6,
        out_specs=[VMEM] * 4 + [ANY] * len(grads),
        out_shape=[
            full,
            full,
            jax.ShapeDtypeStruct((seq, width), BF16),
            jax.ShapeDtypeStruct((8, width), F32),
        ]
        + grads,
        scratch_shapes=[
            pltpu.VMEM((width, width), BF16),
            pltpu.VMEM((width, units), BF16),
            pltpu.VMEM((width, units), BF16),
            pltpu.VMEM((seq, units), BF16),
            pltpu.VMEM((seq, units), BF16),
            pltpu.VMEM((width, seq), BF16),
            pltpu.VMEM((width, seq), BF16),
            pltpu.VMEM((2, width, 512), BF16),
            pltpu.VMEM((32, 16, EXTRA), BF16),
            pltpu.SemaphoreType.DMA((96,)),
            pltpu.SemaphoreType.DMA((2, 16)),
            pltpu.SemaphoreType.DMA((32,)),
        ],
        compiler_params=PARAMS,
        name="middle",
        cost_estimate=cost(35),
    )(spot, count, *pieces, attended, states, upstream, teacher, valid, gain)


def attend_back_kernel(
    blocked, spot, pms, pos, nt_ref, q_ref, k_ref, v_ref, g_ref, p_ref, pm_ref, po_ref,
    dq_ref, dk_ref, dv_ref, mix_ref, *rest,
):
    outs = 2 if blocked else 3
    grads = rest[:outs]
    vt, qt, gt, dq, dkt, dvt, pre, slots, sems = rest[outs:]
    step = pl.program_id(0)
    seq, width = q_ref.shape
    half = seq // 2

    @pl.when(step == 0)
    def _():
        vt[...] = v_ref[...].T
        qt[...] = q_ref[...].T
        gt[...] = g_ref[...].T
        dq[...] = jnp.zeros_like(dq)
        dkt[...] = jnp.zeros_like(dkt)
        dvt[...] = jnp.zeros_like(dvt)
        pre[...] = jnp.zeros_like(pre)
        mix_ref[...] = jnp.zeros_like(mix_ref)

    pm = pm_ref[0]
    po = po_ref[0]
    p0, p1, p2 = (p_ref[0, :, b * half : (b + 1) * half] for b in range(3))
    top = (g_ref[:half].astype(F32) * po).astype(BF16)
    low = (g_ref[half:].astype(F32) * po).astype(BF16)
    g0 = dot(top, vt[:, :half])
    g1 = dot(low, vt[:, :half])
    g2 = dot(low, vt[:, half:])
    u0 = dot(gt[:, :half], p0) + dot(gt[:, half:], p1)
    u1 = dot(gt[:, half:], p2)
    f0, f1, f2 = p0.astype(F32), p1.astype(F32), p2.astype(F32)
    t0 = f0 * g0
    d0 = (t0 - f0 * jnp.sum(t0, axis=1, keepdims=True)).astype(BF16)
    t1, t2 = f1 * g1, f2 * g2
    r1 = jnp.sum(t1, axis=1, keepdims=True) + jnp.sum(t2, axis=1, keepdims=True)
    d1 = (t1 - f1 * r1).astype(BF16)
    d2 = (t2 - f2 * r1).astype(BF16)
    w0 = dot(d0, k_ref[:half])
    w1 = dot(d1, k_ref[:half]) + dot(d2, k_ref[half:])
    dq[:half] += pm * w0
    dq[half:] += pm * w1
    row = jnp.sum(q_ref[:half].astype(F32) * w0, axis=0, keepdims=True) + jnp.sum(
        q_ref[half:].astype(F32) * w1, axis=0, keepdims=True
    )
    pre[...] += jnp.where(lax.broadcasted_iota(jnp.int32, pre.shape, 0) == step, row, 0.0)
    lane = lax.broadcasted_iota(jnp.int32, (1, 128), 1)
    posts = jnp.zeros((1, 128), F32)
    for g in range(HEADS):
        at = slice(g * HEAD_DIM, (g + 1) * HEAD_DIM)
        b = pos[step, g]
        u0g, u1g = u0[at], u1[at]
        dvt[at, :half] += b * u0g
        dvt[at, half:] += b * u1g
        both = u0g * vt[at, :half].astype(F32) + u1g * vt[at, half:].astype(F32)
        post = jnp.sum(jnp.sum(both, axis=0, keepdims=True), axis=1, keepdims=True)
        posts += jnp.where(lane == 16 + g, post, 0.0)
    mix_ref[...] += jnp.where(
        lax.broadcasted_iota(jnp.int32, mix_ref.shape, 0) == step, posts, 0.0
    )
    qs = jnp.concatenate(
        [
            (qt[g * HEAD_DIM : (g + 1) * HEAD_DIM].astype(F32) * pms[step, g]).astype(BF16)
            for g in range(HEADS)
        ],
        axis=0,
    )
    dkt[:, :half] += dot(qs[:, :half], d0) + dot(qs[:, half:], d1)
    dkt[:, half:] += dot(qs[:, half:], d2)

    @pl.when(step == HEADS - 1)
    def _():
        feature = lax.broadcasted_iota(jnp.int32, (width, 128), 0)
        head = lax.broadcasted_iota(jnp.int32, (width, 128), 1)
        member = (feature >= head * HEAD_DIM) & (feature < (head + 1) * HEAD_DIM)
        turned = lax.dot_general(
            member.astype(F32),
            pre[...],
            (((0,), (1,)), ((), ())),
            precision=lax.Precision.HIGHEST,
            preferred_element_type=F32,
        )
        mix_ref[:, :16] += turned[:16]
        dq_ref[...] = dq[...].astype(BF16)
        dk_ref[...] = dkt[...].astype(BF16).T
        dv_ref[...] = dvt[...].astype(BF16).T
        made = []
        for n, ref in enumerate((dq_ref, dk_ref, dv_ref)):
            slots[n] = dot(nt_ref[...], ref[...]).astype(BF16)
            if blocked:
                part = width // 2
                for c in range(2):
                    made += send_copies(
                        spot,
                        slots.at[n, :, pl.ds(c * part, part)],
                        grads[0],
                        grads[1],
                        n * (width // 16),
                        c,
                        0,
                        part,
                        sems.at[2 * n + c],
                        True,
                    )
            else:
                made.append(pltpu.make_async_copy(slots.at[n], grads[n], sems.at[n, 0]))
            for copy in made[-32 if blocked else -1 :]:
                copy.start()
        for copy in made:
            copy.wait()


def attend_back(spot, blocked, nt, q, k, v, g, p, pm, po, pms, pos):
    seq, width = q.shape
    half = seq // 2
    whole = pl.BlockSpec((seq, width), lambda h: (0, 0))
    row = pl.BlockSpec((1, 1, width), lambda h: (h, 0, 0))
    low = jax.ShapeDtypeStruct((seq, width), BF16)
    if blocked:
        grads = [jax.ShapeDtypeStruct((4, 4, 3 * (width // 16), width // 2), BF16)] * 2
    else:
        grads = [jax.ShapeDtypeStruct((width, width), BF16)] * 3
    return pl.pallas_call(
        functools.partial(attend_back_kernel, blocked),
        grid=(HEADS,),
        in_specs=[SMEM, SMEM, SMEM, pl.BlockSpec((width, seq), lambda h: (0, 0))]
        + [whole] * 4
        + [pl.BlockSpec((1, half, 3 * half), lambda h: (h, 0, 0)), row, row],
        out_specs=[whole] * 3
        + [pl.BlockSpec((16, 128), lambda h: (0, 0))]
        + [ANY] * len(grads),
        out_shape=[low] * 3
        + [jax.ShapeDtypeStruct((16, 128), F32)]
        + grads,
        scratch_shapes=[pltpu.VMEM((width, seq), BF16)] * 3
        + [
            pltpu.VMEM((seq, width), F32),
            pltpu.VMEM((width, seq), F32),
            pltpu.VMEM((width, seq), F32),
            pltpu.VMEM((16, width), F32),
            pltpu.VMEM((3, width, width), BF16),
            pltpu.SemaphoreType.DMA((6, 16)),
        ],
        compiler_params=PARAMS,
        name="attend_back",
        cost_estimate=cost(28),
    )(spot, pms, pos, nt, q, k, v, g, p, pm, po)


def input_kernel(blocks, spot, *rest):
    pieces, rest = rest[:blocks], rest[blocks:]
    dq_ref, dk_ref, dv_ref, states_ref, mid_ref, gain_ref, sums_ref, mix_ref = rest[:8]
    out_ref, small_ref, wq, wk, wv, sems = rest[8:]
    features = wq.shape[1]
    width = features // 2
    depth = wq.shape[0] // 16
    copies = place_copies(
        spot, pieces, (wq, wk, wv), (0, depth, 2 * depth), (0, 0, 0), (width,) * 3, sems, True
    )
    for copy in copies:
        copy.start()
    states = states_ref[...]
    scale = lax.rsqrt(jnp.mean(states * states, axis=1, keepdims=True) + EPSILON)
    for copy in copies:
        copy.wait()
    grad = (
        dot_nt(dq_ref[...], wq[...]) + dot_nt(dk_ref[...], wk[...]) + dot_nt(dv_ref[...], wv[...])
    )
    first = jnp.sum(grad * states * scale, axis=0, keepdims=True)
    parts = features // 128
    lane = lax.broadcasted_iota(jnp.int32, (1, 128), 1)
    losses = [jnp.sum(sums_ref[n : n + 1], axis=1, keepdims=True) for n in (1, 2)]
    for n in range(parts):
        at = slice(n * 128, (n + 1) * 128)
        small_ref[n : n + 1] = first[:, at]
        small_ref[parts + n : parts + n + 1] = sums_ref[:1, at]
    small_ref[2 * parts :] = mix_ref[:HEADS]
    small_ref[2 * parts : 2 * parts + 1] += jnp.where(
        lane == 32, losses[0], jnp.where(lane == 33, losses[1], 0.0)
    )
    term = gain_ref[...] * grad
    inner = jnp.mean(term * states, axis=1, keepdims=True)
    out_ref[...] = mid_ref[...] + scale * term - states * (scale * scale * scale) * inner


def input_block(spot, pieces, dq, dk, dv, states, mid_grad, gain, sums, mix):
    seq, width = dq.shape
    return pl.pallas_call(
        functools.partial(input_kernel, len(pieces)),
        in_specs=[SMEM] + [ANY] * len(pieces) + [VMEM] * 8,
        out_specs=[VMEM] * 2,
        out_shape=[
            jax.ShapeDtypeStruct((seq, width), F32),
            jax.ShapeDtypeStruct((2 * width // 128 + HEADS, 128), F32),
        ],
        scratch_shapes=[pltpu.VMEM((width, width), BF16)] * 3 + [pltpu.SemaphoreType.DMA((96,))],
        compiler_params=PARAMS,
        name="input_grad",
        cost_estimate=cost(9),
    )(spot, *pieces, dq, dk, dv, states, mid_grad, gain, sums, mix)


def exchange(value, mask, total):
    return lax.ppermute(value, AXES, [(i, i ^ mask) for i in range(total)])


def after(value, *others):
    return lax.optimization_barrier((value, *others))[0]


def over_lines(blocks):
    return lax.all_to_all(blocks, "row", 0, 0, axis_index_groups=LINES, tiled=True)


def gather_line(packet):
    return over_lines(jnp.broadcast_to(packet, (4, *packet.shape)))


def gather_near(packet, total):
    return jnp.stack([packet, *[exchange(packet, m * Z_BIT, total) for m in (1, 2, 3)]])


def gather_sides(line, total):
    return exchange(line, X_BIT, total), exchange(line, Y_BIT, total)


def gather_halves(over_x, over_y, total):
    return exchange(over_x, Y_BIT, total), exchange(over_y, X_BIT, total)


def add_low(*terms):
    return functools.reduce(jnp.add, [t.astype(F32) for t in terms])


def reduce_core(keep, other):
    mine = add_low(keep, other).astype(BF16)
    return mine, mine[2:, :2], mine[1::2, 2:]


def reduce_first(over_y, over_x, total):
    return exchange(over_y, Y_BIT, total), exchange(over_x, X_BIT, total)


def reduce_sides(mine, over_y, over_x):
    return add_low(mine[1, :2], over_y[1]).astype(BF16), add_low(mine[2, 2:], over_x[1]).astype(BF16)


def reduce_second(side_x, side_y, total):
    return exchange(side_x, X_BIT, total), exchange(side_y, Y_BIT, total)


def reduce_own(mine, over_y, over_x):
    return add_low(mine[0, :2], over_y[0]), add_low(mine[0, 2:], over_x[0])


def reduce_line(head, tail, side_x, side_y):
    return jnp.concatenate([add_low(head, side_x), add_low(tail, side_y)])


def reduce_far(line, total):
    return [exchange(line[m].astype(BF16), m * Z_BIT, total) for m in (1, 2, 3)]


def gather_whole(block):
    rows, cols = lax.axis_size("row"), lax.axis_size("col")
    depth, width = block.shape
    every = lax.all_gather(block[None], AXES, axis=0, tiled=True)
    every = every.reshape(rows, cols, depth, width).transpose(0, 2, 1, 3)
    return every.reshape(rows * depth, cols * width)


def scatter_whole(grad):
    rows, cols = lax.axis_size("row"), lax.axis_size("col")
    depth, width = grad.shape[0] // rows, grad.shape[1] // cols
    parts = grad.reshape(rows, depth, cols, width).transpose(0, 2, 1, 3)
    parts = parts.reshape(rows * cols, depth, width).astype(F32)
    return lax.psum_scatter(parts, AXES, scatter_dimension=0, tiled=True)[0]


def shards(
    states,
    upstream,
    teacher,
    validity,
    picture_start,
    first_gain,
    query_weight,
    key_weight,
    value_weight,
    premix,
    postmix,
    output_weight,
    second_gain,
    up_weight,
    down_weight,
):
    row_total = lax.axis_size("row")
    col_total = lax.axis_size("col")
    total = row_total * col_total
    seq_len, features = states.shape
    depth, width = query_weight.shape
    units = up_weight.shape[1] * col_total
    blocked = (row_total, col_total) == (16, 2)
    row = lax.axis_index("row")
    spot = jnp.stack([row // 4, (row // 2) % 2, row % 2, lax.axis_index("col")]).astype(jnp.int32)
    down_turned = down_weight.T
    if blocked:
        packet = jnp.concatenate([query_weight, key_weight, value_weight], axis=0)
        qkv_line = gather_near(packet, total)
        qkv_sides = gather_sides(qkv_line, total)
        marks = jnp.sum(validity.reshape(-1, EXTRA), axis=0).astype(BF16)
        marks = jnp.broadcast_to(marks, (depth, EXTRA))
        packet = jnp.concatenate(
            [up_weight, output_weight, marks, down_turned], axis=1
        )
        line = gather_line(packet)
        *halves, qkv_line, side_x, side_y = lax.optimization_barrier(
            (qkv_sides[0][:2], qkv_sides[1][2:], qkv_line, *qkv_sides)
        )
        qkv_halves = jnp.stack(gather_halves(*halves, total))
        qkv_lines = jnp.stack([qkv_line, side_x, side_y])
        qkv = [qkv_lines, qkv_halves]
        qkv += [exchange(part, CORE_BIT, total) for part in qkv]
        line, *qkv = lax.optimization_barrier((line, *qkv))
        sides = gather_sides(line, total)
        total_valid = jnp.zeros((), F32)
    else:
        qkv = [gather_whole(w) for w in (query_weight, key_weight, value_weight)]
        rest = [gather_whole(w) for w in (output_weight, up_weight, down_turned)]
        total_valid = lax.psum(jnp.sum(validity).astype(F32), AXES)
    first_scale = lax.rsqrt(jnp.mean(states * states, axis=-1, keepdims=True) + EPSILON)
    normed = (states * first_scale * first_gain).astype(BF16)
    pms = premix.T * (HEAD_DIM**-0.5)
    pos = postmix
    pm = jnp.repeat(pms, HEAD_DIM, axis=1)[:, None]
    po = jnp.repeat(pos, HEAD_DIM, axis=1)[:, None]
    queries, keys, values, attended, probs = attend(spot, picture_start, normed, qkv, pm, po)
    if blocked:
        *sides, attended = lax.optimization_barrier((*sides, attended))
        *halves, line, side_x, side_y = lax.optimization_barrier(
            (sides[0][:2], sides[1][2:], line, *sides)
        )
        rest = [jnp.stack([line, side_x, side_y]), jnp.stack(gather_halves(*halves, total))]
        rest += [exchange(part, CORE_BIT, total) for part in rest]
    layer_out, mid_grad, attended_grad, sums, *grads = middle_block(
        blocked,
        spot,
        total_valid.reshape(1, 1),
        seq_len * total,
        rest,
        attended,
        states,
        upstream,
        teacher,
        validity[:, None],
        second_gain[None],
        units,
    )
    total_valid = sums[3, 0]
    nt = normed.T
    if blocked:
        ffn_mine, *first, attended_grad = lax.optimization_barrier(
            (*reduce_core(grads[0], exchange(grads[1], CORE_BIT, total)), attended_grad)
        )
        ffn_first = reduce_first(*first, total)
    else:
        up_grad, down_grad, output_grad = (scatter_whole(g) for g in grads)
        down_grad = down_grad.T
    dq, dk, dv, mix, *grads = attend_back(
        spot, blocked, nt, queries, keys, values, attended_grad, probs, pm, po, pms, pos
    )
    if blocked:
        *ffn_first, dq, dk, dv, mix, keep, send = lax.optimization_barrier(
            (*ffn_first, dq, dk, dv, mix, *grads)
        )
        other = exchange(send, CORE_BIT, total)
        ffn_sides = reduce_second(*reduce_sides(ffn_mine, *ffn_first), total)
        mine, *first, dq, dk, dv = lax.optimization_barrier((*reduce_core(keep, other), dq, dk, dv))
        first = reduce_first(*first, total)
        input_grad, small = input_block(
            spot, qkv, dq, dk, dv, states, mid_grad, first_gain[None], sums, mix
        )
        *ffn_sides, small = lax.optimization_barrier((*ffn_sides, small))
        ffn_line = reduce_line(*reduce_own(ffn_mine, *ffn_first), *ffn_sides)
        small += exchange(small, CORE_BIT, total)
        near = lax.reduce_precision(small, 8, 7)
        small = jnp.broadcast_to(jnp.concatenate([near, small - near]), (4, depth, 128))
        ffn_line = jnp.concatenate([ffn_line, small], axis=2)
        blocks = [ffn_line[m].astype(BF16) for m in (1, 2, 3)]
        ffn_far = [exchange(block, m * Z_BIT, total) for m, block in enumerate(blocks, 1)]
        *first, _, _, _ = lax.optimization_barrier((*first, *blocks))
        sides = reduce_second(*reduce_sides(mine, *first), total)
        line = reduce_line(*reduce_own(mine, *first), *sides)
        ffn_far = [after(far, line) for far in ffn_far]
        ffn = with_layout_constraint(add_low(ffn_line[0], *ffn_far), Layout((0, 1)))
        attn = add_low(line[0], *reduce_far(line, total))
        half = units // col_total
        up_grad, output_grad, down_grad, small = jnp.split(
            ffn, [half, half + width, 2 * half + width], axis=1
        )
        small = small[: depth // 2] + small[depth // 2 :]
        for bit in (X_BIT, Y_BIT):
            small += exchange(small, bit, total)
        down_grad = down_grad.T
        query_grad, key_grad, value_grad = (attn[n * depth : (n + 1) * depth] for n in range(3))
    else:
        query_grad, key_grad, value_grad = (scatter_whole(g) for g in grads)
        input_grad, small = input_block(
            spot, qkv, dq, dk, dv, states, mid_grad, first_gain[None], sums, mix
        )
        small = lax.psum(small, AXES)
    parts = features // 128
    first_grad = small[:parts].reshape(-1)
    second_grad = small[parts : 2 * parts].reshape(-1)
    small = small[2 * parts :]
    premix_grad = small[:, :HEADS] * (HEAD_DIM**-0.5)
    postmix_grad = small[:, 16 : 16 + HEADS]
    losses = small[0, 32:34]
    return (
        layer_out,
        losses[0] / (total_valid * features),
        losses[1] / total_valid,
        input_grad,
        first_grad,
        query_grad,
        key_grad,
        value_grad,
        premix_grad,
        postmix_grad,
        output_grad,
        second_grad,
        up_grad,
        down_grad,
    )


def solution(mesh):
    tokens, block = P(AXES, None), P("row", "col")
    return jax.shard_map(
        shards,
        mesh=mesh,
        in_specs=(
            tokens, tokens, tokens, P(AXES), tokens, P(), block, block, block, P(), P(), block,
            P(), block, P("col", "row"),
        ),
        out_specs=(
            tokens, P(), P(), tokens, P(), block, block, block, P(), P(), block, P(), block,
            P("col", "row"),
        ),
        check_vma=False,
    )
```

```python
import functools

import jax
import jax.numpy as jnp
from jax import lax
from jax.experimental import pallas as pl
from jax.experimental.layout import Layout, with_layout_constraint
from jax.experimental.pallas import tpu as pltpu
from jax.sharding import PartitionSpec as P

HEADS = 12
HEAD_DIM = 64
PIC = 256
EPSILON = 1e-06
F32 = jnp.float32
BF16 = jnp.bfloat16
AXES = ("row", "col")
X_BIT, CORE_BIT, Y_BIT, Z_BIT = 1, 2, 4, 8
LINES = [[at + Z_BIT // 2 * z for z in range(4)] for at in range(4)]
EXTRA = 128
PIECES = ((0, 0, 0), (0, 1, 0), (1, 0, 0), (1, 1, 0), (1, 1, 2))
PARAMS = pltpu.CompilerParams(vmem_limit_bytes=60000 * 1024)
SMEM = pl.BlockSpec(memory_space=pltpu.SMEM)
ANY = pl.BlockSpec(memory_space=pl.ANY)
VMEM = pl.BlockSpec(memory_space=pltpu.VMEM)


def dot(a, b):
    return lax.dot_general(a, b, (((1,), (0,)), ((), ())), preferred_element_type=F32)


def dot_nt(a, b):
    return lax.dot_general(a, b, (((1,), (1,)), ((), ())), preferred_element_type=F32)


def cost(micros):
    return pl.CostEstimate(flops=micros * 10**9, bytes_accessed=10**6, transcendentals=0)


def placed(pieces):
    for n, piece in enumerate(pieces):
        y, x, first = PIECES[n % len(PIECES)]
        for z in range(piece.shape[0]):
            yield piece, (z,), n // len(PIECES), y, x, first + z


def place_copies(spot, pieces, wholes, rows_at, cols_at, widths, sems, near=False):
    if len(pieces) == len(wholes):
        return [
            pltpu.make_async_copy(piece, whole, sems.at[n])
            for n, (piece, whole) in enumerate(zip(pieces, wholes))
        ]
    copies = []
    for piece, index, core, y, x, z in placed(pieces):
        r = ((spot[0] ^ z if near else z) * 2 + (spot[1] ^ y)) * 2 + (spot[2] ^ core)
        c = spot[3] ^ x
        for whole, row, col, width in zip(wholes, rows_at, cols_at, widths):
            depth = whole.shape[0] // 16
            copies.append(
                pltpu.make_async_copy(
                    piece.at[(*index, pl.ds(row, depth), pl.ds(col, width))],
                    whole.at[
                        pl.ds(pl.multiple_of(r * depth, 16), depth),
                        pl.ds(pl.multiple_of(c * width, 128), width),
                    ],
                    sems.at[len(copies)],
                )
            )
    return copies


def send_copies(spot, source, keep, send, row, half, col, width, sems, near=False):
    depth = source.shape[0] // 16
    copies = []
    for j in range(8):
        z, y = j // 2, j % 2
        plane = (spot[1] ^ y) * 2 + (spot[3] ^ half)
        for n, (target, core) in enumerate(((keep, spot[2]), (send, 1 - spot[2]))):
            start = pl.multiple_of((2 * j + core) * depth, 16)
            copies.append(
                pltpu.make_async_copy(
                    source.at[pl.ds(start, depth), pl.ds(0, width)],
                    target.at[plane, spot[0] ^ z if near else z, pl.ds(row, depth), pl.ds(col, width)],
                    sems.at[2 * j + n],
                )
            )
    return copies


def attend_kernel(blocks, spot, starts, normed_ref, *rest):
    pieces, rest = rest[:blocks], rest[blocks:]
    pm_ref, po_ref, q_ref, k_ref, v_ref, out_ref, p_ref, wq, wk, wv, kt, bias, acc, sems = rest
    step = pl.program_id(0)
    half = normed_ref.shape[0] // 2

    @pl.when(step == 0)
    def _():
        width = wq.shape[1] // 2
        depth = wq.shape[0] // 16
        copies = place_copies(
            spot, pieces, (wq, wk, wv), (0, depth, 2 * depth), (0, 0, 0), (width,) * 3, sems, True
        )
        for copy in copies:
            copy.start()
        rows = lax.broadcasted_iota(jnp.int32, (half, half), 0)
        cols = lax.broadcasted_iota(jnp.int32, (half, half), 1)
        for b in range(2):
            i, j = rows + b * half, cols + b * half
            ok = j <= i
            for s in range(2):
                p = starts[0, s]
                ok = ok | ((i >= p) & (i < p + PIC) & (j >= p) & (j < p + PIC))
            bias[b] = jnp.where(ok, 0.0, -1e30)
        acc[...] = jnp.zeros_like(acc)
        for copy in copies:
            copy.wait()
        k_ref[...] = dot(normed_ref[...], wk[...]).astype(BF16)
        kt[...] = k_ref[...].T
        q_ref[...] = dot(normed_ref[...], wq[...]).astype(BF16)
        v_ref[...] = dot(normed_ref[...], wv[...]).astype(BF16)

    pm = pm_ref[0]
    po = po_ref[0]
    vs = (v_ref[...].astype(F32) * po).astype(BF16)
    top = (q_ref[:half].astype(F32) * pm).astype(BF16)
    low = (q_ref[half:].astype(F32) * pm).astype(BF16)
    s0 = dot(top, kt[:, :half]) + bias[0]
    s1 = dot(low, kt[:, :half])
    s2 = dot(low, kt[:, half:]) + bias[1]
    m0 = jnp.max(s0, axis=1, keepdims=True)
    e0 = jnp.exp(s0 - m0)
    p0 = (e0 / jnp.sum(e0, axis=1, keepdims=True)).astype(BF16)
    m1 = jnp.maximum(jnp.max(s1, axis=1, keepdims=True), jnp.max(s2, axis=1, keepdims=True))
    e1 = jnp.exp(s1 - m1)
    e2 = jnp.exp(s2 - m1)
    inv = 1.0 / (jnp.sum(e1, axis=1, keepdims=True) + jnp.sum(e2, axis=1, keepdims=True))
    p1 = (e1 * inv).astype(BF16)
    p2 = (e2 * inv).astype(BF16)
    p_ref[0, :, :half] = p0
    p_ref[0, :, half : 2 * half] = p1
    p_ref[0, :, 2 * half :] = p2
    acc[:half] += dot(p0, vs[:half])
    acc[half:] += dot(p1, vs[:half]) + dot(p2, vs[half:])

    @pl.when(step == HEADS - 1)
    def _():
        out_ref[...] = acc[...].astype(BF16)


def attend(spot, starts, normed, pieces, pm, po):
    seq, width = normed.shape
    half = seq // 2
    whole = pl.BlockSpec((seq, width), lambda h: (0, 0))
    row = pl.BlockSpec((1, 1, width), lambda h: (h, 0, 0))
    low = jax.ShapeDtypeStruct((seq, width), BF16)
    return pl.pallas_call(
        functools.partial(attend_kernel, len(pieces)),
        grid=(HEADS,),
        in_specs=[SMEM, SMEM, whole] + [ANY] * len(pieces) + [row, row],
        out_specs=[whole] * 4 + [pl.BlockSpec((1, half, 3 * half), lambda h: (h, 0, 0))],
        out_shape=[low] * 4 + [jax.ShapeDtypeStruct((HEADS, half, 3 * half), BF16)],
        scratch_shapes=[pltpu.VMEM((width, width), BF16)] * 3
        + [
            pltpu.VMEM((width, seq), BF16),
            pltpu.VMEM((2, half, half), F32),
            pltpu.VMEM((seq, width), F32),
            pltpu.SemaphoreType.DMA((96,)),
        ],
        compiler_params=PARAMS,
        name="attend",
        cost_estimate=cost(20),
    )(spot, starts, normed, *pieces, pm, po)


def middle_kernel(blocks, outs, tokens, spot, count, *rest):
    pieces, rest = rest[:blocks], rest[blocks:]
    att_ref, states_ref, up_ref, teach_ref, valid_ref, gain_ref = rest[:6]
    layer_ref, mid_ref, agrad_ref, sums_ref = rest[6:10]
    grads, rest = rest[10 : 10 + outs], rest[10 + outs :]
    wo, wu, wd, hidden, pre, n2t, olt, slots, marks, sems, out_sems, mark_sems = rest
    seq, width = att_ref.shape
    units = wu.shape[1]
    blocked = outs == 2
    mark_copies = []
    if blocked:
        for n, (piece, index, *_) in enumerate(placed(pieces)):
            mark_copies.append(
                pltpu.make_async_copy(
                    piece.at[(*index, pl.ds(0, 16), pl.ds((units + width) // 2, EXTRA))],
                    marks.at[n],
                    mark_sems.at[n],
                )
            )
    copies = place_copies(
        spot,
        pieces,
        (wo, wu, wd),
        (0, 0, 0),
        (units // 2, 0, (units + width) // 2 + EXTRA),
        (width // 2, units // 2, units // 2),
        sems,
    )
    for copy in mark_copies + copies[::3] + copies[1::3] + copies[2::3]:
        copy.start()
    for copy in mark_copies:
        copy.wait()
    total_valid = jnp.full((1, 1), count[0, 0], F32)
    if blocked:
        by_lane = jnp.sum(marks[...].astype(F32), axis=0)[:1]
        total_valid += jnp.sum(by_lane, axis=1, keepdims=True)
    factor = tokens / total_valid
    sums_ref[...] = jnp.broadcast_to(total_valid, sums_ref.shape)
    for copy in copies[::3]:
        copy.wait()
    mid_ref[...] = states_ref[...] + dot(att_ref[...], wo[...])
    middle = mid_ref[...]
    scale = lax.rsqrt(jnp.mean(middle * middle, axis=1, keepdims=True) + EPSILON)
    n2 = (middle * scale * gain_ref[...]).astype(BF16)
    n2t[...] = n2.T
    for copy in copies[1::3]:
        copy.wait()

    chunk = 512
    steps = units // chunk

    def up_step(j, _):
        at = pl.ds(pl.multiple_of(j * chunk, chunk), chunk)
        hidden[:, at] = jnp.maximum(dot(n2, wu[:, at]), 0.0).astype(BF16)
        return 0

    lax.fori_loop(0, steps, up_step, 0)
    for copy in copies[2::3]:
        copy.wait()
    layer_ref[...] = mid_ref[...] + dot_nt(hidden[...], wd[...])
    layer = layer_ref[...]
    valid = valid_ref[...].astype(F32)
    upstream = up_ref[...]
    differ = layer - teach_ref[...]
    sums_ref[1:2, :] = jnp.sum(valid * (differ * differ), axis=0, keepdims=True)
    sums_ref[2:3, :] = jnp.sum(valid * (upstream * layer), axis=0, keepdims=True)
    out_grad = (factor * valid) * (upstream + differ)
    out_low = out_grad.astype(BF16)
    olt[...] = out_low.T

    def down_step(j, _):
        at = pl.ds(pl.multiple_of(j * chunk, chunk), chunk)
        part = hidden[:, at]
        back = jnp.where(part > 0, dot(out_low, wd[:, at]), 0.0).astype(BF16)
        pre[:, at] = back
        for which, (left, right) in enumerate(((n2t, back), (olt, part))):
            slot = slots.at[which]

            @pl.when(j > 0)
            def _():
                for copy in grad_copies(which, j - 1):
                    copy.wait()

            slot[...] = dot(left[...], right).astype(BF16)
            for copy in grad_copies(which, j):
                copy.start()
        return 0

    def grad_copies(which, j):
        if not blocked:
            at = pl.ds(pl.multiple_of(j * chunk, chunk), chunk)
            return [pltpu.make_async_copy(slots.at[which], grads[which].at[:, at], out_sems.at[which, 0])]
        per = steps // 2
        return send_copies(
            spot,
            slots.at[which],
            grads[0],
            grads[1],
            0,
            j // per,
            pl.multiple_of(which * ((units + width) // 2) + (j % per) * chunk, 128),
            chunk,
            out_sems.at[which],
            True,
        )

    lax.fori_loop(0, steps, down_step, 0)
    grad = dot_nt(pre[...], wu[...])
    middle = mid_ref[...]
    scale = lax.rsqrt(jnp.mean(middle * middle, axis=1, keepdims=True) + EPSILON)
    sums_ref[0:1, :] = jnp.sum(grad * middle * scale, axis=0, keepdims=True)
    term = gain_ref[...] * grad
    inner = jnp.mean(term * middle, axis=1, keepdims=True)
    layer = layer_ref[...]
    out_grad = (factor * valid_ref[...].astype(F32)) * (
        up_ref[...] + (layer - teach_ref[...])
    )
    mid_grad = out_grad + scale * term - middle * (scale * scale * scale) * inner
    mid_ref[...] = mid_grad
    branch = mid_grad.astype(BF16)
    agrad_ref[...] = dot_nt(branch, wo[...]).astype(BF16)
    n2t[...] = att_ref[...].T
    for which in range(2):
        for copy in grad_copies(which, steps - 1):
            copy.wait()
    half = width // 2
    last = []
    for c in range(2):
        slots[c, :, :half] = dot(n2t[...], branch[:, c * half : (c + 1) * half]).astype(BF16)
        if blocked:
            made = send_copies(
                spot, slots.at[c], grads[0], grads[1], 0, c, units // 2, half, out_sems.at[c], True
            )
        else:
            made = [
                pltpu.make_async_copy(
                    slots.at[c, :, pl.ds(0, half)],
                    grads[2].at[:, pl.ds(c * half, half)],
                    out_sems.at[c, 0],
                )
            ]
        for copy in made:
            copy.start()
        last += made
    for copy in last:
        copy.wait()


def middle_block(blocked, spot, count, tokens, pieces, attended, states, upstream, teacher, valid, gain, units):
    seq, width = attended.shape
    full = jax.ShapeDtypeStruct((seq, width), F32)
    if blocked:
        depth = width // 16
        grads = [jax.ShapeDtypeStruct((4, 4, depth, units + width // 2), BF16)] * 2
    else:
        grads = [
            jax.ShapeDtypeStruct((width, units), BF16),
            jax.ShapeDtypeStruct((width, units), BF16),
            jax.ShapeDtypeStruct((width, width), BF16),
        ]
    return pl.pallas_call(
        functools.partial(middle_kernel, len(pieces), len(grads), tokens),
        in_specs=[SMEM, SMEM] + [ANY] * len(pieces) + [VMEM] * 6,
        out_specs=[VMEM] * 4 + [ANY] * len(grads),
        out_shape=[
            full,
            full,
            jax.ShapeDtypeStruct((seq, width), BF16),
            jax.ShapeDtypeStruct((8, width), F32),
        ]
        + grads,
        scratch_shapes=[
            pltpu.VMEM((width, width), BF16),
            pltpu.VMEM((width, units), BF16),
            pltpu.VMEM((width, units), BF16),
            pltpu.VMEM((seq, units), BF16),
            pltpu.VMEM((seq, units), BF16),
            pltpu.VMEM((width, seq), BF16),
            pltpu.VMEM((width, seq), BF16),
            pltpu.VMEM((2, width, 512), BF16),
            pltpu.VMEM((32, 16, EXTRA), BF16),
            pltpu.SemaphoreType.DMA((96,)),
            pltpu.SemaphoreType.DMA((2, 16)),
            pltpu.SemaphoreType.DMA((32,)),
        ],
        compiler_params=PARAMS,
        name="middle",
        cost_estimate=cost(35),
    )(spot, count, *pieces, attended, states, upstream, teacher, valid, gain)


def attend_back_kernel(
    blocked, spot, pms, pos, nt_ref, q_ref, k_ref, v_ref, g_ref, p_ref, pm_ref, po_ref,
    dq_ref, dk_ref, dv_ref, mix_ref, *rest,
):
    outs = 2 if blocked else 3
    grads = rest[:outs]
    vt, qt, gt, dq, dkt, dvt, pre, slots, sems = rest[outs:]
    step = pl.program_id(0)
    seq, width = q_ref.shape
    half = seq // 2

    @pl.when(step == 0)
    def _():
        vt[...] = v_ref[...].T
        qt[...] = q_ref[...].T
        gt[...] = g_ref[...].T
        dq[...] = jnp.zeros_like(dq)
        dkt[...] = jnp.zeros_like(dkt)
        dvt[...] = jnp.zeros_like(dvt)
        pre[...] = jnp.zeros_like(pre)
        mix_ref[...] = jnp.zeros_like(mix_ref)

    pm = pm_ref[0]
    po = po_ref[0]
    p0, p1, p2 = (p_ref[0, :, b * half : (b + 1) * half] for b in range(3))
    top = (g_ref[:half].astype(F32) * po).astype(BF16)
    low = (g_ref[half:].astype(F32) * po).astype(BF16)
    g0 = dot(top, vt[:, :half])
    g1 = dot(low, vt[:, :half])
    g2 = dot(low, vt[:, half:])
    u0 = dot(gt[:, :half], p0) + dot(gt[:, half:], p1)
    u1 = dot(gt[:, half:], p2)
    f0, f1, f2 = p0.astype(F32), p1.astype(F32), p2.astype(F32)
    t0 = f0 * g0
    d0 = (t0 - f0 * jnp.sum(t0, axis=1, keepdims=True)).astype(BF16)
    t1, t2 = f1 * g1, f2 * g2
    r1 = jnp.sum(t1, axis=1, keepdims=True) + jnp.sum(t2, axis=1, keepdims=True)
    d1 = (t1 - f1 * r1).astype(BF16)
    d2 = (t2 - f2 * r1).astype(BF16)
    w0 = dot(d0, k_ref[:half])
    w1 = dot(d1, k_ref[:half]) + dot(d2, k_ref[half:])
    dq[:half] += pm * w0
    dq[half:] += pm * w1
    row = jnp.sum(q_ref[:half].astype(F32) * w0, axis=0, keepdims=True) + jnp.sum(
        q_ref[half:].astype(F32) * w1, axis=0, keepdims=True
    )
    pre[...] += jnp.where(lax.broadcasted_iota(jnp.int32, pre.shape, 0) == step, row, 0.0)
    lane = lax.broadcasted_iota(jnp.int32, (1, 128), 1)
    posts = jnp.zeros((1, 128), F32)
    for g in range(HEADS):
        at = slice(g * HEAD_DIM, (g + 1) * HEAD_DIM)
        b = pos[step, g]
        u0g, u1g = u0[at], u1[at]
        dvt[at, :half] += b * u0g
        dvt[at, half:] += b * u1g
        both = u0g * vt[at, :half].astype(F32) + u1g * vt[at, half:].astype(F32)
        post = jnp.sum(jnp.sum(both, axis=0, keepdims=True), axis=1, keepdims=True)
        posts += jnp.where(lane == 16 + g, post, 0.0)
    mix_ref[...] += jnp.where(
        lax.broadcasted_iota(jnp.int32, mix_ref.shape, 0) == step, posts, 0.0
    )
    qs = jnp.concatenate(
        [
            (qt[g * HEAD_DIM : (g + 1) * HEAD_DIM].astype(F32) * pms[step, g]).astype(BF16)
            for g in range(HEADS)
        ],
        axis=0,
    )
    dkt[:, :half] += dot(qs[:, :half], d0) + dot(qs[:, half:], d1)
    dkt[:, half:] += dot(qs[:, half:], d2)

    @pl.when(step == HEADS - 1)
    def _():
        feature = lax.broadcasted_iota(jnp.int32, (width, 128), 0)
        head = lax.broadcasted_iota(jnp.int32, (width, 128), 1)
        member = (feature >= head * HEAD_DIM) & (feature < (head + 1) * HEAD_DIM)
        turned = lax.dot_general(
            member.astype(F32),
            pre[...],
            (((0,), (1,)), ((), ())),
            precision=lax.Precision.HIGHEST,
            preferred_element_type=F32,
        )
        mix_ref[:, :16] += turned[:16]
        dq_ref[...] = dq[...].astype(BF16)
        dk_ref[...] = dkt[...].astype(BF16).T
        dv_ref[...] = dvt[...].astype(BF16).T
        made = []
        for n, ref in enumerate((dq_ref, dk_ref, dv_ref)):
            slots[n] = dot(nt_ref[...], ref[...]).astype(BF16)
            if blocked:
                part = width // 2
                for c in range(2):
                    made += send_copies(
                        spot,
                        slots.at[n, :, pl.ds(c * part, part)],
                        grads[0],
                        grads[1],
                        n * (width // 16),
                        c,
                        0,
                        part,
                        sems.at[2 * n + c],
                        True,
                    )
            else:
                made.append(pltpu.make_async_copy(slots.at[n], grads[n], sems.at[n, 0]))
            for copy in made[-32 if blocked else -1 :]:
                copy.start()
        for copy in made:
            copy.wait()


def attend_back(spot, blocked, nt, q, k, v, g, p, pm, po, pms, pos):
    seq, width = q.shape
    half = seq // 2
    whole = pl.BlockSpec((seq, width), lambda h: (0, 0))
    row = pl.BlockSpec((1, 1, width), lambda h: (h, 0, 0))
    low = jax.ShapeDtypeStruct((seq, width), BF16)
    if blocked:
        grads = [jax.ShapeDtypeStruct((4, 4, 3 * (width // 16), width // 2), BF16)] * 2
    else:
        grads = [jax.ShapeDtypeStruct((width, width), BF16)] * 3
    return pl.pallas_call(
        functools.partial(attend_back_kernel, blocked),
        grid=(HEADS,),
        in_specs=[SMEM, SMEM, SMEM, pl.BlockSpec((width, seq), lambda h: (0, 0))]
        + [whole] * 4
        + [pl.BlockSpec((1, half, 3 * half), lambda h: (h, 0, 0)), row, row],
        out_specs=[whole] * 3
        + [pl.BlockSpec((16, 128), lambda h: (0, 0))]
        + [ANY] * len(grads),
        out_shape=[low] * 3
        + [jax.ShapeDtypeStruct((16, 128), F32)]
        + grads,
        scratch_shapes=[pltpu.VMEM((width, seq), BF16)] * 3
        + [
            pltpu.VMEM((seq, width), F32),
            pltpu.VMEM((width, seq), F32),
            pltpu.VMEM((width, seq), F32),
            pltpu.VMEM((16, width), F32),
            pltpu.VMEM((3, width, width), BF16),
            pltpu.SemaphoreType.DMA((6, 16)),
        ],
        compiler_params=PARAMS,
        name="attend_back",
        cost_estimate=cost(28),
    )(spot, pms, pos, nt, q, k, v, g, p, pm, po)


def input_kernel(blocks, spot, *rest):
    pieces, rest = rest[:blocks], rest[blocks:]
    dq_ref, dk_ref, dv_ref, states_ref, mid_ref, gain_ref, sums_ref, mix_ref = rest[:8]
    out_ref, small_ref, wq, wk, wv, sems = rest[8:]
    features = wq.shape[1]
    width = features // 2
    depth = wq.shape[0] // 16
    copies = place_copies(
        spot, pieces, (wq, wk, wv), (0, depth, 2 * depth), (0, 0, 0), (width,) * 3, sems, True
    )
    for copy in copies:
        copy.start()
    states = states_ref[...]
    scale = lax.rsqrt(jnp.mean(states * states, axis=1, keepdims=True) + EPSILON)
    for copy in copies:
        copy.wait()
    grad = (
        dot_nt(dq_ref[...], wq[...]) + dot_nt(dk_ref[...], wk[...]) + dot_nt(dv_ref[...], wv[...])
    )
    first = jnp.sum(grad * states * scale, axis=0, keepdims=True)
    parts = features // 128
    lane = lax.broadcasted_iota(jnp.int32, (1, 128), 1)
    losses = [jnp.sum(sums_ref[n : n + 1], axis=1, keepdims=True) for n in (1, 2)]
    for n in range(parts):
        at = slice(n * 128, (n + 1) * 128)
        small_ref[n : n + 1] = first[:, at]
        small_ref[parts + n : parts + n + 1] = sums_ref[:1, at]
    small_ref[2 * parts :] = mix_ref[:HEADS]
    small_ref[2 * parts : 2 * parts + 1] += jnp.where(
        lane == 32, losses[0], jnp.where(lane == 33, losses[1], 0.0)
    )
    term = gain_ref[...] * grad
    inner = jnp.mean(term * states, axis=1, keepdims=True)
    out_ref[...] = mid_ref[...] + scale * term - states * (scale * scale * scale) * inner


def input_block(spot, pieces, dq, dk, dv, states, mid_grad, gain, sums, mix):
    seq, width = dq.shape
    return pl.pallas_call(
        functools.partial(input_kernel, len(pieces)),
        in_specs=[SMEM] + [ANY] * len(pieces) + [VMEM] * 8,
        out_specs=[VMEM] * 2,
        out_shape=[
            jax.ShapeDtypeStruct((seq, width), F32),
            jax.ShapeDtypeStruct((2 * width // 128 + HEADS, 128), F32),
        ],
        scratch_shapes=[pltpu.VMEM((width, width), BF16)] * 3 + [pltpu.SemaphoreType.DMA((96,))],
        compiler_params=PARAMS,
        name="input_grad",
        cost_estimate=cost(9),
    )(spot, *pieces, dq, dk, dv, states, mid_grad, gain, sums, mix)


def exchange(value, mask, total):
    return lax.ppermute(value, AXES, [(i, i ^ mask) for i in range(total)])


def after(value, *others):
    return lax.optimization_barrier((value, *others))[0]


def over_lines(blocks):
    return lax.all_to_all(blocks, "row", 0, 0, axis_index_groups=LINES, tiled=True)


def late(value, rank):
    return 0.0 * value[(0,) * (value.ndim - rank)][(slice(1),) * rank].astype(F32)


def gather_line(packet):
    return over_lines(jnp.broadcast_to(packet, (4, *packet.shape)))


def gather_near(packet, total):
    return jnp.stack([packet, *[exchange(packet, m * Z_BIT, total) for m in (1, 2, 3)]])


def gather_sides(line, total):
    return exchange(line, X_BIT, total), exchange(line, Y_BIT, total)


def gather_halves(over_x, over_y, total):
    return exchange(over_x, Y_BIT, total), exchange(over_y, X_BIT, total)


def add_low(*terms):
    return functools.reduce(jnp.add, [t.astype(F32) for t in terms])


def reduce_core(keep, other):
    mine = add_low(keep, other).astype(BF16)
    return mine, mine[2:, :2], mine[1::2, 2:]


def reduce_first(over_y, over_x, total):
    return exchange(over_y, Y_BIT, total), exchange(over_x, X_BIT, total)


def reduce_sides(mine, over_y, over_x):
    return add_low(mine[1, :2], over_y[1]).astype(BF16), add_low(mine[2, 2:], over_x[1]).astype(BF16)


def reduce_second(side_x, side_y, total):
    return exchange(side_x, X_BIT, total), exchange(side_y, Y_BIT, total)


def reduce_own(mine, over_y, over_x):
    return add_low(mine[0, :2], over_y[0]), add_low(mine[0, 2:], over_x[0])


def reduce_line(head, tail, side_x, side_y):
    return jnp.concatenate([add_low(head, side_x), add_low(tail, side_y)])


def reduce_far(line, total):
    return [exchange(line[m].astype(BF16), m * Z_BIT, total) for m in (1, 2, 3)]


def gather_whole(block):
    rows, cols = lax.axis_size("row"), lax.axis_size("col")
    depth, width = block.shape
    every = lax.all_gather(block[None], AXES, axis=0, tiled=True)
    every = every.reshape(rows, cols, depth, width).transpose(0, 2, 1, 3)
    return every.reshape(rows * depth, cols * width)


def scatter_whole(grad):
    rows, cols = lax.axis_size("row"), lax.axis_size("col")
    depth, width = grad.shape[0] // rows, grad.shape[1] // cols
    parts = grad.reshape(rows, depth, cols, width).transpose(0, 2, 1, 3)
    parts = parts.reshape(rows * cols, depth, width).astype(F32)
    return lax.psum_scatter(parts, AXES, scatter_dimension=0, tiled=True)[0]


def shards(
    states,
    upstream,
    teacher,
    validity,
    picture_start,
    first_gain,
    query_weight,
    key_weight,
    value_weight,
    premix,
    postmix,
    output_weight,
    second_gain,
    up_weight,
    down_weight,
):
    row_total = lax.axis_size("row")
    col_total = lax.axis_size("col")
    total = row_total * col_total
    seq_len, features = states.shape
    depth, width = query_weight.shape
    units = up_weight.shape[1] * col_total
    blocked = (row_total, col_total) == (16, 2)
    row = lax.axis_index("row")
    spot = jnp.stack([row // 4, (row // 2) % 2, row % 2, lax.axis_index("col")]).astype(jnp.int32)
    down_turned = down_weight.T
    if blocked:
        packet = jnp.concatenate([query_weight, key_weight, value_weight], axis=0)
        qkv_line = gather_near(packet, total)
        qkv_sides = gather_sides(qkv_line, total)
        marks = jnp.sum(validity.reshape(-1, EXTRA), axis=0).astype(BF16)
        marks = jnp.broadcast_to(marks, (depth, EXTRA))
        packet = jnp.concatenate(
            [up_weight, output_weight, marks, down_turned], axis=1
        )
        line = gather_line(packet)
        *halves, qkv_line, side_x, side_y = lax.optimization_barrier(
            (qkv_sides[0][:2], qkv_sides[1][2:], qkv_line, *qkv_sides)
        )
        qkv = [qkv_line, side_x, side_y, *gather_halves(*halves, total)]
        qkv += [exchange(part, CORE_BIT, total) for part in qkv]
        line, *qkv = lax.optimization_barrier((line, *qkv))
        sides = gather_sides(line, total)
        total_valid = jnp.zeros((), F32)
    else:
        qkv = [gather_whole(w) for w in (query_weight, key_weight, value_weight)]
        rest = [gather_whole(w) for w in (output_weight, up_weight, down_turned)]
        total_valid = lax.psum(jnp.sum(validity).astype(F32), AXES)
    first_scale = lax.rsqrt(jnp.mean(states * states, axis=-1, keepdims=True) + EPSILON)
    normed = (states * first_scale * first_gain).astype(BF16)
    pms = premix.T * (HEAD_DIM**-0.5)
    pos = postmix
    pm = jnp.repeat(pms, HEAD_DIM, axis=1)[:, None]
    po = jnp.repeat(pos, HEAD_DIM, axis=1)[:, None]
    queries, keys, values, attended, probs = attend(spot, picture_start, normed, qkv, pm, po)
    if blocked:
        *sides, attended = lax.optimization_barrier((*sides, attended))
        *halves, line, side_x, side_y = lax.optimization_barrier(
            (sides[0][:2], sides[1][2:], line, *sides)
        )
        rest = [line, side_x, side_y, *gather_halves(*halves, total)]
        rest += [exchange(part, CORE_BIT, total) for part in rest]
    layer_out, mid_grad, attended_grad, sums, *grads = middle_block(
        blocked,
        spot,
        total_valid.reshape(1, 1),
        seq_len * total,
        rest,
        attended,
        states,
        upstream,
        teacher,
        validity[:, None],
        second_gain[None],
        units,
    )
    total_valid = sums[3, 0]
    nt = normed.T
    if blocked:
        ffn_mine, *first, attended_grad = lax.optimization_barrier(
            (*reduce_core(grads[0], exchange(grads[1], CORE_BIT, total)), attended_grad)
        )
        ffn_first = reduce_first(*first, total)
    else:
        up_grad, down_grad, output_grad = (scatter_whole(g) for g in grads)
        down_grad = down_grad.T
    dq, dk, dv, mix, *grads = attend_back(
        spot, blocked, nt, queries, keys, values, attended_grad, probs, pm, po, pms, pos
    )
    if blocked:
        *ffn_first, dq, dk, dv, mix, keep, send = lax.optimization_barrier(
            (*ffn_first, dq, dk, dv, mix, *grads)
        )
        other = exchange(send, CORE_BIT, total)
        ffn_sides = reduce_second(*reduce_sides(ffn_mine, *ffn_first), total)
        mine, *first, dq, dk, dv = lax.optimization_barrier((*reduce_core(keep, other), dq, dk, dv))
        first = reduce_first(*first, total)
        input_grad, small = input_block(
            spot, qkv, dq, dk, dv, states, mid_grad, first_gain[None], sums, mix
        )
        *ffn_sides, small = lax.optimization_barrier((*ffn_sides, small))
        ffn_line = reduce_line(*reduce_own(ffn_mine, *ffn_first), *ffn_sides)
        small += exchange(small, CORE_BIT, total)
        near = lax.reduce_precision(small, 8, 7)
        small = jnp.broadcast_to(jnp.concatenate([near, small - near]), (4, depth, 128))
        ffn_line = jnp.concatenate([ffn_line, small], axis=2)
        blocks = [ffn_line[m].astype(BF16) for m in (1, 2, 3)]
        ffn_far = [exchange(block, m * Z_BIT, total) for m, block in enumerate(blocks, 1)]
        *first, _, _, _ = lax.optimization_barrier((*first, *blocks))
        sides = reduce_sides(mine, *first)
        sides = reduce_second(*sides, total)
        ffn = add_low(ffn_line[0], *ffn_far) + late(sides[0], 2)
        ffn = with_layout_constraint(ffn, Layout((0, 1)))
        head, tail, ffn = lax.optimization_barrier((*reduce_own(mine, *first), ffn))
        line = reduce_line(head, tail, *sides)
        attn = add_low(line[0], *reduce_far(line, total))
        half = units // col_total
        up_grad, output_grad, down_grad, small = jnp.split(
            ffn, [half, half + width, 2 * half + width], axis=1
        )
        small = small[: depth // 2] + small[depth // 2 :] + late(line, 2)
        for bit in (X_BIT, Y_BIT):
            small += exchange(small, bit, total)
        down_grad = down_grad.T
        query_grad, key_grad, value_grad = (attn[n * depth : (n + 1) * depth] for n in range(3))
    else:
        query_grad, key_grad, value_grad = (scatter_whole(g) for g in grads)
        input_grad, small = input_block(
            spot, qkv, dq, dk, dv, states, mid_grad, first_gain[None], sums, mix
        )
        small = lax.psum(small, AXES)
    parts = features // 128
    first_grad = small[:parts].reshape(-1)
    second_grad = small[parts : 2 * parts].reshape(-1)
    small = small[2 * parts :]
    premix_grad = small[:, :HEADS] * (HEAD_DIM**-0.5)
    postmix_grad = small[:, 16 : 16 + HEADS]
    losses = small[0, 32:34]
    return (
        layer_out,
        losses[0] / (total_valid * features),
        losses[1] / total_valid,
        input_grad,
        first_grad,
        query_grad,
        key_grad,
        value_grad,
        premix_grad,
        postmix_grad,
        output_grad,
        second_grad,
        up_grad,
        down_grad,
    )


def solution(mesh):
    tokens, block = P(AXES, None), P("row", "col")
    return jax.shard_map(
        shards,
        mesh=mesh,
        in_specs=(
            tokens, tokens, tokens, P(AXES), tokens, P(), block, block, block, P(), P(), block,
            P(), block, P("col", "row"),
        ),
        out_specs=(
            tokens, P(), P(), tokens, P(), block, block, block, P(), P(), block, P(), block,
            P("col", "row"),
        ),
        check_vma=False,
    )
```

```python
import functools

import jax
import jax.numpy as jnp
from jax import lax
from jax.experimental import pallas as pl
from jax.experimental.layout import Layout, with_layout_constraint
from jax.experimental.pallas import tpu as pltpu
from jax.sharding import PartitionSpec as P

HEADS = 12
HEAD_DIM = 64
PIC = 256
EPSILON = 1e-06
F32 = jnp.float32
BF16 = jnp.bfloat16
AXES = ("row", "col")
X_BIT, CORE_BIT, Y_BIT, Z_BIT = 1, 2, 4, 8
LINES = [[at + Z_BIT // 2 * z for z in range(4)] for at in range(4)]
EXTRA = 128
PIECES = ((0, 0, 0), (0, 1, 0), (1, 0, 0), (1, 1, 0), (1, 1, 2))
PARAMS = pltpu.CompilerParams(vmem_limit_bytes=60000 * 1024)
SMEM = pl.BlockSpec(memory_space=pltpu.SMEM)
ANY = pl.BlockSpec(memory_space=pl.ANY)
VMEM = pl.BlockSpec(memory_space=pltpu.VMEM)


def dot(a, b):
    return lax.dot_general(a, b, (((1,), (0,)), ((), ())), preferred_element_type=F32)


def dot_nt(a, b):
    return lax.dot_general(a, b, (((1,), (1,)), ((), ())), preferred_element_type=F32)


def cost(micros):
    return pl.CostEstimate(flops=micros * 10**9, bytes_accessed=10**6, transcendentals=0)


def placed(pieces):
    if len(pieces) == 4:
        pieces = [p.at[n] for p, size in zip(pieces, (3, 2, 3, 2)) for n in range(size)]
    for n, piece in enumerate(pieces):
        y, x, first = PIECES[n % len(PIECES)]
        for z in range(piece.shape[0]):
            yield piece, (z,), n // len(PIECES), y, x, first + z


def place_copies(spot, pieces, wholes, rows_at, cols_at, widths, sems, near=False):
    if len(pieces) == len(wholes):
        return [
            pltpu.make_async_copy(piece, whole, sems.at[n])
            for n, (piece, whole) in enumerate(zip(pieces, wholes))
        ]
    copies = []
    for piece, index, core, y, x, z in placed(pieces):
        r = ((spot[0] ^ z if near else z) * 2 + (spot[1] ^ y)) * 2 + (spot[2] ^ core)
        c = spot[3] ^ x
        for whole, row, col, width in zip(wholes, rows_at, cols_at, widths):
            depth = whole.shape[0] // 16
            copies.append(
                pltpu.make_async_copy(
                    piece.at[(*index, pl.ds(row, depth), pl.ds(col, width))],
                    whole.at[
                        pl.ds(pl.multiple_of(r * depth, 16), depth),
                        pl.ds(pl.multiple_of(c * width, 128), width),
                    ],
                    sems.at[len(copies)],
                )
            )
    return copies


def send_copies(spot, source, keep, send, row, half, col, width, sems, near=False):
    depth = source.shape[0] // 16
    copies = []
    for j in range(8):
        z, y = j // 2, j % 2
        plane = (spot[1] ^ y) * 2 + (spot[3] ^ half)
        for n, (target, core) in enumerate(((keep, spot[2]), (send, 1 - spot[2]))):
            start = pl.multiple_of((2 * j + core) * depth, 16)
            copies.append(
                pltpu.make_async_copy(
                    source.at[pl.ds(start, depth), pl.ds(0, width)],
                    target.at[plane, spot[0] ^ z if near else z, pl.ds(row, depth), pl.ds(col, width)],
                    sems.at[2 * j + n],
                )
            )
    return copies


def attend_kernel(blocks, spot, starts, normed_ref, *rest):
    pieces, rest = rest[:blocks], rest[blocks:]
    pm_ref, po_ref, q_ref, k_ref, v_ref, out_ref, p_ref, wq, wk, wv, kt, bias, acc, sems = rest
    step = pl.program_id(0)
    half = normed_ref.shape[0] // 2

    @pl.when(step == 0)
    def _():
        width = wq.shape[1] // 2
        depth = wq.shape[0] // 16
        copies = place_copies(
            spot, pieces, (wq, wk, wv), (0, depth, 2 * depth), (0, 0, 0), (width,) * 3, sems, True
        )
        for copy in copies:
            copy.start()
        rows = lax.broadcasted_iota(jnp.int32, (half, half), 0)
        cols = lax.broadcasted_iota(jnp.int32, (half, half), 1)
        for b in range(2):
            i, j = rows + b * half, cols + b * half
            ok = j <= i
            for s in range(2):
                p = starts[0, s]
                ok = ok | ((i >= p) & (i < p + PIC) & (j >= p) & (j < p + PIC))
            bias[b] = jnp.where(ok, 0.0, -1e30)
        acc[...] = jnp.zeros_like(acc)
        for copy in copies:
            copy.wait()
        k_ref[...] = dot(normed_ref[...], wk[...]).astype(BF16)
        kt[...] = k_ref[...].T
        q_ref[...] = dot(normed_ref[...], wq[...]).astype(BF16)
        v_ref[...] = dot(normed_ref[...], wv[...]).astype(BF16)

    pm = pm_ref[0]
    po = po_ref[0]
    vs = (v_ref[...].astype(F32) * po).astype(BF16)
    top = (q_ref[:half].astype(F32) * pm).astype(BF16)
    low = (q_ref[half:].astype(F32) * pm).astype(BF16)
    s0 = dot(top, kt[:, :half]) + bias[0]
    s1 = dot(low, kt[:, :half])
    s2 = dot(low, kt[:, half:]) + bias[1]
    m0 = jnp.max(s0, axis=1, keepdims=True)
    e0 = jnp.exp(s0 - m0)
    p0 = (e0 / jnp.sum(e0, axis=1, keepdims=True)).astype(BF16)
    m1 = jnp.maximum(jnp.max(s1, axis=1, keepdims=True), jnp.max(s2, axis=1, keepdims=True))
    e1 = jnp.exp(s1 - m1)
    e2 = jnp.exp(s2 - m1)
    inv = 1.0 / (jnp.sum(e1, axis=1, keepdims=True) + jnp.sum(e2, axis=1, keepdims=True))
    p1 = (e1 * inv).astype(BF16)
    p2 = (e2 * inv).astype(BF16)
    p_ref[0, :, :half] = p0
    p_ref[0, :, half : 2 * half] = p1
    p_ref[0, :, 2 * half :] = p2
    acc[:half] += dot(p0, vs[:half])
    acc[half:] += dot(p1, vs[:half]) + dot(p2, vs[half:])

    @pl.when(step == HEADS - 1)
    def _():
        out_ref[...] = acc[...].astype(BF16)


def attend(spot, starts, normed, pieces, pm, po):
    seq, width = normed.shape
    half = seq // 2
    whole = pl.BlockSpec((seq, width), lambda h: (0, 0))
    row = pl.BlockSpec((1, 1, width), lambda h: (h, 0, 0))
    low = jax.ShapeDtypeStruct((seq, width), BF16)
    return pl.pallas_call(
        functools.partial(attend_kernel, len(pieces)),
        grid=(HEADS,),
        in_specs=[SMEM, SMEM, whole] + [ANY] * len(pieces) + [row, row],
        out_specs=[whole] * 4 + [pl.BlockSpec((1, half, 3 * half), lambda h: (h, 0, 0))],
        out_shape=[low] * 4 + [jax.ShapeDtypeStruct((HEADS, half, 3 * half), BF16)],
        scratch_shapes=[pltpu.VMEM((width, width), BF16)] * 3
        + [
            pltpu.VMEM((width, seq), BF16),
            pltpu.VMEM((2, half, half), F32),
            pltpu.VMEM((seq, width), F32),
            pltpu.SemaphoreType.DMA((96,)),
        ],
        compiler_params=PARAMS,
        name="attend",
        cost_estimate=cost(20),
    )(spot, starts, normed, *pieces, pm, po)


def middle_kernel(blocks, outs, tokens, spot, count, *rest):
    pieces, rest = rest[:blocks], rest[blocks:]
    att_ref, states_ref, up_ref, teach_ref, valid_ref, gain_ref = rest[:6]
    layer_ref, mid_ref, agrad_ref, sums_ref = rest[6:10]
    grads, rest = rest[10 : 10 + outs], rest[10 + outs :]
    wo, wu, wd, hidden, pre, n2t, olt, slots, marks, sems, out_sems, mark_sems = rest
    seq, width = att_ref.shape
    units = wu.shape[1]
    blocked = outs == 2
    mark_copies = []
    if blocked:
        for n, (piece, index, *_) in enumerate(placed(pieces)):
            mark_copies.append(
                pltpu.make_async_copy(
                    piece.at[(*index, pl.ds(0, 16), pl.ds((units + width) // 2, EXTRA))],
                    marks.at[n],
                    mark_sems.at[n],
                )
            )
    copies = place_copies(
        spot,
        pieces,
        (wo, wu, wd),
        (0, 0, 0),
        (units // 2, 0, (units + width) // 2 + EXTRA),
        (width // 2, units // 2, units // 2),
        sems,
    )
    for copy in mark_copies + copies[::3] + copies[1::3] + copies[2::3]:
        copy.start()
    for copy in mark_copies:
        copy.wait()
    total_valid = jnp.full((1, 1), count[0, 0], F32)
    if blocked:
        by_lane = jnp.sum(marks[...].astype(F32), axis=0)[:1]
        total_valid += jnp.sum(by_lane, axis=1, keepdims=True)
    factor = tokens / total_valid
    sums_ref[...] = jnp.broadcast_to(total_valid, sums_ref.shape)
    for copy in copies[::3]:
        copy.wait()
    mid_ref[...] = states_ref[...] + dot(att_ref[...], wo[...])
    middle = mid_ref[...]
    scale = lax.rsqrt(jnp.mean(middle * middle, axis=1, keepdims=True) + EPSILON)
    n2 = (middle * scale * gain_ref[...]).astype(BF16)
    n2t[...] = n2.T
    for copy in copies[1::3]:
        copy.wait()

    chunk = 512
    steps = units // chunk

    def up_step(j, _):
        at = pl.ds(pl.multiple_of(j * chunk, chunk), chunk)
        hidden[:, at] = jnp.maximum(dot(n2, wu[:, at]), 0.0).astype(BF16)
        return 0

    lax.fori_loop(0, steps, up_step, 0)
    for copy in copies[2::3]:
        copy.wait()
    layer_ref[...] = mid_ref[...] + dot_nt(hidden[...], wd[...])
    layer = layer_ref[...]
    valid = valid_ref[...].astype(F32)
    upstream = up_ref[...]
    differ = layer - teach_ref[...]
    sums_ref[1:2, :] = jnp.sum(valid * (differ * differ), axis=0, keepdims=True)
    sums_ref[2:3, :] = jnp.sum(valid * (upstream * layer), axis=0, keepdims=True)
    out_grad = (factor * valid) * (upstream + differ)
    out_low = out_grad.astype(BF16)
    olt[...] = out_low.T

    def down_step(j, _):
        at = pl.ds(pl.multiple_of(j * chunk, chunk), chunk)
        part = hidden[:, at]
        back = jnp.where(part > 0, dot(out_low, wd[:, at]), 0.0).astype(BF16)
        pre[:, at] = back
        for which, (left, right) in enumerate(((n2t, back), (olt, part))):
            slot = slots.at[which]

            @pl.when(j > 0)
            def _():
                for copy in grad_copies(which, j - 1):
                    copy.wait()

            slot[...] = dot(left[...], right).astype(BF16)
            for copy in grad_copies(which, j):
                copy.start()
        return 0

    def grad_copies(which, j):
        if not blocked:
            at = pl.ds(pl.multiple_of(j * chunk, chunk), chunk)
            return [pltpu.make_async_copy(slots.at[which], grads[which].at[:, at], out_sems.at[which, 0])]
        per = steps // 2
        return send_copies(
            spot,
            slots.at[which],
            grads[0],
            grads[1],
            0,
            j // per,
            pl.multiple_of(which * ((units + width) // 2) + (j % per) * chunk, 128),
            chunk,
            out_sems.at[which],
            True,
        )

    lax.fori_loop(0, steps, down_step, 0)
    grad = dot_nt(pre[...], wu[...])
    middle = mid_ref[...]
    scale = lax.rsqrt(jnp.mean(middle * middle, axis=1, keepdims=True) + EPSILON)
    sums_ref[0:1, :] = jnp.sum(grad * middle * scale, axis=0, keepdims=True)
    term = gain_ref[...] * grad
    inner = jnp.mean(term * middle, axis=1, keepdims=True)
    layer = layer_ref[...]
    out_grad = (factor * valid_ref[...].astype(F32)) * (
        up_ref[...] + (layer - teach_ref[...])
    )
    mid_grad = out_grad + scale * term - middle * (scale * scale * scale) * inner
    mid_ref[...] = mid_grad
    branch = mid_grad.astype(BF16)
    agrad_ref[...] = dot_nt(branch, wo[...]).astype(BF16)
    n2t[...] = att_ref[...].T
    for which in range(2):
        for copy in grad_copies(which, steps - 1):
            copy.wait()
    half = width // 2
    last = []
    for c in range(2):
        slots[c, :, :half] = dot(n2t[...], branch[:, c * half : (c + 1) * half]).astype(BF16)
        if blocked:
            made = send_copies(
                spot, slots.at[c], grads[0], grads[1], 0, c, units // 2, half, out_sems.at[c], True
            )
        else:
            made = [
                pltpu.make_async_copy(
                    slots.at[c, :, pl.ds(0, half)],
                    grads[2].at[:, pl.ds(c * half, half)],
                    out_sems.at[c, 0],
                )
            ]
        for copy in made:
            copy.start()
        last += made
    for copy in last:
        copy.wait()


def middle_block(blocked, spot, count, tokens, pieces, attended, states, upstream, teacher, valid, gain, units):
    seq, width = attended.shape
    full = jax.ShapeDtypeStruct((seq, width), F32)
    if blocked:
        depth = width // 16
        grads = [jax.ShapeDtypeStruct((4, 4, depth, units + width // 2), BF16)] * 2
    else:
        grads = [
            jax.ShapeDtypeStruct((width, units), BF16),
            jax.ShapeDtypeStruct((width, units), BF16),
            jax.ShapeDtypeStruct((width, width), BF16),
        ]
    return pl.pallas_call(
        functools.partial(middle_kernel, len(pieces), len(grads), tokens),
        in_specs=[SMEM, SMEM] + [ANY] * len(pieces) + [VMEM] * 6,
        out_specs=[VMEM] * 4 + [ANY] * len(grads),
        out_shape=[
            full,
            full,
            jax.ShapeDtypeStruct((seq, width), BF16),
            jax.ShapeDtypeStruct((8, width), F32),
        ]
        + grads,
        scratch_shapes=[
            pltpu.VMEM((width, width), BF16),
            pltpu.VMEM((width, units), BF16),
            pltpu.VMEM((width, units), BF16),
            pltpu.VMEM((seq, units), BF16),
            pltpu.VMEM((seq, units), BF16),
            pltpu.VMEM((width, seq), BF16),
            pltpu.VMEM((width, seq), BF16),
            pltpu.VMEM((2, width, 512), BF16),
            pltpu.VMEM((32, 16, EXTRA), BF16),
            pltpu.SemaphoreType.DMA((96,)),
            pltpu.SemaphoreType.DMA((2, 16)),
            pltpu.SemaphoreType.DMA((32,)),
        ],
        compiler_params=PARAMS,
        name="middle",
        cost_estimate=cost(35),
    )(spot, count, *pieces, attended, states, upstream, teacher, valid, gain)


def attend_back_kernel(
    blocked, spot, pms, pos, nt_ref, q_ref, k_ref, v_ref, g_ref, p_ref, pm_ref, po_ref,
    dq_ref, dk_ref, dv_ref, mix_ref, *rest,
):
    outs = 2 if blocked else 3
    grads = rest[:outs]
    vt, qt, gt, dq, dkt, dvt, pre, slots, sems = rest[outs:]
    step = pl.program_id(0)
    seq, width = q_ref.shape
    half = seq // 2

    @pl.when(step == 0)
    def _():
        vt[...] = v_ref[...].T
        qt[...] = q_ref[...].T
        gt[...] = g_ref[...].T
        dq[...] = jnp.zeros_like(dq)
        dkt[...] = jnp.zeros_like(dkt)
        dvt[...] = jnp.zeros_like(dvt)
        pre[...] = jnp.zeros_like(pre)
        mix_ref[...] = jnp.zeros_like(mix_ref)

    pm = pm_ref[0]
    po = po_ref[0]
    p0, p1, p2 = (p_ref[0, :, b * half : (b + 1) * half] for b in range(3))
    top = (g_ref[:half].astype(F32) * po).astype(BF16)
    low = (g_ref[half:].astype(F32) * po).astype(BF16)
    g0 = dot(top, vt[:, :half])
    g1 = dot(low, vt[:, :half])
    g2 = dot(low, vt[:, half:])
    u0 = dot(gt[:, :half], p0) + dot(gt[:, half:], p1)
    u1 = dot(gt[:, half:], p2)
    f0, f1, f2 = p0.astype(F32), p1.astype(F32), p2.astype(F32)
    t0 = f0 * g0
    d0 = (t0 - f0 * jnp.sum(t0, axis=1, keepdims=True)).astype(BF16)
    t1, t2 = f1 * g1, f2 * g2
    r1 = jnp.sum(t1, axis=1, keepdims=True) + jnp.sum(t2, axis=1, keepdims=True)
    d1 = (t1 - f1 * r1).astype(BF16)
    d2 = (t2 - f2 * r1).astype(BF16)
    w0 = dot(d0, k_ref[:half])
    w1 = dot(d1, k_ref[:half]) + dot(d2, k_ref[half:])
    dq[:half] += pm * w0
    dq[half:] += pm * w1
    row = jnp.sum(q_ref[:half].astype(F32) * w0, axis=0, keepdims=True) + jnp.sum(
        q_ref[half:].astype(F32) * w1, axis=0, keepdims=True
    )
    pre[...] += jnp.where(lax.broadcasted_iota(jnp.int32, pre.shape, 0) == step, row, 0.0)
    lane = lax.broadcasted_iota(jnp.int32, (1, 128), 1)
    posts = jnp.zeros((1, 128), F32)
    for g in range(HEADS):
        at = slice(g * HEAD_DIM, (g + 1) * HEAD_DIM)
        b = pos[step, g]
        u0g, u1g = u0[at], u1[at]
        dvt[at, :half] += b * u0g
        dvt[at, half:] += b * u1g
        both = u0g * vt[at, :half].astype(F32) + u1g * vt[at, half:].astype(F32)
        post = jnp.sum(jnp.sum(both, axis=0, keepdims=True), axis=1, keepdims=True)
        posts += jnp.where(lane == 16 + g, post, 0.0)
    mix_ref[...] += jnp.where(
        lax.broadcasted_iota(jnp.int32, mix_ref.shape, 0) == step, posts, 0.0
    )
    qs = jnp.concatenate(
        [
            (qt[g * HEAD_DIM : (g + 1) * HEAD_DIM].astype(F32) * pms[step, g]).astype(BF16)
            for g in range(HEADS)
        ],
        axis=0,
    )
    dkt[:, :half] += dot(qs[:, :half], d0) + dot(qs[:, half:], d1)
    dkt[:, half:] += dot(qs[:, half:], d2)

    @pl.when(step == HEADS - 1)
    def _():
        feature = lax.broadcasted_iota(jnp.int32, (width, 128), 0)
        head = lax.broadcasted_iota(jnp.int32, (width, 128), 1)
        member = (feature >= head * HEAD_DIM) & (feature < (head + 1) * HEAD_DIM)
        turned = lax.dot_general(
            member.astype(F32),
            pre[...],
            (((0,), (1,)), ((), ())),
            precision=lax.Precision.HIGHEST,
            preferred_element_type=F32,
        )
        mix_ref[:, :16] += turned[:16]
        dq_ref[...] = dq[...].astype(BF16)
        dk_ref[...] = dkt[...].astype(BF16).T
        dv_ref[...] = dvt[...].astype(BF16).T
        made = []
        for n, ref in enumerate((dq_ref, dk_ref, dv_ref)):
            slots[n] = dot(nt_ref[...], ref[...]).astype(BF16)
            if blocked:
                part = width // 2
                for c in range(2):
                    made += send_copies(
                        spot,
                        slots.at[n, :, pl.ds(c * part, part)],
                        grads[0],
                        grads[1],
                        n * (width // 16),
                        c,
                        0,
                        part,
                        sems.at[2 * n + c],
                        True,
                    )
            else:
                made.append(pltpu.make_async_copy(slots.at[n], grads[n], sems.at[n, 0]))
            for copy in made[-32 if blocked else -1 :]:
                copy.start()
        for copy in made:
            copy.wait()


def attend_back(spot, blocked, nt, q, k, v, g, p, pm, po, pms, pos):
    seq, width = q.shape
    half = seq // 2
    whole = pl.BlockSpec((seq, width), lambda h: (0, 0))
    row = pl.BlockSpec((1, 1, width), lambda h: (h, 0, 0))
    low = jax.ShapeDtypeStruct((seq, width), BF16)
    if blocked:
        grads = [jax.ShapeDtypeStruct((4, 4, 3 * (width // 16), width // 2), BF16)] * 2
    else:
        grads = [jax.ShapeDtypeStruct((width, width), BF16)] * 3
    return pl.pallas_call(
        functools.partial(attend_back_kernel, blocked),
        grid=(HEADS,),
        in_specs=[SMEM, SMEM, SMEM, pl.BlockSpec((width, seq), lambda h: (0, 0))]
        + [whole] * 4
        + [pl.BlockSpec((1, half, 3 * half), lambda h: (h, 0, 0)), row, row],
        out_specs=[whole] * 3
        + [pl.BlockSpec((16, 128), lambda h: (0, 0))]
        + [ANY] * len(grads),
        out_shape=[low] * 3
        + [jax.ShapeDtypeStruct((16, 128), F32)]
        + grads,
        scratch_shapes=[pltpu.VMEM((width, seq), BF16)] * 3
        + [
            pltpu.VMEM((seq, width), F32),
            pltpu.VMEM((width, seq), F32),
            pltpu.VMEM((width, seq), F32),
            pltpu.VMEM((16, width), F32),
            pltpu.VMEM((3, width, width), BF16),
            pltpu.SemaphoreType.DMA((6, 16)),
        ],
        compiler_params=PARAMS,
        name="attend_back",
        cost_estimate=cost(28),
    )(spot, pms, pos, nt, q, k, v, g, p, pm, po)


def input_kernel(blocks, spot, *rest):
    pieces, rest = rest[:blocks], rest[blocks:]
    dq_ref, dk_ref, dv_ref, states_ref, mid_ref, gain_ref, sums_ref, mix_ref = rest[:8]
    out_ref, small_ref, wq, wk, wv, sems = rest[8:]
    features = wq.shape[1]
    width = features // 2
    depth = wq.shape[0] // 16
    copies = place_copies(
        spot, pieces, (wq, wk, wv), (0, depth, 2 * depth), (0, 0, 0), (width,) * 3, sems, True
    )
    for copy in copies:
        copy.start()
    states = states_ref[...]
    scale = lax.rsqrt(jnp.mean(states * states, axis=1, keepdims=True) + EPSILON)
    for copy in copies:
        copy.wait()
    grad = (
        dot_nt(dq_ref[...], wq[...]) + dot_nt(dk_ref[...], wk[...]) + dot_nt(dv_ref[...], wv[...])
    )
    first = jnp.sum(grad * states * scale, axis=0, keepdims=True)
    parts = features // 128
    lane = lax.broadcasted_iota(jnp.int32, (1, 128), 1)
    losses = [jnp.sum(sums_ref[n : n + 1], axis=1, keepdims=True) for n in (1, 2)]
    for n in range(parts):
        at = slice(n * 128, (n + 1) * 128)
        small_ref[n : n + 1] = first[:, at]
        small_ref[parts + n : parts + n + 1] = sums_ref[:1, at]
    small_ref[2 * parts :] = mix_ref[:HEADS]
    small_ref[2 * parts : 2 * parts + 1] += jnp.where(
        lane == 32, losses[0], jnp.where(lane == 33, losses[1], 0.0)
    )
    term = gain_ref[...] * grad
    inner = jnp.mean(term * states, axis=1, keepdims=True)
    out_ref[...] = mid_ref[...] + scale * term - states * (scale * scale * scale) * inner


def input_block(spot, pieces, dq, dk, dv, states, mid_grad, gain, sums, mix):
    seq, width = dq.shape
    return pl.pallas_call(
        functools.partial(input_kernel, len(pieces)),
        in_specs=[SMEM] + [ANY] * len(pieces) + [VMEM] * 8,
        out_specs=[VMEM] * 2,
        out_shape=[
            jax.ShapeDtypeStruct((seq, width), F32),
            jax.ShapeDtypeStruct((2 * width // 128 + HEADS, 128), F32),
        ],
        scratch_shapes=[pltpu.VMEM((width, width), BF16)] * 3 + [pltpu.SemaphoreType.DMA((96,))],
        compiler_params=PARAMS,
        name="input_grad",
        cost_estimate=cost(9),
    )(spot, *pieces, dq, dk, dv, states, mid_grad, gain, sums, mix)


def exchange(value, mask, total):
    return lax.ppermute(value, AXES, [(i, i ^ mask) for i in range(total)])


def after(value, *others):
    return lax.optimization_barrier((value, *others))[0]


def over_lines(blocks):
    return lax.all_to_all(blocks, "row", 0, 0, axis_index_groups=LINES, tiled=True)


def late(value, rank):
    return 0.0 * value[(0,) * (value.ndim - rank)][(slice(1),) * rank].astype(F32)


def gather_line(packet):
    return over_lines(jnp.broadcast_to(packet, (4, *packet.shape)))


def gather_near(packet, total):
    return [packet, *[exchange(packet, m * Z_BIT, total) for m in (1, 2, 3)]]


def gather_sides(line, total):
    return exchange(line, X_BIT, total), exchange(line, Y_BIT, total)


def gather_halves(over_x, over_y, total):
    return exchange(over_x, Y_BIT, total), exchange(over_y, X_BIT, total)


def add_low(*terms):
    return functools.reduce(jnp.add, [t.astype(F32) for t in terms])


def reduce_core(keep, other):
    mine = add_low(keep, other).astype(BF16)
    return mine, mine[2:, :2], mine[1::2, 2:]


def reduce_first(over_y, over_x, total):
    return exchange(over_y, Y_BIT, total), exchange(over_x, X_BIT, total)


def reduce_sides(mine, over_y, over_x):
    return add_low(mine[1, :2], over_y[1]).astype(BF16), add_low(mine[2, 2:], over_x[1]).astype(BF16)


def reduce_second(side_x, side_y, total):
    return exchange(side_x, X_BIT, total), exchange(side_y, Y_BIT, total)


def reduce_own(mine, over_y, over_x):
    return add_low(mine[0, :2], over_y[0]), add_low(mine[0, 2:], over_x[0])


def reduce_line(head, tail, side_x, side_y):
    return jnp.concatenate([add_low(head, side_x), add_low(tail, side_y)])


def reduce_far(line, total):
    return [exchange(line[m].astype(BF16), m * Z_BIT, total) for m in (1, 2, 3)]


def gather_whole(block):
    rows, cols = lax.axis_size("row"), lax.axis_size("col")
    depth, width = block.shape
    every = lax.all_gather(block[None], AXES, axis=0, tiled=True)
    every = every.reshape(rows, cols, depth, width).transpose(0, 2, 1, 3)
    return every.reshape(rows * depth, cols * width)


def scatter_whole(grad):
    rows, cols = lax.axis_size("row"), lax.axis_size("col")
    depth, width = grad.shape[0] // rows, grad.shape[1] // cols
    parts = grad.reshape(rows, depth, cols, width).transpose(0, 2, 1, 3)
    parts = parts.reshape(rows * cols, depth, width).astype(F32)
    return lax.psum_scatter(parts, AXES, scatter_dimension=0, tiled=True)[0]


def shards(
    states,
    upstream,
    teacher,
    validity,
    picture_start,
    first_gain,
    query_weight,
    key_weight,
    value_weight,
    premix,
    postmix,
    output_weight,
    second_gain,
    up_weight,
    down_weight,
):
    row_total = lax.axis_size("row")
    col_total = lax.axis_size("col")
    total = row_total * col_total
    seq_len, features = states.shape
    depth, width = query_weight.shape
    units = up_weight.shape[1] * col_total
    blocked = (row_total, col_total) == (16, 2)
    row = lax.axis_index("row")
    spot = jnp.stack([row // 4, (row // 2) % 2, row % 2, lax.axis_index("col")]).astype(jnp.int32)
    down_turned = down_weight.T
    if blocked:
        packet = jnp.concatenate([query_weight, key_weight, value_weight], axis=0)
        qkv_near = gather_near(packet, total)
        qkv_line = jnp.stack(qkv_near)
        qkv_sides = gather_sides(qkv_line, total)
        marks = jnp.sum(validity.reshape(-1, EXTRA), axis=0).astype(F32)
        marks = jnp.broadcast_to(marks, (depth, EXTRA)).astype(BF16)
        packet = jnp.concatenate(
            [up_weight, output_weight, marks, down_turned], axis=1
        )
        line = gather_line(packet)
        *halves, qkv_line, side_x, side_y = lax.optimization_barrier(
            (qkv_sides[0][:2], qkv_sides[1][2:], qkv_line, *qkv_sides)
        )
        qkv = [jnp.stack([qkv_line, side_x, side_y]), jnp.stack(gather_halves(*halves, total))]
        qkv += [exchange(part, CORE_BIT, total) for part in qkv]
        line, *qkv = lax.optimization_barrier((line, *qkv))
        sides = gather_sides(line, total)
        total_valid = jnp.zeros((), F32)
    else:
        qkv = [gather_whole(w) for w in (query_weight, key_weight, value_weight)]
        rest = [gather_whole(w) for w in (output_weight, up_weight, down_turned)]
        total_valid = lax.psum(jnp.sum(validity).astype(F32), AXES)
    first_scale = lax.rsqrt(jnp.mean(states * states, axis=-1, keepdims=True) + EPSILON)
    normed = (states * first_scale * first_gain).astype(BF16)
    pms = premix.T * (HEAD_DIM**-0.5)
    pos = postmix
    pm = jnp.repeat(pms, HEAD_DIM, axis=1)[:, None]
    po = jnp.repeat(pos, HEAD_DIM, axis=1)[:, None]
    queries, keys, values, attended, probs = attend(spot, picture_start, normed, qkv, pm, po)
    if blocked:
        *sides, attended = lax.optimization_barrier((*sides, attended))
        *halves, line, side_x, side_y = lax.optimization_barrier(
            (sides[0][:2], sides[1][2:], line, *sides)
        )
        rest = [line, side_x, side_y, *gather_halves(*halves, total)]
        rest += [exchange(part, CORE_BIT, total) for part in rest]
    layer_out, mid_grad, attended_grad, sums, *grads = middle_block(
        blocked,
        spot,
        total_valid.reshape(1, 1),
        seq_len * total,
        rest,
        attended,
        states,
        upstream,
        teacher,
        validity[:, None],
        second_gain[None],
        units,
    )
    total_valid = sums[3, 0]
    nt = normed.T
    if blocked:
        ffn_mine, *first, attended_grad = lax.optimization_barrier(
            (*reduce_core(grads[0], exchange(grads[1], CORE_BIT, total)), attended_grad)
        )
        ffn_first = reduce_first(*first, total)
    else:
        up_grad, down_grad, output_grad = (scatter_whole(g) for g in grads)
        down_grad = down_grad.T
    dq, dk, dv, mix, *grads = attend_back(
        spot, blocked, nt, queries, keys, values, attended_grad, probs, pm, po, pms, pos
    )
    if blocked:
        *ffn_first, dq, dk, dv, mix, keep, send = lax.optimization_barrier(
            (*ffn_first, dq, dk, dv, mix, *grads)
        )
        other = exchange(send, CORE_BIT, total)
        ffn_sides = reduce_second(*reduce_sides(ffn_mine, *ffn_first), total)
        mine, *first, dq, dk, dv = lax.optimization_barrier((*reduce_core(keep, other), dq, dk, dv))
        first = reduce_first(*first, total)
        input_grad, small = input_block(
            spot, qkv, dq, dk, dv, states, mid_grad, first_gain[None], sums, mix
        )
        *ffn_sides, small = lax.optimization_barrier((*ffn_sides, small))
        ffn_line = reduce_line(*reduce_own(ffn_mine, *ffn_first), *ffn_sides)
        small += exchange(small, CORE_BIT, total)
        near = lax.reduce_precision(small, 8, 7)
        small = jnp.broadcast_to(jnp.concatenate([near, small - near]), (4, depth, 128))
        ffn_line = jnp.concatenate([ffn_line, small], axis=2)
        blocks = [ffn_line[m].astype(BF16) for m in (1, 2, 3)]
        ffn_far = [exchange(block, m * Z_BIT, total) for m, block in enumerate(blocks, 1)]
        *first, _, _, _ = lax.optimization_barrier((*first, *blocks))
        sides = reduce_sides(mine, *first)
        sides = reduce_second(*sides, total)
        ffn = add_low(ffn_line[0], *ffn_far) + late(sides[0], 2)
        ffn = with_layout_constraint(ffn, Layout((0, 1)))
        head, tail, ffn = lax.optimization_barrier((*reduce_own(mine, *first), ffn))
        line = reduce_line(head, tail, *sides)
        attn = add_low(line[0], *reduce_far(line, total))
        half = units // col_total
        up_grad, output_grad, down_grad, small = jnp.split(
            ffn, [half, half + width, 2 * half + width], axis=1
        )
        small = small[: depth // 2] + small[depth // 2 :] + late(line, 2)
        for bit in (X_BIT, Y_BIT):
            small += exchange(small, bit, total)
        down_grad = down_grad.T
        query_grad, key_grad, value_grad = (attn[n * depth : (n + 1) * depth] for n in range(3))
    else:
        query_grad, key_grad, value_grad = (scatter_whole(g) for g in grads)
        input_grad, small = input_block(
            spot, qkv, dq, dk, dv, states, mid_grad, first_gain[None], sums, mix
        )
        small = lax.psum(small, AXES)
    parts = features // 128
    first_grad = small[:parts].reshape(-1)
    second_grad = small[parts : 2 * parts].reshape(-1)
    small = small[2 * parts :]
    premix_grad = small[:, :HEADS] * (HEAD_DIM**-0.5)
    postmix_grad = small[:, 16 : 16 + HEADS]
    losses = small[0, 32:34]
    return (
        layer_out,
        losses[0] / (total_valid * features),
        losses[1] / total_valid,
        input_grad,
        first_grad,
        query_grad,
        key_grad,
        value_grad,
        premix_grad,
        postmix_grad,
        output_grad,
        second_grad,
        up_grad,
        down_grad,
    )


def solution(mesh):
    tokens, block = P(AXES, None), P("row", "col")
    return jax.shard_map(
        shards,
        mesh=mesh,
        in_specs=(
            tokens, tokens, tokens, P(AXES), tokens, P(), block, block, block, P(), P(), block,
            P(), block, P("col", "row"),
        ),
        out_specs=(
            tokens, P(), P(), tokens, P(), block, block, block, P(), P(), block, P(), block,
            P("col", "row"),
        ),
        check_vma=False,
    )
```

```python
import functools

import jax
import jax.numpy as jnp
from jax import lax
from jax.experimental import pallas as pl
from jax.experimental.layout import Layout, with_layout_constraint
from jax.experimental.pallas import tpu as pltpu
from jax.sharding import PartitionSpec as P

HEADS = 12
HEAD_DIM = 64
PIC = 256
EPSILON = 1e-06
F32 = jnp.float32
BF16 = jnp.bfloat16
AXES = ("row", "col")
X_BIT, CORE_BIT, Y_BIT, Z_BIT = 1, 2, 4, 8
LINES = [[at + Z_BIT // 2 * z for z in range(4)] for at in range(4)]
EXTRA = 128
PIECES = ((0, 0, 0), (0, 1, 0), (1, 0, 0), (1, 1, 0), (1, 1, 2))
PARAMS = pltpu.CompilerParams(vmem_limit_bytes=60000 * 1024)
SMEM = pl.BlockSpec(memory_space=pltpu.SMEM)
ANY = pl.BlockSpec(memory_space=pl.ANY)
VMEM = pl.BlockSpec(memory_space=pltpu.VMEM)


def dot(a, b):
    return lax.dot_general(a, b, (((1,), (0,)), ((), ())), preferred_element_type=F32)


def dot_nt(a, b):
    return lax.dot_general(a, b, (((1,), (1,)), ((), ())), preferred_element_type=F32)


def cost(micros):
    return pl.CostEstimate(flops=micros * 10**9, bytes_accessed=10**6, transcendentals=0)


def placed(pieces):
    if len(pieces) == 4:
        pieces = [p.at[n] for p, size in zip(pieces, (3, 2, 3, 2)) for n in range(size)]
    for n, piece in enumerate(pieces):
        y, x, first = PIECES[n % len(PIECES)]
        for z in range(piece.shape[0]):
            yield piece, (z,), n // len(PIECES), y, x, first + z


def place_copies(spot, pieces, wholes, rows_at, cols_at, widths, sems, near=False):
    if len(pieces) == len(wholes):
        return [
            pltpu.make_async_copy(piece, whole, sems.at[n])
            for n, (piece, whole) in enumerate(zip(pieces, wholes))
        ]
    copies = []
    for piece, index, core, y, x, z in placed(pieces):
        r = ((spot[0] ^ z if near else z) * 2 + (spot[1] ^ y)) * 2 + (spot[2] ^ core)
        c = spot[3] ^ x
        for whole, row, col, width in zip(wholes, rows_at, cols_at, widths):
            depth = whole.shape[0] // 16
            copies.append(
                pltpu.make_async_copy(
                    piece.at[(*index, pl.ds(row, depth), pl.ds(col, width))],
                    whole.at[
                        pl.ds(pl.multiple_of(r * depth, 16), depth),
                        pl.ds(pl.multiple_of(c * width, 128), width),
                    ],
                    sems.at[len(copies)],
                )
            )
    return copies


def send_copies(spot, source, keep, send, row, half, col, width, sems, near=False):
    depth = source.shape[0] // 16
    copies = []
    for j in range(8):
        z, y = j // 2, j % 2
        plane = (spot[1] ^ y) * 2 + (spot[3] ^ half)
        for n, (target, core) in enumerate(((keep, spot[2]), (send, 1 - spot[2]))):
            start = pl.multiple_of((2 * j + core) * depth, 16)
            copies.append(
                pltpu.make_async_copy(
                    source.at[pl.ds(start, depth), pl.ds(0, width)],
                    target.at[plane, spot[0] ^ z if near else z, pl.ds(row, depth), pl.ds(col, width)],
                    sems.at[2 * j + n],
                )
            )
    return copies


def attend_kernel(blocks, spot, starts, normed_ref, *rest):
    pieces, rest = rest[:blocks], rest[blocks:]
    pm_ref, po_ref, q_ref, k_ref, v_ref, out_ref, p_ref, wq, wk, wv, kt, bias, acc, sems = rest
    step = pl.program_id(0)
    half = normed_ref.shape[0] // 2

    @pl.when(step == 0)
    def _():
        width = wq.shape[1] // 2
        depth = wq.shape[0] // 16
        copies = place_copies(
            spot, pieces, (wq, wk, wv), (0, depth, 2 * depth), (0, 0, 0), (width,) * 3, sems, True
        )
        for copy in copies:
            copy.start()
        rows = lax.broadcasted_iota(jnp.int32, (half, half), 0)
        cols = lax.broadcasted_iota(jnp.int32, (half, half), 1)
        for b in range(2):
            i, j = rows + b * half, cols + b * half
            ok = j <= i
            for s in range(2):
                p = starts[0, s]
                ok = ok | ((i >= p) & (i < p + PIC) & (j >= p) & (j < p + PIC))
            bias[b] = jnp.where(ok, 0.0, -1e30)
        acc[...] = jnp.zeros_like(acc)
        for copy in copies:
            copy.wait()
        k_ref[...] = dot(normed_ref[...], wk[...]).astype(BF16)
        kt[...] = k_ref[...].T
        q_ref[...] = dot(normed_ref[...], wq[...]).astype(BF16)
        v_ref[...] = dot(normed_ref[...], wv[...]).astype(BF16)

    pm = pm_ref[0]
    po = po_ref[0]
    vs = (v_ref[...].astype(F32) * po).astype(BF16)
    top = (q_ref[:half].astype(F32) * pm).astype(BF16)
    low = (q_ref[half:].astype(F32) * pm).astype(BF16)
    s0 = dot(top, kt[:, :half]) + bias[0]
    s1 = dot(low, kt[:, :half])
    s2 = dot(low, kt[:, half:]) + bias[1]
    m0 = jnp.max(s0, axis=1, keepdims=True)
    e0 = jnp.exp(s0 - m0)
    p0 = (e0 / jnp.sum(e0, axis=1, keepdims=True)).astype(BF16)
    m1 = jnp.maximum(jnp.max(s1, axis=1, keepdims=True), jnp.max(s2, axis=1, keepdims=True))
    e1 = jnp.exp(s1 - m1)
    e2 = jnp.exp(s2 - m1)
    inv = 1.0 / (jnp.sum(e1, axis=1, keepdims=True) + jnp.sum(e2, axis=1, keepdims=True))
    p1 = (e1 * inv).astype(BF16)
    p2 = (e2 * inv).astype(BF16)
    p_ref[0, :, :half] = p0
    p_ref[0, :, half : 2 * half] = p1
    p_ref[0, :, 2 * half :] = p2
    acc[:half] += dot(p0, vs[:half])
    acc[half:] += dot(p1, vs[:half]) + dot(p2, vs[half:])

    @pl.when(step == HEADS - 1)
    def _():
        out_ref[...] = acc[...].astype(BF16)


def attend(spot, starts, normed, pieces, pm, po):
    seq, width = normed.shape
    half = seq // 2
    whole = pl.BlockSpec((seq, width), lambda h: (0, 0))
    row = pl.BlockSpec((1, 1, width), lambda h: (h, 0, 0))
    low = jax.ShapeDtypeStruct((seq, width), BF16)
    return pl.pallas_call(
        functools.partial(attend_kernel, len(pieces)),
        grid=(HEADS,),
        in_specs=[SMEM, SMEM, whole] + [ANY] * len(pieces) + [row, row],
        out_specs=[whole] * 4 + [pl.BlockSpec((1, half, 3 * half), lambda h: (h, 0, 0))],
        out_shape=[low] * 4 + [jax.ShapeDtypeStruct((HEADS, half, 3 * half), BF16)],
        scratch_shapes=[pltpu.VMEM((width, width), BF16)] * 3
        + [
            pltpu.VMEM((width, seq), BF16),
            pltpu.VMEM((2, half, half), F32),
            pltpu.VMEM((seq, width), F32),
            pltpu.SemaphoreType.DMA((96,)),
        ],
        compiler_params=PARAMS,
        name="attend",
        cost_estimate=cost(20),
    )(spot, starts, normed, *pieces, pm, po)


def middle_kernel(blocks, outs, tokens, spot, count, *rest):
    pieces, rest = rest[:blocks], rest[blocks:]
    sources, valid_ref, gain_ref = rest[:4], rest[4], rest[5]
    layer_ref, mid_ref, agrad_ref, sums_ref = rest[6:10]
    grads, rest = rest[10 : 10 + outs], rest[10 + outs :]
    wo, wu, wd, hidden, pre, n2t, olt, slots, marks, sems, out_sems, mark_sems, *rest = rest
    att_ref, states_ref, up_ref, teach_ref, in_sems = rest
    seq, width = att_ref.shape
    units = wu.shape[1]
    blocked = outs == 2
    mark_copies = []
    if blocked:
        for n, (piece, index, *_) in enumerate(placed(pieces)):
            mark_copies.append(
                pltpu.make_async_copy(
                    piece.at[(*index, pl.ds(0, 16), pl.ds((units + width) // 2, EXTRA))],
                    marks.at[n],
                    mark_sems.at[n],
                )
            )
    copies = place_copies(
        spot,
        pieces,
        (wo, wu, wd),
        (0, 0, 0),
        (units // 2, 0, (units + width) // 2 + EXTRA),
        (width // 2, units // 2, units // 2),
        sems,
    )
    loads = [
        pltpu.make_async_copy(source, target, in_sems.at[n])
        for n, (source, target) in enumerate(zip(sources, (att_ref, states_ref, up_ref, teach_ref)))
    ]
    early = mark_copies + loads[:1] + copies[::3] + loads[1:2]
    for copy in early + copies[1::3] + copies[2::3] + loads[2:]:
        copy.start()
    for copy in mark_copies:
        copy.wait()
    total_valid = jnp.full((1, 1), count[0, 0], F32)
    if blocked:
        by_lane = jnp.sum(marks[...].astype(F32), axis=0)[:1]
        total_valid += jnp.sum(by_lane, axis=1, keepdims=True)
    factor = tokens / total_valid
    sums_ref[...] = jnp.broadcast_to(total_valid, sums_ref.shape)
    for copy in loads[:1] + copies[::3] + loads[1:2]:
        copy.wait()
    mid_ref[...] = states_ref[...] + dot(att_ref[...], wo[...])
    middle = mid_ref[...]
    scale = lax.rsqrt(jnp.mean(middle * middle, axis=1, keepdims=True) + EPSILON)
    n2 = (middle * scale * gain_ref[...]).astype(BF16)
    n2t[...] = n2.T
    for copy in copies[1::3]:
        copy.wait()

    chunk = 512
    steps = units // chunk

    def up_step(j, _):
        at = pl.ds(pl.multiple_of(j * chunk, chunk), chunk)
        hidden[:, at] = jnp.maximum(dot(n2, wu[:, at]), 0.0).astype(BF16)
        return 0

    lax.fori_loop(0, steps, up_step, 0)
    for copy in copies[2::3] + loads[2:]:
        copy.wait()
    layer_ref[...] = mid_ref[...] + dot_nt(hidden[...], wd[...])
    layer = layer_ref[...]
    valid = valid_ref[...].astype(F32)
    upstream = up_ref[...]
    differ = layer - teach_ref[...]
    sums_ref[1:2, :] = jnp.sum(valid * (differ * differ), axis=0, keepdims=True)
    sums_ref[2:3, :] = jnp.sum(valid * (upstream * layer), axis=0, keepdims=True)
    out_grad = (factor * valid) * (upstream + differ)
    out_low = out_grad.astype(BF16)
    olt[...] = out_low.T

    def down_step(j, _):
        at = pl.ds(pl.multiple_of(j * chunk, chunk), chunk)
        part = hidden[:, at]
        back = jnp.where(part > 0, dot(out_low, wd[:, at]), 0.0).astype(BF16)
        pre[:, at] = back
        for which, (left, right) in enumerate(((n2t, back), (olt, part))):
            slot = slots.at[which]

            @pl.when(j > 0)
            def _():
                for copy in grad_copies(which, j - 1):
                    copy.wait()

            slot[...] = dot(left[...], right).astype(BF16)
            for copy in grad_copies(which, j):
                copy.start()
        return 0

    def grad_copies(which, j):
        if not blocked:
            at = pl.ds(pl.multiple_of(j * chunk, chunk), chunk)
            return [pltpu.make_async_copy(slots.at[which], grads[which].at[:, at], out_sems.at[which, 0])]
        per = steps // 2
        return send_copies(
            spot,
            slots.at[which],
            grads[0],
            grads[1],
            0,
            j // per,
            pl.multiple_of(which * ((units + width) // 2) + (j % per) * chunk, 128),
            chunk,
            out_sems.at[which],
            True,
        )

    lax.fori_loop(0, steps, down_step, 0)
    grad = dot_nt(pre[...], wu[...])
    middle = mid_ref[...]
    scale = lax.rsqrt(jnp.mean(middle * middle, axis=1, keepdims=True) + EPSILON)
    sums_ref[0:1, :] = jnp.sum(grad * middle * scale, axis=0, keepdims=True)
    term = gain_ref[...] * grad
    inner = jnp.mean(term * middle, axis=1, keepdims=True)
    layer = layer_ref[...]
    out_grad = (factor * valid_ref[...].astype(F32)) * (
        up_ref[...] + (layer - teach_ref[...])
    )
    mid_grad = out_grad + scale * term - middle * (scale * scale * scale) * inner
    mid_ref[...] = mid_grad
    branch = mid_grad.astype(BF16)
    agrad_ref[...] = dot_nt(branch, wo[...]).astype(BF16)
    n2t[...] = att_ref[...].T
    for which in range(2):
        for copy in grad_copies(which, steps - 1):
            copy.wait()
    half = width // 2
    last = []
    for c in range(2):
        slots[c, :, :half] = dot(n2t[...], branch[:, c * half : (c + 1) * half]).astype(BF16)
        if blocked:
            made = send_copies(
                spot, slots.at[c], grads[0], grads[1], 0, c, units // 2, half, out_sems.at[c], True
            )
        else:
            made = [
                pltpu.make_async_copy(
                    slots.at[c, :, pl.ds(0, half)],
                    grads[2].at[:, pl.ds(c * half, half)],
                    out_sems.at[c, 0],
                )
            ]
        for copy in made:
            copy.start()
        last += made
    for copy in last:
        copy.wait()


def middle_block(blocked, spot, count, tokens, pieces, attended, states, upstream, teacher, valid, gain, units):
    seq, width = attended.shape
    full = jax.ShapeDtypeStruct((seq, width), F32)
    if blocked:
        depth = width // 16
        grads = [jax.ShapeDtypeStruct((4, 4, depth, units + width // 2), BF16)] * 2
    else:
        grads = [
            jax.ShapeDtypeStruct((width, units), BF16),
            jax.ShapeDtypeStruct((width, units), BF16),
            jax.ShapeDtypeStruct((width, width), BF16),
        ]
    return pl.pallas_call(
        functools.partial(middle_kernel, len(pieces), len(grads), tokens),
        in_specs=[SMEM, SMEM] + [ANY] * (len(pieces) + 4) + [VMEM] * 2,
        out_specs=[VMEM] * 4 + [ANY] * len(grads),
        out_shape=[
            full,
            full,
            jax.ShapeDtypeStruct((seq, width), BF16),
            jax.ShapeDtypeStruct((8, width), F32),
        ]
        + grads,
        scratch_shapes=[
            pltpu.VMEM((width, width), BF16),
            pltpu.VMEM((width, units), BF16),
            pltpu.VMEM((width, units), BF16),
            pltpu.VMEM((seq, units), BF16),
            pltpu.VMEM((seq, units), BF16),
            pltpu.VMEM((width, seq), BF16),
            pltpu.VMEM((width, seq), BF16),
            pltpu.VMEM((2, width, 512), BF16),
            pltpu.VMEM((32, 16, EXTRA), BF16),
            pltpu.SemaphoreType.DMA((96,)),
            pltpu.SemaphoreType.DMA((2, 16)),
            pltpu.SemaphoreType.DMA((32,)),
            pltpu.VMEM((seq, width), BF16),
            pltpu.VMEM((seq, width), F32),
            pltpu.VMEM((seq, width), F32),
            pltpu.VMEM((seq, width), F32),
            pltpu.SemaphoreType.DMA((4,)),
        ],
        compiler_params=PARAMS,
        name="middle",
        cost_estimate=cost(35),
    )(spot, count, *pieces, attended, states, upstream, teacher, valid, gain)


def attend_back_kernel(
    blocked, spot, pms, pos, nt_ref, q_ref, k_ref, v_ref, g_ref, p_ref, pm_ref, po_ref,
    dq_ref, dk_ref, dv_ref, mix_ref, *rest,
):
    outs = 2 if blocked else 3
    grads = rest[:outs]
    vt, qt, gt, dq, dkt, dvt, pre, slots, sems = rest[outs:]
    step = pl.program_id(0)
    seq, width = q_ref.shape
    half = seq // 2

    @pl.when(step == 0)
    def _():
        vt[...] = v_ref[...].T
        qt[...] = q_ref[...].T
        gt[...] = g_ref[...].T
        dq[...] = jnp.zeros_like(dq)
        dkt[...] = jnp.zeros_like(dkt)
        dvt[...] = jnp.zeros_like(dvt)
        pre[...] = jnp.zeros_like(pre)
        mix_ref[...] = jnp.zeros_like(mix_ref)

    pm = pm_ref[0]
    po = po_ref[0]
    p0, p1, p2 = (p_ref[0, :, b * half : (b + 1) * half] for b in range(3))
    top = (g_ref[:half].astype(F32) * po).astype(BF16)
    low = (g_ref[half:].astype(F32) * po).astype(BF16)
    g0 = dot(top, vt[:, :half])
    g1 = dot(low, vt[:, :half])
    g2 = dot(low, vt[:, half:])
    u0 = dot(gt[:, :half], p0) + dot(gt[:, half:], p1)
    u1 = dot(gt[:, half:], p2)
    f0, f1, f2 = p0.astype(F32), p1.astype(F32), p2.astype(F32)
    t0 = f0 * g0
    d0 = (t0 - f0 * jnp.sum(t0, axis=1, keepdims=True)).astype(BF16)
    t1, t2 = f1 * g1, f2 * g2
    r1 = jnp.sum(t1, axis=1, keepdims=True) + jnp.sum(t2, axis=1, keepdims=True)
    d1 = (t1 - f1 * r1).astype(BF16)
    d2 = (t2 - f2 * r1).astype(BF16)
    w0 = dot(d0, k_ref[:half])
    w1 = dot(d1, k_ref[:half]) + dot(d2, k_ref[half:])
    dq[:half] += pm * w0
    dq[half:] += pm * w1
    row = jnp.sum(q_ref[:half].astype(F32) * w0, axis=0, keepdims=True) + jnp.sum(
        q_ref[half:].astype(F32) * w1, axis=0, keepdims=True
    )
    pre[...] += jnp.where(lax.broadcasted_iota(jnp.int32, pre.shape, 0) == step, row, 0.0)
    lane = lax.broadcasted_iota(jnp.int32, (1, 128), 1)
    posts = jnp.zeros((1, 128), F32)
    for g in range(HEADS):
        at = slice(g * HEAD_DIM, (g + 1) * HEAD_DIM)
        b = pos[step, g]
        u0g, u1g = u0[at], u1[at]
        dvt[at, :half] += b * u0g
        dvt[at, half:] += b * u1g
        both = u0g * vt[at, :half].astype(F32) + u1g * vt[at, half:].astype(F32)
        post = jnp.sum(jnp.sum(both, axis=0, keepdims=True), axis=1, keepdims=True)
        posts += jnp.where(lane == 16 + g, post, 0.0)
    mix_ref[...] += jnp.where(
        lax.broadcasted_iota(jnp.int32, mix_ref.shape, 0) == step, posts, 0.0
    )
    qs = jnp.concatenate(
        [
            (qt[g * HEAD_DIM : (g + 1) * HEAD_DIM].astype(F32) * pms[step, g]).astype(BF16)
            for g in range(HEADS)
        ],
        axis=0,
    )
    dkt[:, :half] += dot(qs[:, :half], d0) + dot(qs[:, half:], d1)
    dkt[:, half:] += dot(qs[:, half:], d2)

    @pl.when(step == HEADS - 1)
    def _():
        feature = lax.broadcasted_iota(jnp.int32, (width, 128), 0)
        head = lax.broadcasted_iota(jnp.int32, (width, 128), 1)
        member = (feature >= head * HEAD_DIM) & (feature < (head + 1) * HEAD_DIM)
        turned = lax.dot_general(
            member.astype(F32),
            pre[...],
            (((0,), (1,)), ((), ())),
            precision=lax.Precision.HIGHEST,
            preferred_element_type=F32,
        )
        mix_ref[:, :16] += turned[:16]
        dq_ref[...] = dq[...].astype(BF16)
        dk_ref[...] = dkt[...].astype(BF16).T
        dv_ref[...] = dvt[...].astype(BF16).T
        made = []
        for n, ref in enumerate((dq_ref, dk_ref, dv_ref)):
            slots[n] = dot(nt_ref[...], ref[...]).astype(BF16)
            if blocked:
                part = width // 2
                for c in range(2):
                    made += send_copies(
                        spot,
                        slots.at[n, :, pl.ds(c * part, part)],
                        grads[0],
                        grads[1],
                        n * (width // 16),
                        c,
                        0,
                        part,
                        sems.at[2 * n + c],
                        True,
                    )
            else:
                made.append(pltpu.make_async_copy(slots.at[n], grads[n], sems.at[n, 0]))
            for copy in made[-32 if blocked else -1 :]:
                copy.start()
        for copy in made:
            copy.wait()


def attend_back(spot, blocked, nt, q, k, v, g, p, pm, po, pms, pos):
    seq, width = q.shape
    half = seq // 2
    whole = pl.BlockSpec((seq, width), lambda h: (0, 0))
    row = pl.BlockSpec((1, 1, width), lambda h: (h, 0, 0))
    low = jax.ShapeDtypeStruct((seq, width), BF16)
    if blocked:
        grads = [jax.ShapeDtypeStruct((4, 4, 3 * (width // 16), width // 2), BF16)] * 2
    else:
        grads = [jax.ShapeDtypeStruct((width, width), BF16)] * 3
    return pl.pallas_call(
        functools.partial(attend_back_kernel, blocked),
        grid=(HEADS,),
        in_specs=[SMEM, SMEM, SMEM, pl.BlockSpec((width, seq), lambda h: (0, 0))]
        + [whole] * 4
        + [pl.BlockSpec((1, half, 3 * half), lambda h: (h, 0, 0)), row, row],
        out_specs=[whole] * 3
        + [pl.BlockSpec((16, 128), lambda h: (0, 0))]
        + [ANY] * len(grads),
        out_shape=[low] * 3
        + [jax.ShapeDtypeStruct((16, 128), F32)]
        + grads,
        scratch_shapes=[pltpu.VMEM((width, seq), BF16)] * 3
        + [
            pltpu.VMEM((seq, width), F32),
            pltpu.VMEM((width, seq), F32),
            pltpu.VMEM((width, seq), F32),
            pltpu.VMEM((16, width), F32),
            pltpu.VMEM((3, width, width), BF16),
            pltpu.SemaphoreType.DMA((6, 16)),
        ],
        compiler_params=PARAMS,
        name="attend_back",
        cost_estimate=cost(28),
    )(spot, pms, pos, nt, q, k, v, g, p, pm, po)


def input_kernel(blocks, spot, *rest):
    pieces, rest = rest[:blocks], rest[blocks:]
    dq_ref, dk_ref, dv_ref, states_ref, mid_ref, gain_ref, sums_ref, mix_ref = rest[:8]
    out_ref, small_ref, wq, wk, wv, sems = rest[8:]
    features = wq.shape[1]
    width = features // 2
    depth = wq.shape[0] // 16
    copies = place_copies(
        spot, pieces, (wq, wk, wv), (0, depth, 2 * depth), (0, 0, 0), (width,) * 3, sems, True
    )
    for copy in copies:
        copy.start()
    states = states_ref[...]
    scale = lax.rsqrt(jnp.mean(states * states, axis=1, keepdims=True) + EPSILON)
    for copy in copies:
        copy.wait()
    grad = (
        dot_nt(dq_ref[...], wq[...]) + dot_nt(dk_ref[...], wk[...]) + dot_nt(dv_ref[...], wv[...])
    )
    first = jnp.sum(grad * states * scale, axis=0, keepdims=True)
    parts = features // 128
    lane = lax.broadcasted_iota(jnp.int32, (1, 128), 1)
    losses = [jnp.sum(sums_ref[n : n + 1], axis=1, keepdims=True) for n in (1, 2)]
    for n in range(parts):
        at = slice(n * 128, (n + 1) * 128)
        small_ref[n : n + 1] = first[:, at]
        small_ref[parts + n : parts + n + 1] = sums_ref[:1, at]
    small_ref[2 * parts :] = mix_ref[:HEADS]
    small_ref[2 * parts : 2 * parts + 1] += jnp.where(
        lane == 32, losses[0], jnp.where(lane == 33, losses[1], 0.0)
    )
    term = gain_ref[...] * grad
    inner = jnp.mean(term * states, axis=1, keepdims=True)
    out_ref[...] = mid_ref[...] + scale * term - states * (scale * scale * scale) * inner


def input_block(spot, pieces, dq, dk, dv, states, mid_grad, gain, sums, mix):
    seq, width = dq.shape
    return pl.pallas_call(
        functools.partial(input_kernel, len(pieces)),
        in_specs=[SMEM] + [ANY] * len(pieces) + [VMEM] * 8,
        out_specs=[VMEM] * 2,
        out_shape=[
            jax.ShapeDtypeStruct((seq, width), F32),
            jax.ShapeDtypeStruct((2 * width // 128 + HEADS, 128), F32),
        ],
        scratch_shapes=[pltpu.VMEM((width, width), BF16)] * 3 + [pltpu.SemaphoreType.DMA((96,))],
        compiler_params=PARAMS,
        name="input_grad",
        cost_estimate=cost(9),
    )(spot, *pieces, dq, dk, dv, states, mid_grad, gain, sums, mix)


def exchange(value, mask, total):
    return lax.ppermute(value, AXES, [(i, i ^ mask) for i in range(total)])


def after(value, *others):
    return lax.optimization_barrier((value, *others))[0]


def over_lines(blocks):
    return lax.all_to_all(blocks, "row", 0, 0, axis_index_groups=LINES, tiled=True)


def late(value, rank):
    return 0.0 * value[(0,) * (value.ndim - rank)][(slice(1),) * rank].astype(F32)


def gather_line(packet):
    return over_lines(jnp.broadcast_to(packet, (4, *packet.shape)))


def gather_near(packet, total):
    return [packet, *[exchange(packet, m * Z_BIT, total) for m in (1, 2, 3)]]


def gather_sides(line, total):
    return exchange(line, X_BIT, total), exchange(line, Y_BIT, total)


def gather_halves(over_x, over_y, total):
    return exchange(over_x, Y_BIT, total), exchange(over_y, X_BIT, total)


def add_low(*terms):
    return functools.reduce(jnp.add, [t.astype(F32) for t in terms])


def core_sum(terms, *index):
    return add_low(*[term[index] for term in terms])


def reduce_core(terms):
    low, high = slice(0, 2), slice(2, 4)
    planes = slice(2, 4), slice(1, 4, 2)
    return [core_sum(terms, p, z).astype(BF16) for p, z in zip(planes, (low, high))]


def reduce_first(over_y, over_x, total):
    return exchange(over_y, Y_BIT, total), exchange(over_x, X_BIT, total)


def reduce_sides(terms, over_y, over_x):
    return [
        (core_sum(terms, plane, z) + over[1]).astype(BF16)
        for plane, z, over in ((1, slice(0, 2), over_y), (2, slice(2, 4), over_x))
    ]


def reduce_second(side_x, side_y, total):
    return exchange(side_x, X_BIT, total), exchange(side_y, Y_BIT, total)


def reduce_own(terms, over_y, over_x):
    return [
        core_sum(terms, 0, z) + over[0]
        for z, over in ((slice(0, 2), over_y), (slice(2, 4), over_x))
    ]


def reduce_line(head, tail, side_x, side_y):
    return jnp.concatenate([add_low(head, side_x), add_low(tail, side_y)])


def reduce_far(line, total):
    return [exchange(line[m].astype(BF16), m * Z_BIT, total) for m in (1, 2, 3)]


def gather_whole(block):
    rows, cols = lax.axis_size("row"), lax.axis_size("col")
    depth, width = block.shape
    every = lax.all_gather(block[None], AXES, axis=0, tiled=True)
    every = every.reshape(rows, cols, depth, width).transpose(0, 2, 1, 3)
    return every.reshape(rows * depth, cols * width)


def scatter_whole(grad):
    rows, cols = lax.axis_size("row"), lax.axis_size("col")
    depth, width = grad.shape[0] // rows, grad.shape[1] // cols
    parts = grad.reshape(rows, depth, cols, width).transpose(0, 2, 1, 3)
    parts = parts.reshape(rows * cols, depth, width).astype(F32)
    return lax.psum_scatter(parts, AXES, scatter_dimension=0, tiled=True)[0]


def shards(
    states,
    upstream,
    teacher,
    validity,
    picture_start,
    first_gain,
    query_weight,
    key_weight,
    value_weight,
    premix,
    postmix,
    output_weight,
    second_gain,
    up_weight,
    down_weight,
):
    row_total = lax.axis_size("row")
    col_total = lax.axis_size("col")
    total = row_total * col_total
    seq_len, features = states.shape
    depth, width = query_weight.shape
    units = up_weight.shape[1] * col_total
    blocked = (row_total, col_total) == (16, 2)
    row = lax.axis_index("row")
    spot = jnp.stack([row // 4, (row // 2) % 2, row % 2, lax.axis_index("col")]).astype(jnp.int32)
    down_turned = down_weight.T
    if blocked:
        packet = jnp.concatenate([query_weight, key_weight, value_weight], axis=0)
        qkv_near = gather_near(packet, total)
        qkv_line = jnp.stack(qkv_near)
        qkv_sides = gather_sides(qkv_line, total)
        marks = jnp.sum(validity.reshape(-1, EXTRA), axis=0).astype(F32)
        marks = jnp.broadcast_to(marks, (depth, EXTRA)).astype(BF16)
        packet = jnp.concatenate(
            [up_weight, output_weight, marks, down_turned], axis=1
        )
        line = gather_line(packet)
        *halves, qkv_line, side_x, side_y = lax.optimization_barrier(
            (qkv_sides[0][:2], qkv_sides[1][2:], qkv_line, *qkv_sides)
        )
        qkv = [jnp.stack([qkv_line, side_x, side_y]), jnp.stack(gather_halves(*halves, total))]
        qkv += [exchange(part, CORE_BIT, total) for part in qkv]
        line, *qkv = lax.optimization_barrier((line, *qkv))
        sides = gather_sides(line, total)
        total_valid = jnp.zeros((), F32)
    else:
        qkv = [gather_whole(w) for w in (query_weight, key_weight, value_weight)]
        rest = [gather_whole(w) for w in (output_weight, up_weight, down_turned)]
        total_valid = lax.psum(jnp.sum(validity).astype(F32), AXES)
    first_scale = lax.rsqrt(jnp.mean(states * states, axis=-1, keepdims=True) + EPSILON)
    normed = (states * first_scale * first_gain).astype(BF16)
    pms = premix.T * (HEAD_DIM**-0.5)
    pos = postmix
    pm = jnp.repeat(pms, HEAD_DIM, axis=1)[:, None]
    po = jnp.repeat(pos, HEAD_DIM, axis=1)[:, None]
    queries, keys, values, attended, probs = attend(spot, picture_start, normed, qkv, pm, po)
    if blocked:
        *sides, attended = lax.optimization_barrier((*sides, attended))
        *halves, line, side_x, side_y = lax.optimization_barrier(
            (sides[0][:2], sides[1][2:], line, *sides)
        )
        rest = [line, side_x, side_y, *gather_halves(*halves, total)]
        rest += [exchange(part, CORE_BIT, total) for part in rest]
    layer_out, mid_grad, attended_grad, sums, *grads = middle_block(
        blocked,
        spot,
        total_valid.reshape(1, 1),
        seq_len * total,
        rest,
        attended,
        states,
        upstream,
        teacher,
        validity[:, None],
        second_gain[None],
        units,
    )
    nt = normed.T
    if blocked:
        ffn_mine = grads[0], exchange(grads[1], CORE_BIT, total)
        *first, attended_grad = lax.optimization_barrier((*reduce_core(ffn_mine), attended_grad))
        ffn_first = reduce_first(*first, total)
    else:
        up_grad, down_grad, output_grad = (scatter_whole(g) for g in grads)
        down_grad = down_grad.T
    dq, dk, dv, mix, *grads = attend_back(
        spot, blocked, nt, queries, keys, values, attended_grad, probs, pm, po, pms, pos
    )
    if blocked:
        *ffn_first, dq, dk, dv, mix, keep, send = lax.optimization_barrier(
            (*ffn_first, dq, dk, dv, mix, *grads)
        )
        other = exchange(send, CORE_BIT, total)
        ffn_sides = reduce_second(*reduce_sides(ffn_mine, *ffn_first), total)
        mine = keep, other
        *first, dq, dk, dv = lax.optimization_barrier((*reduce_core(mine), dq, dk, dv))
        first = reduce_first(*first, total)
        input_grad, small = input_block(
            spot, qkv, dq, dk, dv, states, mid_grad, first_gain[None], sums, mix
        )
        *ffn_sides, small = lax.optimization_barrier((*ffn_sides, small))
        ffn_line = reduce_line(*reduce_own(ffn_mine, *ffn_first), *ffn_sides)
        small += exchange(small, CORE_BIT, total)
        near = lax.reduce_precision(small, 8, 7)
        small = jnp.broadcast_to(jnp.concatenate([near, small - near]), (4, depth, 128))
        ffn_line = jnp.concatenate([ffn_line, small], axis=2)
        blocks = [ffn_line[m].astype(BF16) for m in (1, 2, 3)]
        ffn_far = [exchange(block, m * Z_BIT, total) for m, block in enumerate(blocks, 1)]
        *first, _, _, _ = lax.optimization_barrier((*first, *blocks))
        sides = reduce_sides(mine, *first)
        sides = reduce_second(*sides, total)
        ffn = add_low(ffn_line[0], *ffn_far) + late(sides[0], 2)
        ffn = with_layout_constraint(ffn, Layout((0, 1)))
        head, tail, ffn = lax.optimization_barrier((*reduce_own(mine, *first), ffn))
        line = reduce_line(head, tail, *sides)
        total_valid = sums[3, 0] + late(line, 0)
        attn = add_low(line[0], *reduce_far(line, total))
        half = units // col_total
        up_grad, output_grad, down_grad, small = jnp.split(
            ffn, [half, half + width, 2 * half + width], axis=1
        )
        small = small[: depth // 2] + small[depth // 2 :] + late(line, 2)
        for bit in (X_BIT, Y_BIT):
            small += exchange(small, bit, total)
        down_grad = down_grad.T
        query_grad, key_grad, value_grad = (attn[n * depth : (n + 1) * depth] for n in range(3))
    else:
        query_grad, key_grad, value_grad = (scatter_whole(g) for g in grads)
        input_grad, small = input_block(
            spot, qkv, dq, dk, dv, states, mid_grad, first_gain[None], sums, mix
        )
        small = lax.psum(small, AXES)
        total_valid = sums[3, 0]
    parts = features // 128
    first_grad = small[:parts].reshape(-1)
    second_grad = small[parts : 2 * parts].reshape(-1)
    small = small[2 * parts :]
    premix_grad = small[:, :HEADS] * (HEAD_DIM**-0.5)
    postmix_grad = small[:, 16 : 16 + HEADS]
    losses = small[0, 32:34]
    return (
        layer_out,
        losses[0] / (total_valid * features),
        losses[1] / total_valid,
        input_grad,
        first_grad,
        query_grad,
        key_grad,
        value_grad,
        premix_grad,
        postmix_grad,
        output_grad,
        second_grad,
        up_grad,
        down_grad,
    )


def solution(mesh):
    tokens, block = P(AXES, None), P("row", "col")
    return jax.shard_map(
        shards,
        mesh=mesh,
        in_specs=(
            tokens, tokens, tokens, P(AXES), tokens, P(), block, block, block, P(), P(), block,
            P(), block, P("col", "row"),
        ),
        out_specs=(
            tokens, P(), P(), tokens, P(), block, block, block, P(), P(), block, P(), block,
            P("col", "row"),
        ),
        check_vma=False,
    )
```

```python
import functools

import jax
import jax.numpy as jnp
from jax import lax
from jax.experimental import pallas as pl
from jax.experimental.layout import Layout, with_layout_constraint
from jax.experimental.pallas import tpu as pltpu
from jax.sharding import PartitionSpec as P

HEADS = 12
HEAD_DIM = 64
PIC = 256
EPSILON = 1e-06
F32 = jnp.float32
BF16 = jnp.bfloat16
AXES = ("row", "col")
X_BIT, CORE_BIT, Y_BIT, Z_BIT = 1, 2, 4, 8
LINES = [[at + Z_BIT // 2 * z for z in range(4)] for at in range(4)]
EXTRA = 128
PIECES = ((0, 0, 0), (0, 1, 0), (1, 0, 0), (1, 1, 0), (1, 1, 2))
PARAMS = pltpu.CompilerParams(vmem_limit_bytes=60000 * 1024)
SMEM = pl.BlockSpec(memory_space=pltpu.SMEM)
ANY = pl.BlockSpec(memory_space=pl.ANY)
VMEM = pl.BlockSpec(memory_space=pltpu.VMEM)


def dot(a, b):
    return lax.dot_general(a, b, (((1,), (0,)), ((), ())), preferred_element_type=F32)


def dot_nt(a, b):
    return lax.dot_general(a, b, (((1,), (1,)), ((), ())), preferred_element_type=F32)


def cost(micros):
    return pl.CostEstimate(flops=micros * 10**9, bytes_accessed=10**6, transcendentals=0)


def placed(pieces):
    if len(pieces) == 4:
        pieces = [p.at[n] for p, size in zip(pieces, (3, 2, 3, 2)) for n in range(size)]
    for n, piece in enumerate(pieces):
        y, x, first = PIECES[n % len(PIECES)]
        for z in range(piece.shape[0]):
            yield piece, (z,), n // len(PIECES), y, x, first + z


def place_copies(spot, pieces, wholes, rows_at, cols_at, widths, sems, near=False):
    if len(pieces) == len(wholes):
        return [
            pltpu.make_async_copy(piece, whole, sems.at[n])
            for n, (piece, whole) in enumerate(zip(pieces, wholes))
        ]
    copies = []
    for piece, index, core, y, x, z in placed(pieces):
        r = ((spot[0] ^ z if near else z) * 2 + (spot[1] ^ y)) * 2 + (spot[2] ^ core)
        c = spot[3] ^ x
        for whole, row, col, width in zip(wholes, rows_at, cols_at, widths):
            depth = whole.shape[0] // 16
            copies.append(
                pltpu.make_async_copy(
                    piece.at[(*index, pl.ds(row, depth), pl.ds(col, width))],
                    whole.at[
                        pl.ds(pl.multiple_of(r * depth, 16), depth),
                        pl.ds(pl.multiple_of(c * width, 128), width),
                    ],
                    sems.at[len(copies)],
                )
            )
    return copies


def send_copies(spot, source, keep, send, row, half, col, width, sems, near=False):
    depth = source.shape[0] // 16
    copies = []
    for j in range(8):
        z, y = j // 2, j % 2
        plane = (spot[1] ^ y) * 2 + (spot[3] ^ half)
        for n, (target, core) in enumerate(((keep, spot[2]), (send, 1 - spot[2]))):
            start = pl.multiple_of((2 * j + core) * depth, 16)
            copies.append(
                pltpu.make_async_copy(
                    source.at[pl.ds(start, depth), pl.ds(0, width)],
                    target.at[plane, spot[0] ^ z if near else z, pl.ds(row, depth), pl.ds(col, width)],
                    sems.at[2 * j + n],
                )
            )
    return copies


def attend_kernel(blocks, spot, starts, normed_ref, *rest):
    pieces, rest = rest[:blocks], rest[blocks:]
    pm_ref, po_ref, q_ref, k_ref, v_ref, out_ref, p_ref, wq, wk, wv, kt, bias, acc, sems = rest
    step = pl.program_id(0)
    half = normed_ref.shape[0] // 2

    @pl.when(step == 0)
    def _():
        width = wq.shape[1] // 2
        depth = wq.shape[0] // 16
        copies = place_copies(
            spot, pieces, (wq, wk, wv), (0, depth, 2 * depth), (0, 0, 0), (width,) * 3, sems, True
        )
        for copy in copies:
            copy.start()
        rows = lax.broadcasted_iota(jnp.int32, (half, half), 0)
        cols = lax.broadcasted_iota(jnp.int32, (half, half), 1)
        for b in range(2):
            i, j = rows + b * half, cols + b * half
            ok = j <= i
            for s in range(2):
                p = starts[0, s]
                ok = ok | ((i >= p) & (i < p + PIC) & (j >= p) & (j < p + PIC))
            bias[b] = jnp.where(ok, 0.0, -1e30)
        acc[...] = jnp.zeros_like(acc)
        for copy in copies:
            copy.wait()
        k_ref[...] = dot(normed_ref[...], wk[...]).astype(BF16)
        kt[...] = k_ref[...].T
        q_ref[...] = dot(normed_ref[...], wq[...]).astype(BF16)
        v_ref[...] = dot(normed_ref[...], wv[...]).astype(BF16)

    pm = pm_ref[0]
    po = po_ref[0]
    vs = (v_ref[...].astype(F32) * po).astype(BF16)
    top = (q_ref[:half].astype(F32) * pm).astype(BF16)
    low = (q_ref[half:].astype(F32) * pm).astype(BF16)
    s0 = dot(top, kt[:, :half]) + bias[0]
    s1 = dot(low, kt[:, :half])
    s2 = dot(low, kt[:, half:]) + bias[1]
    m0 = jnp.max(s0, axis=1, keepdims=True)
    e0 = jnp.exp(s0 - m0)
    p0 = (e0 / jnp.sum(e0, axis=1, keepdims=True)).astype(BF16)
    m1 = jnp.maximum(jnp.max(s1, axis=1, keepdims=True), jnp.max(s2, axis=1, keepdims=True))
    e1 = jnp.exp(s1 - m1)
    e2 = jnp.exp(s2 - m1)
    inv = 1.0 / (jnp.sum(e1, axis=1, keepdims=True) + jnp.sum(e2, axis=1, keepdims=True))
    p1 = (e1 * inv).astype(BF16)
    p2 = (e2 * inv).astype(BF16)
    p_ref[0, :, :half] = p0
    p_ref[0, :, half : 2 * half] = p1
    p_ref[0, :, 2 * half :] = p2
    acc[:half] += dot(p0, vs[:half])
    acc[half:] += dot(p1, vs[:half]) + dot(p2, vs[half:])

    @pl.when(step == HEADS - 1)
    def _():
        out_ref[...] = acc[...].astype(BF16)


def attend(spot, starts, normed, pieces, pm, po):
    seq, width = normed.shape
    half = seq // 2
    whole = pl.BlockSpec((seq, width), lambda h: (0, 0))
    row = pl.BlockSpec((1, 1, width), lambda h: (h, 0, 0))
    low = jax.ShapeDtypeStruct((seq, width), BF16)
    return pl.pallas_call(
        functools.partial(attend_kernel, len(pieces)),
        grid=(HEADS,),
        in_specs=[SMEM, SMEM, whole] + [ANY] * len(pieces) + [row, row],
        out_specs=[whole] * 4 + [pl.BlockSpec((1, half, 3 * half), lambda h: (h, 0, 0))],
        out_shape=[low] * 4 + [jax.ShapeDtypeStruct((HEADS, half, 3 * half), BF16)],
        scratch_shapes=[pltpu.VMEM((width, width), BF16)] * 3
        + [
            pltpu.VMEM((width, seq), BF16),
            pltpu.VMEM((2, half, half), F32),
            pltpu.VMEM((seq, width), F32),
            pltpu.SemaphoreType.DMA((96,)),
        ],
        compiler_params=PARAMS,
        name="attend",
        cost_estimate=cost(20),
    )(spot, starts, normed, *pieces, pm, po)


def middle_kernel(blocks, outs, tokens, spot, count, *rest):
    pieces, rest = rest[:blocks], rest[blocks:]
    sources, valid_ref, gain_ref = rest[:4], rest[4], rest[5]
    layer_ref, mid_ref, agrad_ref, sums_ref = rest[6:10]
    grads, rest = rest[10 : 10 + outs], rest[10 + outs :]
    wo, wu, wd, hidden, pre, n2t, olt, slots, marks, sems, out_sems, mark_sems, *rest = rest
    att_ref, states_ref, up_ref, teach_ref, in_sems = rest
    seq, width = att_ref.shape
    units = wu.shape[1]
    blocked = outs == 2
    mark_copies = []
    if blocked:
        for n, (piece, index, *_) in enumerate(placed(pieces)):
            mark_copies.append(
                pltpu.make_async_copy(
                    piece.at[(*index, pl.ds(0, 16), pl.ds((units + width) // 2, EXTRA))],
                    marks.at[n],
                    mark_sems.at[n],
                )
            )
    copies = place_copies(
        spot,
        pieces,
        (wo, wu, wd),
        (0, 0, 0),
        (units // 2, 0, (units + width) // 2 + EXTRA),
        (width // 2, units // 2, units // 2),
        sems,
    )
    loads = [
        pltpu.make_async_copy(source, target, in_sems.at[n])
        for n, (source, target) in enumerate(zip(sources, (att_ref, states_ref, up_ref, teach_ref)))
    ]
    early = mark_copies + loads[:1] + copies[::3] + loads[1:2]
    for copy in early + copies[1::3] + copies[2::3] + loads[2:]:
        copy.start()
    for copy in mark_copies:
        copy.wait()
    total_valid = jnp.full((1, 1), count[0, 0], F32)
    if blocked:
        by_lane = jnp.sum(marks[...].astype(F32), axis=0)[:1]
        total_valid += jnp.sum(by_lane, axis=1, keepdims=True)
    factor = tokens / total_valid
    sums_ref[...] = jnp.broadcast_to(total_valid, sums_ref.shape)
    for copy in loads[:1] + copies[::3] + loads[1:2]:
        copy.wait()
    mid_ref[...] = states_ref[...] + dot(att_ref[...], wo[...])
    middle = mid_ref[...]
    scale = lax.rsqrt(jnp.mean(middle * middle, axis=1, keepdims=True) + EPSILON)
    n2 = (middle * scale * gain_ref[...]).astype(BF16)
    n2t[...] = n2.T
    for copy in copies[1::3]:
        copy.wait()

    chunk = 512
    steps = units // chunk

    def up_step(j, _):
        at = pl.ds(pl.multiple_of(j * chunk, chunk), chunk)
        hidden[:, at] = jnp.maximum(dot(n2, wu[:, at]), 0.0).astype(BF16)
        return 0

    lax.fori_loop(0, steps, up_step, 0)
    for copy in copies[2::3] + loads[2:]:
        copy.wait()
    layer_ref[...] = mid_ref[...] + dot_nt(hidden[...], wd[...])
    layer = layer_ref[...]
    valid = valid_ref[...].astype(F32)
    upstream = up_ref[...]
    differ = layer - teach_ref[...]
    sums_ref[1:2, :] = jnp.sum(valid * (differ * differ), axis=0, keepdims=True)
    sums_ref[2:3, :] = jnp.sum(valid * (upstream * layer), axis=0, keepdims=True)
    out_grad = (factor * valid) * (upstream + differ)
    out_low = out_grad.astype(BF16)
    olt[...] = out_low.T

    def down_step(j, _):
        at = pl.ds(pl.multiple_of(j * chunk, chunk), chunk)
        part = hidden[:, at]
        back = jnp.where(part > 0, dot(out_low, wd[:, at]), 0.0).astype(BF16)
        pre[:, at] = back
        for which, (left, right) in enumerate(((n2t, back), (olt, part))):
            slot = slots.at[which]

            @pl.when(j > 0)
            def _():
                for copy in grad_copies(which, j - 1):
                    copy.wait()

            slot[...] = dot(left[...], right).astype(BF16)
            for copy in grad_copies(which, j):
                copy.start()
        return 0

    def grad_copies(which, j):
        if not blocked:
            at = pl.ds(pl.multiple_of(j * chunk, chunk), chunk)
            return [pltpu.make_async_copy(slots.at[which], grads[which].at[:, at], out_sems.at[which, 0])]
        per = steps // 2
        return send_copies(
            spot,
            slots.at[which],
            grads[0],
            grads[1],
            0,
            j // per,
            pl.multiple_of(which * ((units + width) // 2) + (j % per) * chunk, 128),
            chunk,
            out_sems.at[which],
            True,
        )

    lax.fori_loop(0, steps, down_step, 0)
    grad = dot_nt(pre[...], wu[...])
    middle = mid_ref[...]
    scale = lax.rsqrt(jnp.mean(middle * middle, axis=1, keepdims=True) + EPSILON)
    sums_ref[0:1, :] = jnp.sum(grad * middle * scale, axis=0, keepdims=True)
    term = gain_ref[...] * grad
    inner = jnp.mean(term * middle, axis=1, keepdims=True)
    layer = layer_ref[...]
    out_grad = (factor * valid_ref[...].astype(F32)) * (
        up_ref[...] + (layer - teach_ref[...])
    )
    mid_grad = out_grad + scale * term - middle * (scale * scale * scale) * inner
    mid_ref[...] = mid_grad
    branch = mid_grad.astype(BF16)
    agrad_ref[...] = dot_nt(branch, wo[...]).astype(BF16)
    n2t[...] = att_ref[...].T
    for which in range(2):
        for copy in grad_copies(which, steps - 1):
            copy.wait()
    half = width // 2
    last = []
    for c in range(2):
        slots[c, :, :half] = dot(n2t[...], branch[:, c * half : (c + 1) * half]).astype(BF16)
        if blocked:
            made = send_copies(
                spot, slots.at[c], grads[0], grads[1], 0, c, units // 2, half, out_sems.at[c], True
            )
        else:
            made = [
                pltpu.make_async_copy(
                    slots.at[c, :, pl.ds(0, half)],
                    grads[2].at[:, pl.ds(c * half, half)],
                    out_sems.at[c, 0],
                )
            ]
        for copy in made:
            copy.start()
        last += made
    for copy in last:
        copy.wait()


def middle_block(blocked, spot, count, tokens, pieces, attended, states, upstream, teacher, valid, gain, units):
    seq, width = attended.shape
    full = jax.ShapeDtypeStruct((seq, width), F32)
    if blocked:
        depth = width // 16
        grads = [jax.ShapeDtypeStruct((4, 4, depth, units + width // 2), BF16)] * 2
    else:
        grads = [
            jax.ShapeDtypeStruct((width, units), BF16),
            jax.ShapeDtypeStruct((width, units), BF16),
            jax.ShapeDtypeStruct((width, width), BF16),
        ]
    return pl.pallas_call(
        functools.partial(middle_kernel, len(pieces), len(grads), tokens),
        in_specs=[SMEM, SMEM] + [ANY] * (len(pieces) + 4) + [VMEM] * 2,
        out_specs=[VMEM] * 4 + [ANY] * len(grads),
        out_shape=[
            full,
            full,
            jax.ShapeDtypeStruct((seq, width), BF16),
            jax.ShapeDtypeStruct((8, width), F32),
        ]
        + grads,
        scratch_shapes=[
            pltpu.VMEM((width, width), BF16),
            pltpu.VMEM((width, units), BF16),
            pltpu.VMEM((width, units), BF16),
            pltpu.VMEM((seq, units), BF16),
            pltpu.VMEM((seq, units), BF16),
            pltpu.VMEM((width, seq), BF16),
            pltpu.VMEM((width, seq), BF16),
            pltpu.VMEM((2, width, 512), BF16),
            pltpu.VMEM((32, 16, EXTRA), BF16),
            pltpu.SemaphoreType.DMA((96,)),
            pltpu.SemaphoreType.DMA((2, 16)),
            pltpu.SemaphoreType.DMA((32,)),
            pltpu.VMEM((seq, width), BF16),
            pltpu.VMEM((seq, width), F32),
            pltpu.VMEM((seq, width), F32),
            pltpu.VMEM((seq, width), F32),
            pltpu.SemaphoreType.DMA((4,)),
        ],
        compiler_params=PARAMS,
        name="middle",
        cost_estimate=cost(35),
    )(spot, count, *pieces, attended, states, upstream, teacher, valid, gain)


def attend_back_kernel(
    blocked, spot, pms, pos, nt_ref, q_ref, k_ref, v_ref, g_ref, p_ref, pm_ref, po_ref,
    dq_ref, dk_ref, dv_ref, mix_ref, *rest,
):
    outs = 2 if blocked else 3
    grads = rest[:outs]
    vt, qt, gt, dq, dkt, dvt, pre, slots, sems = rest[outs:]
    step = pl.program_id(0)
    seq, width = q_ref.shape
    half = seq // 2

    @pl.when(step == 0)
    def _():
        vt[...] = v_ref[...].T
        qt[...] = q_ref[...].T
        gt[...] = g_ref[...].T
        dq[...] = jnp.zeros_like(dq)
        dkt[...] = jnp.zeros_like(dkt)
        dvt[...] = jnp.zeros_like(dvt)
        pre[...] = jnp.zeros_like(pre)
        mix_ref[...] = jnp.zeros_like(mix_ref)

    pm = pm_ref[0]
    po = po_ref[0]
    p0, p1, p2 = (p_ref[0, :, b * half : (b + 1) * half] for b in range(3))
    top = (g_ref[:half].astype(F32) * po).astype(BF16)
    low = (g_ref[half:].astype(F32) * po).astype(BF16)
    g0 = dot(top, vt[:, :half])
    g1 = dot(low, vt[:, :half])
    g2 = dot(low, vt[:, half:])
    u0 = dot(gt[:, :half], p0) + dot(gt[:, half:], p1)
    u1 = dot(gt[:, half:], p2)
    f0, f1, f2 = p0.astype(F32), p1.astype(F32), p2.astype(F32)
    t0 = f0 * g0
    d0 = (t0 - f0 * jnp.sum(t0, axis=1, keepdims=True)).astype(BF16)
    t1, t2 = f1 * g1, f2 * g2
    r1 = jnp.sum(t1, axis=1, keepdims=True) + jnp.sum(t2, axis=1, keepdims=True)
    d1 = (t1 - f1 * r1).astype(BF16)
    d2 = (t2 - f2 * r1).astype(BF16)
    w0 = dot(d0, k_ref[:half])
    w1 = dot(d1, k_ref[:half]) + dot(d2, k_ref[half:])
    dq[:half] += pm * w0
    dq[half:] += pm * w1
    row = jnp.sum(q_ref[:half].astype(F32) * w0, axis=0, keepdims=True) + jnp.sum(
        q_ref[half:].astype(F32) * w1, axis=0, keepdims=True
    )
    pre[...] += jnp.where(lax.broadcasted_iota(jnp.int32, pre.shape, 0) == step, row, 0.0)
    lane = lax.broadcasted_iota(jnp.int32, (1, 128), 1)
    posts = jnp.zeros((1, 128), F32)
    for g in range(HEADS):
        at = slice(g * HEAD_DIM, (g + 1) * HEAD_DIM)
        b = pos[step, g]
        u0g, u1g = u0[at], u1[at]
        dvt[at, :half] += b * u0g
        dvt[at, half:] += b * u1g
        both = u0g * vt[at, :half].astype(F32) + u1g * vt[at, half:].astype(F32)
        post = jnp.sum(jnp.sum(both, axis=0, keepdims=True), axis=1, keepdims=True)
        posts += jnp.where(lane == 16 + g, post, 0.0)
    mix_ref[...] += jnp.where(
        lax.broadcasted_iota(jnp.int32, mix_ref.shape, 0) == step, posts, 0.0
    )
    qs = jnp.concatenate(
        [
            (qt[g * HEAD_DIM : (g + 1) * HEAD_DIM].astype(F32) * pms[step, g]).astype(BF16)
            for g in range(HEADS)
        ],
        axis=0,
    )
    dkt[:, :half] += dot(qs[:, :half], d0) + dot(qs[:, half:], d1)
    dkt[:, half:] += dot(qs[:, half:], d2)

    @pl.when(step == HEADS - 1)
    def _():
        feature = lax.broadcasted_iota(jnp.int32, (width, 128), 0)
        head = lax.broadcasted_iota(jnp.int32, (width, 128), 1)
        member = (feature >= head * HEAD_DIM) & (feature < (head + 1) * HEAD_DIM)
        turned = lax.dot_general(
            member.astype(F32),
            pre[...],
            (((0,), (1,)), ((), ())),
            precision=lax.Precision.HIGHEST,
            preferred_element_type=F32,
        )
        mix_ref[:, :16] += turned[:16]
        dq_ref[...] = dq[...].astype(BF16)
        dk_ref[...] = dkt[...].astype(BF16).T
        dv_ref[...] = dvt[...].astype(BF16).T
        made = []
        for n, ref in enumerate((dq_ref, dk_ref, dv_ref)):
            slots[n] = dot(nt_ref[...], ref[...]).astype(BF16)
            if blocked:
                part = width // 2
                for c in range(2):
                    made += send_copies(
                        spot,
                        slots.at[n, :, pl.ds(c * part, part)],
                        grads[0],
                        grads[1],
                        n * (width // 16),
                        c,
                        0,
                        part,
                        sems.at[2 * n + c],
                        True,
                    )
            else:
                made.append(pltpu.make_async_copy(slots.at[n], grads[n], sems.at[n, 0]))
            for copy in made[-32 if blocked else -1 :]:
                copy.start()
        for copy in made:
            copy.wait()


def attend_back(spot, blocked, nt, q, k, v, g, p, pm, po, pms, pos):
    seq, width = q.shape
    half = seq // 2
    whole = pl.BlockSpec((seq, width), lambda h: (0, 0))
    row = pl.BlockSpec((1, 1, width), lambda h: (h, 0, 0))
    low = jax.ShapeDtypeStruct((seq, width), BF16)
    if blocked:
        grads = [jax.ShapeDtypeStruct((4, 4, 3 * (width // 16), width // 2), BF16)] * 2
    else:
        grads = [jax.ShapeDtypeStruct((width, width), BF16)] * 3
    return pl.pallas_call(
        functools.partial(attend_back_kernel, blocked),
        grid=(HEADS,),
        in_specs=[SMEM, SMEM, SMEM, pl.BlockSpec((width, seq), lambda h: (0, 0))]
        + [whole] * 4
        + [pl.BlockSpec((1, half, 3 * half), lambda h: (h, 0, 0)), row, row],
        out_specs=[whole] * 3
        + [pl.BlockSpec((16, 128), lambda h: (0, 0))]
        + [ANY] * len(grads),
        out_shape=[low] * 3
        + [jax.ShapeDtypeStruct((16, 128), F32)]
        + grads,
        scratch_shapes=[pltpu.VMEM((width, seq), BF16)] * 3
        + [
            pltpu.VMEM((seq, width), F32),
            pltpu.VMEM((width, seq), F32),
            pltpu.VMEM((width, seq), F32),
            pltpu.VMEM((16, width), F32),
            pltpu.VMEM((3, width, width), BF16),
            pltpu.SemaphoreType.DMA((6, 16)),
        ],
        compiler_params=PARAMS,
        name="attend_back",
        cost_estimate=cost(28),
    )(spot, pms, pos, nt, q, k, v, g, p, pm, po)


def input_kernel(blocks, spot, *rest):
    pieces, rest = rest[:blocks], rest[blocks:]
    dq_ref, dk_ref, dv_ref, states_ref, mid_ref, gain_ref, sums_ref, mix_ref = rest[:8]
    out_ref, small_ref, wq, wk, wv, sems = rest[8:]
    features = wq.shape[1]
    width = features // 2
    depth = wq.shape[0] // 16
    copies = place_copies(
        spot, pieces, (wq, wk, wv), (0, depth, 2 * depth), (0, 0, 0), (width,) * 3, sems, True
    )
    for copy in copies:
        copy.start()
    states = states_ref[...]
    scale = lax.rsqrt(jnp.mean(states * states, axis=1, keepdims=True) + EPSILON)
    for copy in copies:
        copy.wait()
    grad = (
        dot_nt(dq_ref[...], wq[...]) + dot_nt(dk_ref[...], wk[...]) + dot_nt(dv_ref[...], wv[...])
    )
    first = jnp.sum(grad * states * scale, axis=0, keepdims=True)
    parts = features // 128
    lane = lax.broadcasted_iota(jnp.int32, (1, 128), 1)
    losses = [jnp.sum(sums_ref[n : n + 1], axis=1, keepdims=True) for n in (1, 2)]
    for n in range(parts):
        at = slice(n * 128, (n + 1) * 128)
        small_ref[n : n + 1] = first[:, at]
        small_ref[parts + n : parts + n + 1] = sums_ref[:1, at]
    small_ref[2 * parts :] = mix_ref[:HEADS]
    small_ref[2 * parts : 2 * parts + 1] += jnp.where(
        lane == 32, losses[0], jnp.where(lane == 33, losses[1], 0.0)
    )
    term = gain_ref[...] * grad
    inner = jnp.mean(term * states, axis=1, keepdims=True)
    out_ref[...] = mid_ref[...] + scale * term - states * (scale * scale * scale) * inner


def input_block(spot, pieces, dq, dk, dv, states, mid_grad, gain, sums, mix):
    seq, width = dq.shape
    return pl.pallas_call(
        functools.partial(input_kernel, len(pieces)),
        in_specs=[SMEM] + [ANY] * len(pieces) + [VMEM] * 8,
        out_specs=[VMEM] * 2,
        out_shape=[
            jax.ShapeDtypeStruct((seq, width), F32),
            jax.ShapeDtypeStruct((2 * width // 128 + HEADS, 128), F32),
        ],
        scratch_shapes=[pltpu.VMEM((width, width), BF16)] * 3 + [pltpu.SemaphoreType.DMA((96,))],
        compiler_params=PARAMS,
        name="input_grad",
        cost_estimate=cost(9),
    )(spot, *pieces, dq, dk, dv, states, mid_grad, gain, sums, mix)


def exchange(value, mask, total):
    return lax.ppermute(value, AXES, [(i, i ^ mask) for i in range(total)])


def after(value, *others):
    return lax.optimization_barrier((value, *others))[0]


def over_lines(blocks):
    return lax.all_to_all(blocks, "row", 0, 0, axis_index_groups=LINES, tiled=True)


def late(value, rank):
    return 0.0 * value[(0,) * (value.ndim - rank)][(slice(1),) * rank].astype(F32)


def gather_line(packet):
    return over_lines(jnp.broadcast_to(packet, (4, *packet.shape)))


def gather_near(packet, total):
    return [packet, *[exchange(packet, m * Z_BIT, total) for m in (1, 2, 3)]]


def gather_sides(line, total):
    return exchange(line, X_BIT, total), exchange(line, Y_BIT, total)


def gather_halves(over_x, over_y, total):
    return exchange(over_x, Y_BIT, total), exchange(over_y, X_BIT, total)


def add_low(*terms):
    return functools.reduce(jnp.add, [t.astype(F32) for t in terms])


def core_sum(terms, *index):
    return add_low(*[term[index] for term in terms])


def reduce_core(terms):
    low, high = slice(0, 2), slice(2, 4)
    planes = slice(2, 4), slice(1, 4, 2)
    return [core_sum(terms, p, z).astype(BF16) for p, z in zip(planes, (low, high))]


def reduce_first(over_y, over_x, total):
    return exchange(over_y, Y_BIT, total), exchange(over_x, X_BIT, total)


def reduce_sides(terms, over_y, over_x):
    return [
        (core_sum(terms, plane, z) + over[1]).astype(BF16)
        for plane, z, over in ((1, slice(0, 2), over_y), (2, slice(2, 4), over_x))
    ]


def reduce_second(side_x, side_y, total):
    return exchange(side_x, X_BIT, total), exchange(side_y, Y_BIT, total)


def reduce_own(terms, over_y, over_x):
    return [
        core_sum(terms, 0, z) + over[0]
        for z, over in ((slice(0, 2), over_y), (slice(2, 4), over_x))
    ]


def reduce_line(head, tail, side_x, side_y):
    return jnp.concatenate([add_low(head, side_x), add_low(tail, side_y)])


def reduce_far(line, total):
    return [exchange(line[m].astype(BF16), m * Z_BIT, total) for m in (1, 2, 3)]


def gather_whole(block):
    rows, cols = lax.axis_size("row"), lax.axis_size("col")
    depth, width = block.shape
    every = lax.all_gather(block[None], AXES, axis=0, tiled=True)
    every = every.reshape(rows, cols, depth, width).transpose(0, 2, 1, 3)
    return every.reshape(rows * depth, cols * width)


def scatter_whole(grad):
    rows, cols = lax.axis_size("row"), lax.axis_size("col")
    depth, width = grad.shape[0] // rows, grad.shape[1] // cols
    parts = grad.reshape(rows, depth, cols, width).transpose(0, 2, 1, 3)
    parts = parts.reshape(rows * cols, depth, width).astype(F32)
    return lax.psum_scatter(parts, AXES, scatter_dimension=0, tiled=True)[0]


def shards(
    states,
    upstream,
    teacher,
    validity,
    picture_start,
    first_gain,
    query_weight,
    key_weight,
    value_weight,
    premix,
    postmix,
    output_weight,
    second_gain,
    up_weight,
    down_weight,
):
    row_total = lax.axis_size("row")
    col_total = lax.axis_size("col")
    total = row_total * col_total
    seq_len, features = states.shape
    depth, width = query_weight.shape
    units = up_weight.shape[1] * col_total
    blocked = (row_total, col_total) == (16, 2)
    row = lax.axis_index("row")
    spot = jnp.stack([row // 4, (row // 2) % 2, row % 2, lax.axis_index("col")]).astype(jnp.int32)
    down_turned = down_weight.T
    if blocked:
        packet = jnp.concatenate([query_weight, key_weight, value_weight], axis=0)
        qkv_near = gather_near(packet, total)
        qkv_line = jnp.stack(qkv_near)
        qkv_sides = gather_sides(qkv_line, total)
        marks = jnp.sum(validity.reshape(-1, EXTRA), axis=0).astype(F32)
        marks = jnp.broadcast_to(marks, (depth, EXTRA)).astype(BF16)
        packet = jnp.concatenate(
            [up_weight, output_weight, marks, down_turned], axis=1
        )
        line = gather_line(packet)
        *halves, qkv_line, side_x, side_y = lax.optimization_barrier(
            (qkv_sides[0][:2], qkv_sides[1][2:], qkv_line, *qkv_sides)
        )
        qkv = [jnp.stack([qkv_line, side_x, side_y]), jnp.stack(gather_halves(*halves, total))]
        qkv += [exchange(part, CORE_BIT, total) for part in qkv]
        line, *qkv = lax.optimization_barrier((line, *qkv))
        sides = gather_sides(line, total)
        total_valid = jnp.zeros((), F32)
    else:
        qkv = [gather_whole(w) for w in (query_weight, key_weight, value_weight)]
        rest = [gather_whole(w) for w in (output_weight, up_weight, down_turned)]
        total_valid = lax.psum(jnp.sum(validity).astype(F32), AXES)
    first_scale = lax.rsqrt(jnp.mean(states * states, axis=-1, keepdims=True) + EPSILON)
    normed = (states * first_scale * first_gain).astype(BF16)
    pms = premix.T * (HEAD_DIM**-0.5)
    pos = postmix
    pm = jnp.repeat(pms, HEAD_DIM, axis=1)[:, None]
    po = jnp.repeat(pos, HEAD_DIM, axis=1)[:, None]
    queries, keys, values, attended, probs = attend(spot, picture_start, normed, qkv, pm, po)
    if blocked:
        *sides, attended = lax.optimization_barrier((*sides, attended))
        *halves, line, side_x, side_y = lax.optimization_barrier(
            (sides[0][:2], sides[1][2:], line, *sides)
        )
        rest = [line, side_x, side_y, *gather_halves(*halves, total)]
        rest += [exchange(part, CORE_BIT, total) for part in rest]
    layer_out, mid_grad, attended_grad, sums, *grads = middle_block(
        blocked,
        spot,
        total_valid.reshape(1, 1),
        seq_len * total,
        rest,
        attended,
        states,
        upstream,
        teacher,
        validity[:, None],
        second_gain[None],
        units,
    )
    nt = normed.T
    if blocked:
        ffn_mine = grads[0], exchange(grads[1], CORE_BIT, total)
        *first, attended_grad = lax.optimization_barrier((*reduce_core(ffn_mine), attended_grad))
        ffn_first = reduce_first(*first, total)
    else:
        up_grad, down_grad, output_grad = (scatter_whole(g) for g in grads)
        down_grad = down_grad.T
    dq, dk, dv, mix, *grads = attend_back(
        spot, blocked, nt, queries, keys, values, attended_grad, probs, pm, po, pms, pos
    )
    if blocked:
        *ffn_first, dq, dk, dv, mix, keep, send = lax.optimization_barrier(
            (*ffn_first, dq, dk, dv, mix, *grads)
        )
        other = exchange(send, CORE_BIT, total)
        half = units // col_total
        ahead = half + width
        ffn_sides = reduce_sides(ffn_mine, *ffn_first)
        down_sides = reduce_second(*[side[..., ahead:] for side in ffn_sides], total)
        ffn_sides = reduce_second(*[side[..., :ahead] for side in ffn_sides], total)
        mine = keep, other
        *first, dq, dk, dv = lax.optimization_barrier((*reduce_core(mine), dq, dk, dv))
        first = reduce_first(*first, total)
        input_grad, small = input_block(
            spot, qkv, dq, dk, dv, states, mid_grad, first_gain[None], sums, mix
        )
        *down_sides, small, input_grad = lax.optimization_barrier((*down_sides, small, input_grad))
        own = reduce_own(ffn_mine, *ffn_first)
        down_line = reduce_line(*[o[..., ahead:] for o in own], *down_sides)
        down = reduce_far(down_line, total)
        *ffn_sides, small, tie = lax.optimization_barrier((*ffn_sides, small, down_line[:1, :1, :1]))
        ffn_line = reduce_line(*[o[..., :ahead] for o in own], *ffn_sides) + late(tie, 3)
        small += exchange(small, CORE_BIT, total)
        near = lax.reduce_precision(small, 8, 7)
        small = jnp.broadcast_to(jnp.concatenate([near, small - near]), (4, depth, 128))
        ffn_line = jnp.concatenate([ffn_line, small], axis=2)
        blocks = [ffn_line[m].astype(BF16) for m in (1, 2, 3)]
        ffn_far = [exchange(block, m * Z_BIT, total) for m, block in enumerate(blocks, 1)]
        *first, _, _, _ = lax.optimization_barrier((*first, *blocks))
        sides = reduce_sides(mine, *first)
        sides = reduce_second(*sides, total)
        ffn = add_low(ffn_line[0], *ffn_far) + late(sides[0], 2)
        ffn = with_layout_constraint(ffn, Layout((0, 1)))
        head, tail, ffn = lax.optimization_barrier((*reduce_own(mine, *first), ffn))
        line = reduce_line(head, tail, *sides)
        total_valid = sums[3, 0] + late(line, 0)
        attn = add_low(line[0], *reduce_far(line, total))
        up_grad, output_grad, small = jnp.split(ffn, [half, ahead], axis=1)
        down_grad = add_low(down_line[0], *down)
        small = small[: depth // 2] + small[depth // 2 :] + late(line, 2)
        for bit in (X_BIT, Y_BIT):
            small += exchange(small, bit, total)
        down_grad = down_grad.T
        query_grad, key_grad, value_grad = (attn[n * depth : (n + 1) * depth] for n in range(3))
    else:
        query_grad, key_grad, value_grad = (scatter_whole(g) for g in grads)
        input_grad, small = input_block(
            spot, qkv, dq, dk, dv, states, mid_grad, first_gain[None], sums, mix
        )
        small = lax.psum(small, AXES)
        total_valid = sums[3, 0]
    parts = features // 128
    first_grad = small[:parts].reshape(-1)
    second_grad = small[parts : 2 * parts].reshape(-1)
    small = small[2 * parts :]
    premix_grad = small[:, :HEADS] * (HEAD_DIM**-0.5)
    postmix_grad = small[:, 16 : 16 + HEADS]
    losses = small[0, 32:34]
    return (
        layer_out,
        losses[0] / (total_valid * features),
        losses[1] / total_valid,
        input_grad,
        first_grad,
        query_grad,
        key_grad,
        value_grad,
        premix_grad,
        postmix_grad,
        output_grad,
        second_grad,
        up_grad,
        down_grad,
    )


def solution(mesh):
    tokens, block = P(AXES, None), P("row", "col")
    return jax.shard_map(
        shards,
        mesh=mesh,
        in_specs=(
            tokens, tokens, tokens, P(AXES), tokens, P(), block, block, block, P(), P(), block,
            P(), block, P("col", "row"),
        ),
        out_specs=(
            tokens, P(), P(), tokens, P(), block, block, block, P(), P(), block, P(), block,
            P("col", "row"),
        ),
        check_vma=False,
    )
```

```python
import functools

import jax
import jax.numpy as jnp
from jax import lax
from jax.experimental import pallas as pl
from jax.experimental.layout import Layout, with_layout_constraint
from jax.experimental.pallas import tpu as pltpu
from jax.sharding import PartitionSpec as P

HEADS = 12
HEAD_DIM = 64
PIC = 256
EPSILON = 1e-06
F32 = jnp.float32
BF16 = jnp.bfloat16
AXES = ("row", "col")
X_BIT, CORE_BIT, Y_BIT, Z_BIT = 1, 2, 4, 8
LINES = [[at + Z_BIT // 2 * z for z in range(4)] for at in range(4)]
EXTRA = 128
PIECES = ((0, 0, 0), (0, 1, 0), (1, 0, 0), (1, 1, 0), (1, 1, 2))
PARAMS = pltpu.CompilerParams(vmem_limit_bytes=60000 * 1024)
SMEM = pl.BlockSpec(memory_space=pltpu.SMEM)
ANY = pl.BlockSpec(memory_space=pl.ANY)
VMEM = pl.BlockSpec(memory_space=pltpu.VMEM)


def dot(a, b):
    return lax.dot_general(a, b, (((1,), (0,)), ((), ())), preferred_element_type=F32)


def dot_nt(a, b):
    return lax.dot_general(a, b, (((1,), (1,)), ((), ())), preferred_element_type=F32)


def cost(micros):
    return pl.CostEstimate(flops=micros * 10**9, bytes_accessed=10**6, transcendentals=0)


def placed(pieces):
    if len(pieces) == 4:
        pieces = [p.at[n] for p, size in zip(pieces, (3, 2, 3, 2)) for n in range(size)]
    for n, piece in enumerate(pieces):
        y, x, first = PIECES[n % len(PIECES)]
        for z in range(piece.shape[0]):
            yield piece, (z,), n // len(PIECES), y, x, first + z


def place_copies(spot, pieces, wholes, rows_at, cols_at, widths, sems, near=False):
    if len(pieces) == len(wholes):
        return [
            pltpu.make_async_copy(piece, whole, sems.at[n])
            for n, (piece, whole) in enumerate(zip(pieces, wholes))
        ]
    copies = []
    for piece, index, core, y, x, z in placed(pieces):
        r = ((spot[0] ^ z if near else z) * 2 + (spot[1] ^ y)) * 2 + (spot[2] ^ core)
        c = spot[3] ^ x
        for whole, row, col, width in zip(wholes, rows_at, cols_at, widths):
            depth = whole.shape[0] // 16
            copies.append(
                pltpu.make_async_copy(
                    piece.at[(*index, pl.ds(row, depth), pl.ds(col, width))],
                    whole.at[
                        pl.ds(pl.multiple_of(r * depth, 16), depth),
                        pl.ds(pl.multiple_of(c * width, 128), width),
                    ],
                    sems.at[len(copies)],
                )
            )
    return copies


def send_copies(spot, source, keep, send, row, half, col, width, sems, near=False):
    depth = source.shape[0] // 16
    copies = []
    for j in range(8):
        z, y = j // 2, j % 2
        plane = (spot[1] ^ y) * 2 + (spot[3] ^ half)
        for n, (target, core) in enumerate(((keep, spot[2]), (send, 1 - spot[2]))):
            start = pl.multiple_of((2 * j + core) * depth, 16)
            copies.append(
                pltpu.make_async_copy(
                    source.at[pl.ds(start, depth), pl.ds(0, width)],
                    target.at[plane, spot[0] ^ z if near else z, pl.ds(row, depth), pl.ds(col, width)],
                    sems.at[2 * j + n],
                )
            )
    return copies


def attend_kernel(blocks, spot, starts, normed_ref, *rest):
    pieces, rest = rest[:blocks], rest[blocks:]
    pm_ref, po_ref, q_ref, k_ref, v_ref, out_ref, p_ref, wq, wk, wv, kt, bias, acc, sems = rest
    step = pl.program_id(0)
    half = normed_ref.shape[0] // 2

    @pl.when(step == 0)
    def _():
        width = wq.shape[1] // 2
        depth = wq.shape[0] // 16
        copies = place_copies(
            spot, pieces, (wq, wk, wv), (0, depth, 2 * depth), (0, 0, 0), (width,) * 3, sems, True
        )
        for copy in copies:
            copy.start()
        rows = lax.broadcasted_iota(jnp.int32, (half, half), 0)
        cols = lax.broadcasted_iota(jnp.int32, (half, half), 1)
        for b in range(2):
            i, j = rows + b * half, cols + b * half
            ok = j <= i
            for s in range(2):
                p = starts[0, s]
                ok = ok | ((i >= p) & (i < p + PIC) & (j >= p) & (j < p + PIC))
            bias[b] = jnp.where(ok, 0.0, -1e30)
        acc[...] = jnp.zeros_like(acc)
        for copy in copies:
            copy.wait()
        k_ref[...] = dot(normed_ref[...], wk[...]).astype(BF16)
        kt[...] = k_ref[...].T
        q_ref[...] = dot(normed_ref[...], wq[...]).astype(BF16)
        v_ref[...] = dot(normed_ref[...], wv[...]).astype(BF16)

    pm = pm_ref[0]
    po = po_ref[0]
    vs = (v_ref[...].astype(F32) * po).astype(BF16)
    top = (q_ref[:half].astype(F32) * pm).astype(BF16)
    low = (q_ref[half:].astype(F32) * pm).astype(BF16)
    s0 = dot(top, kt[:, :half]) + bias[0]
    s1 = dot(low, kt[:, :half])
    s2 = dot(low, kt[:, half:]) + bias[1]
    m0 = jnp.max(s0, axis=1, keepdims=True)
    e0 = jnp.exp(s0 - m0)
    p0 = (e0 / jnp.sum(e0, axis=1, keepdims=True)).astype(BF16)
    m1 = jnp.maximum(jnp.max(s1, axis=1, keepdims=True), jnp.max(s2, axis=1, keepdims=True))
    e1 = jnp.exp(s1 - m1)
    e2 = jnp.exp(s2 - m1)
    inv = 1.0 / (jnp.sum(e1, axis=1, keepdims=True) + jnp.sum(e2, axis=1, keepdims=True))
    p1 = (e1 * inv).astype(BF16)
    p2 = (e2 * inv).astype(BF16)
    p_ref[0, :, :half] = p0
    p_ref[0, :, half : 2 * half] = p1
    p_ref[0, :, 2 * half :] = p2
    acc[:half] += dot(p0, vs[:half])
    acc[half:] += dot(p1, vs[:half]) + dot(p2, vs[half:])

    @pl.when(step == HEADS - 1)
    def _():
        out_ref[...] = acc[...].astype(BF16)


def attend(spot, starts, normed, pieces, pm, po):
    seq, width = normed.shape
    half = seq // 2
    whole = pl.BlockSpec((seq, width), lambda h: (0, 0))
    row = pl.BlockSpec((1, 1, width), lambda h: (h, 0, 0))
    low = jax.ShapeDtypeStruct((seq, width), BF16)
    return pl.pallas_call(
        functools.partial(attend_kernel, len(pieces)),
        grid=(HEADS,),
        in_specs=[SMEM, SMEM, whole] + [ANY] * len(pieces) + [row, row],
        out_specs=[whole] * 4 + [pl.BlockSpec((1, half, 3 * half), lambda h: (h, 0, 0))],
        out_shape=[low] * 4 + [jax.ShapeDtypeStruct((HEADS, half, 3 * half), BF16)],
        scratch_shapes=[pltpu.VMEM((width, width), BF16)] * 3
        + [
            pltpu.VMEM((width, seq), BF16),
            pltpu.VMEM((2, half, half), F32),
            pltpu.VMEM((seq, width), F32),
            pltpu.SemaphoreType.DMA((96,)),
        ],
        compiler_params=PARAMS,
        name="attend",
        cost_estimate=cost(20),
    )(spot, starts, normed, *pieces, pm, po)


def middle_kernel(blocks, outs, tokens, spot, count, *rest):
    pieces, rest = rest[:blocks], rest[blocks:]
    sources, valid_ref, gain_ref = rest[:4], rest[4], rest[5]
    layer_ref, mid_ref, agrad_ref, sums_ref = rest[6:10]
    grads, rest = rest[10 : 10 + outs], rest[10 + outs :]
    wo, wu, wd, hidden, pre, n2t, olt, slots, marks, sems, out_sems, mark_sems, *rest = rest
    att_ref, states_ref, up_ref, teach_ref, in_sems = rest
    seq, width = att_ref.shape
    units = wu.shape[1]
    blocked = outs == 2
    mark_copies = []
    if blocked:
        for n, (piece, index, *_) in enumerate(placed(pieces)):
            mark_copies.append(
                pltpu.make_async_copy(
                    piece.at[(*index, pl.ds(0, 16), pl.ds((units + width) // 2, EXTRA))],
                    marks.at[n],
                    mark_sems.at[n],
                )
            )
    copies = place_copies(
        spot,
        pieces,
        (wo, wu, wd),
        (0, 0, 0),
        (units // 2, 0, (units + width) // 2 + EXTRA),
        (width // 2, units // 2, units // 2),
        sems,
    )
    loads = [
        pltpu.make_async_copy(source, target, in_sems.at[n])
        for n, (source, target) in enumerate(zip(sources, (att_ref, states_ref, up_ref, teach_ref)))
    ]
    early = mark_copies + loads[:1] + copies[::3] + loads[1:2]
    for copy in early + copies[1::3] + copies[2::3] + loads[2:]:
        copy.start()
    for copy in mark_copies:
        copy.wait()
    total_valid = jnp.full((1, 1), count[0, 0], F32)
    if blocked:
        by_lane = jnp.sum(marks[...].astype(F32), axis=0)[:1]
        total_valid += jnp.sum(by_lane, axis=1, keepdims=True)
    factor = tokens / total_valid
    sums_ref[...] = jnp.broadcast_to(total_valid, sums_ref.shape)
    for copy in loads[:1] + copies[::3] + loads[1:2]:
        copy.wait()
    mid_ref[...] = states_ref[...] + dot(att_ref[...], wo[...])
    middle = mid_ref[...]
    scale = lax.rsqrt(jnp.mean(middle * middle, axis=1, keepdims=True) + EPSILON)
    n2 = (middle * scale * gain_ref[...]).astype(BF16)
    n2t[...] = n2.T
    for copy in copies[1::3]:
        copy.wait()

    chunk = 512
    steps = units // chunk

    def up_step(j, _):
        at = pl.ds(pl.multiple_of(j * chunk, chunk), chunk)
        hidden[:, at] = jnp.maximum(dot(n2, wu[:, at]), 0.0).astype(BF16)
        return 0

    lax.fori_loop(0, steps, up_step, 0)
    for copy in copies[2::3] + loads[2:]:
        copy.wait()
    layer_ref[...] = mid_ref[...] + dot_nt(hidden[...], wd[...])
    layer = layer_ref[...]
    valid = valid_ref[...].astype(F32)
    upstream = up_ref[...]
    differ = layer - teach_ref[...]
    sums_ref[1:2, :] = jnp.sum(valid * (differ * differ), axis=0, keepdims=True)
    sums_ref[2:3, :] = jnp.sum(valid * (upstream * layer), axis=0, keepdims=True)
    out_grad = (factor * valid) * (upstream + differ)
    out_low = out_grad.astype(BF16)
    olt[...] = out_low.T

    def down_step(j, _):
        at = pl.ds(pl.multiple_of(j * chunk, chunk), chunk)
        part = hidden[:, at]
        back = jnp.where(part > 0, dot(out_low, wd[:, at]), 0.0).astype(BF16)
        pre[:, at] = back
        for which, (left, right) in enumerate(((n2t, back), (olt, part))):
            slot = slots.at[which]

            @pl.when(j > 0)
            def _():
                for copy in grad_copies(which, j - 1):
                    copy.wait()

            slot[...] = dot(left[...], right).astype(BF16)
            for copy in grad_copies(which, j):
                copy.start()
        return 0

    def grad_copies(which, j):
        if not blocked:
            at = pl.ds(pl.multiple_of(j * chunk, chunk), chunk)
            return [pltpu.make_async_copy(slots.at[which], grads[which].at[:, at], out_sems.at[which, 0])]
        per = steps // 2
        return send_copies(
            spot,
            slots.at[which],
            grads[0],
            grads[1],
            0,
            j // per,
            pl.multiple_of(which * ((units + width) // 2) + (j % per) * chunk, 128),
            chunk,
            out_sems.at[which],
            True,
        )

    lax.fori_loop(0, steps, down_step, 0)
    grad = dot_nt(pre[...], wu[...])
    middle = mid_ref[...]
    scale = lax.rsqrt(jnp.mean(middle * middle, axis=1, keepdims=True) + EPSILON)
    sums_ref[0:1, :] = jnp.sum(grad * middle * scale, axis=0, keepdims=True)
    term = gain_ref[...] * grad
    inner = jnp.mean(term * middle, axis=1, keepdims=True)
    layer = layer_ref[...]
    out_grad = (factor * valid_ref[...].astype(F32)) * (
        up_ref[...] + (layer - teach_ref[...])
    )
    mid_grad = out_grad + scale * term - middle * (scale * scale * scale) * inner
    mid_ref[...] = mid_grad
    branch = mid_grad.astype(BF16)
    agrad_ref[...] = dot_nt(branch, wo[...]).astype(BF16)
    n2t[...] = att_ref[...].T
    for which in range(2):
        for copy in grad_copies(which, steps - 1):
            copy.wait()
    half = width // 2
    last = []
    for c in range(2):
        slots[c, :, :half] = dot(n2t[...], branch[:, c * half : (c + 1) * half]).astype(BF16)
        if blocked:
            made = send_copies(
                spot, slots.at[c], grads[0], grads[1], 0, c, units // 2, half, out_sems.at[c], True
            )
        else:
            made = [
                pltpu.make_async_copy(
                    slots.at[c, :, pl.ds(0, half)],
                    grads[2].at[:, pl.ds(c * half, half)],
                    out_sems.at[c, 0],
                )
            ]
        for copy in made:
            copy.start()
        last += made
    for copy in last:
        copy.wait()


def middle_block(blocked, spot, count, tokens, pieces, attended, states, upstream, teacher, valid, gain, units):
    seq, width = attended.shape
    full = jax.ShapeDtypeStruct((seq, width), F32)
    if blocked:
        depth = width // 16
        grads = [jax.ShapeDtypeStruct((4, 4, depth, units + width // 2), BF16)] * 2
    else:
        grads = [
            jax.ShapeDtypeStruct((width, units), BF16),
            jax.ShapeDtypeStruct((width, units), BF16),
            jax.ShapeDtypeStruct((width, width), BF16),
        ]
    return pl.pallas_call(
        functools.partial(middle_kernel, len(pieces), len(grads), tokens),
        in_specs=[SMEM, SMEM] + [ANY] * (len(pieces) + 4) + [VMEM] * 2,
        out_specs=[VMEM] * 4 + [ANY] * len(grads),
        out_shape=[
            full,
            full,
            jax.ShapeDtypeStruct((seq, width), BF16),
            jax.ShapeDtypeStruct((8, width), F32),
        ]
        + grads,
        scratch_shapes=[
            pltpu.VMEM((width, width), BF16),
            pltpu.VMEM((width, units), BF16),
            pltpu.VMEM((width, units), BF16),
            pltpu.VMEM((seq, units), BF16),
            pltpu.VMEM((seq, units), BF16),
            pltpu.VMEM((width, seq), BF16),
            pltpu.VMEM((width, seq), BF16),
            pltpu.VMEM((2, width, 512), BF16),
            pltpu.VMEM((32, 16, EXTRA), BF16),
            pltpu.SemaphoreType.DMA((96,)),
            pltpu.SemaphoreType.DMA((2, 16)),
            pltpu.SemaphoreType.DMA((32,)),
            pltpu.VMEM((seq, width), BF16),
            pltpu.VMEM((seq, width), F32),
            pltpu.VMEM((seq, width), F32),
            pltpu.VMEM((seq, width), F32),
            pltpu.SemaphoreType.DMA((4,)),
        ],
        compiler_params=PARAMS,
        name="middle",
        cost_estimate=cost(35),
    )(spot, count, *pieces, attended, states, upstream, teacher, valid, gain)


def attend_back_kernel(
    blocked, spot, pms, pos, nt_ref, q_ref, k_ref, v_ref, g_ref, p_ref, pm_ref, po_ref,
    dq_ref, dk_ref, dv_ref, mix_ref, *rest,
):
    outs = 2 if blocked else 3
    grads = rest[:outs]
    vt, qt, gt, dq, dkt, dvt, pre, slots, sems = rest[outs:]
    step = pl.program_id(0)
    seq, width = q_ref.shape
    half = seq // 2

    @pl.when(step == 0)
    def _():
        vt[...] = v_ref[...].T
        qt[...] = q_ref[...].T
        gt[...] = g_ref[...].T
        dq[...] = jnp.zeros_like(dq)
        dkt[...] = jnp.zeros_like(dkt)
        dvt[...] = jnp.zeros_like(dvt)
        pre[...] = jnp.zeros_like(pre)
        mix_ref[...] = jnp.zeros_like(mix_ref)

    pm = pm_ref[0]
    po = po_ref[0]
    p0, p1, p2 = (p_ref[0, :, b * half : (b + 1) * half] for b in range(3))
    top = (g_ref[:half].astype(F32) * po).astype(BF16)
    low = (g_ref[half:].astype(F32) * po).astype(BF16)
    g0 = dot(top, vt[:, :half])
    g1 = dot(low, vt[:, :half])
    g2 = dot(low, vt[:, half:])
    u0 = dot(gt[:, :half], p0) + dot(gt[:, half:], p1)
    u1 = dot(gt[:, half:], p2)
    f0, f1, f2 = p0.astype(F32), p1.astype(F32), p2.astype(F32)
    t0 = f0 * g0
    d0 = (t0 - f0 * jnp.sum(t0, axis=1, keepdims=True)).astype(BF16)
    t1, t2 = f1 * g1, f2 * g2
    r1 = jnp.sum(t1, axis=1, keepdims=True) + jnp.sum(t2, axis=1, keepdims=True)
    d1 = (t1 - f1 * r1).astype(BF16)
    d2 = (t2 - f2 * r1).astype(BF16)
    w0 = dot(d0, k_ref[:half])
    w1 = dot(d1, k_ref[:half]) + dot(d2, k_ref[half:])
    dq[:half] += pm * w0
    dq[half:] += pm * w1
    row = jnp.sum(q_ref[:half].astype(F32) * w0, axis=0, keepdims=True) + jnp.sum(
        q_ref[half:].astype(F32) * w1, axis=0, keepdims=True
    )
    pre[...] += jnp.where(lax.broadcasted_iota(jnp.int32, pre.shape, 0) == step, row, 0.0)
    lane = lax.broadcasted_iota(jnp.int32, (1, 128), 1)
    posts = jnp.zeros((1, 128), F32)
    for g in range(HEADS):
        at = slice(g * HEAD_DIM, (g + 1) * HEAD_DIM)
        b = pos[step, g]
        u0g, u1g = u0[at], u1[at]
        dvt[at, :half] += b * u0g
        dvt[at, half:] += b * u1g
        both = u0g * vt[at, :half].astype(F32) + u1g * vt[at, half:].astype(F32)
        post = jnp.sum(jnp.sum(both, axis=0, keepdims=True), axis=1, keepdims=True)
        posts += jnp.where(lane == 16 + g, post, 0.0)
    mix_ref[...] += jnp.where(
        lax.broadcasted_iota(jnp.int32, mix_ref.shape, 0) == step, posts, 0.0
    )
    qs = jnp.concatenate(
        [
            (qt[g * HEAD_DIM : (g + 1) * HEAD_DIM].astype(F32) * pms[step, g]).astype(BF16)
            for g in range(HEADS)
        ],
        axis=0,
    )
    dkt[:, :half] += dot(qs[:, :half], d0) + dot(qs[:, half:], d1)
    dkt[:, half:] += dot(qs[:, half:], d2)

    @pl.when(step == HEADS - 1)
    def _():
        feature = lax.broadcasted_iota(jnp.int32, (width, 128), 0)
        head = lax.broadcasted_iota(jnp.int32, (width, 128), 1)
        member = (feature >= head * HEAD_DIM) & (feature < (head + 1) * HEAD_DIM)
        turned = lax.dot_general(
            member.astype(F32),
            pre[...],
            (((0,), (1,)), ((), ())),
            precision=lax.Precision.HIGHEST,
            preferred_element_type=F32,
        )
        mix_ref[:, :16] += turned[:16]
        dq_ref[...] = dq[...].astype(BF16)
        dk_ref[...] = dkt[...].astype(BF16).T
        dv_ref[...] = dvt[...].astype(BF16).T
        made = []
        for n, ref in enumerate((dq_ref, dk_ref, dv_ref)):
            slots[n] = dot(nt_ref[...], ref[...]).astype(BF16)
            if blocked:
                part = width // 2
                for c in range(2):
                    made += send_copies(
                        spot,
                        slots.at[n, :, pl.ds(c * part, part)],
                        grads[0],
                        grads[1],
                        n * (width // 16),
                        c,
                        0,
                        part,
                        sems.at[2 * n + c],
                        True,
                    )
            else:
                made.append(pltpu.make_async_copy(slots.at[n], grads[n], sems.at[n, 0]))
            for copy in made[-32 if blocked else -1 :]:
                copy.start()
        for copy in made:
            copy.wait()


def attend_back(spot, blocked, nt, q, k, v, g, p, pm, po, pms, pos):
    seq, width = q.shape
    half = seq // 2
    whole = pl.BlockSpec((seq, width), lambda h: (0, 0))
    row = pl.BlockSpec((1, 1, width), lambda h: (h, 0, 0))
    low = jax.ShapeDtypeStruct((seq, width), BF16)
    if blocked:
        grads = [jax.ShapeDtypeStruct((4, 4, 3 * (width // 16), width // 2), BF16)] * 2
    else:
        grads = [jax.ShapeDtypeStruct((width, width), BF16)] * 3
    return pl.pallas_call(
        functools.partial(attend_back_kernel, blocked),
        grid=(HEADS,),
        in_specs=[SMEM, SMEM, SMEM, pl.BlockSpec((width, seq), lambda h: (0, 0))]
        + [whole] * 4
        + [pl.BlockSpec((1, half, 3 * half), lambda h: (h, 0, 0)), row, row],
        out_specs=[whole] * 3
        + [pl.BlockSpec((16, 128), lambda h: (0, 0))]
        + [ANY] * len(grads),
        out_shape=[low] * 3
        + [jax.ShapeDtypeStruct((16, 128), F32)]
        + grads,
        scratch_shapes=[pltpu.VMEM((width, seq), BF16)] * 3
        + [
            pltpu.VMEM((seq, width), F32),
            pltpu.VMEM((width, seq), F32),
            pltpu.VMEM((width, seq), F32),
            pltpu.VMEM((16, width), F32),
            pltpu.VMEM((3, width, width), BF16),
            pltpu.SemaphoreType.DMA((6, 16)),
        ],
        compiler_params=PARAMS,
        name="attend_back",
        cost_estimate=cost(28),
    )(spot, pms, pos, nt, q, k, v, g, p, pm, po)


def input_kernel(blocks, spot, *rest):
    pieces, rest = rest[:blocks], rest[blocks:]
    dq_ref, dk_ref, dv_ref, states_ref, mid_ref, gain_ref, sums_ref, mix_ref = rest[:8]
    out_ref, small_ref, wq, wk, wv, sems = rest[8:]
    features = wq.shape[1]
    width = features // 2
    depth = wq.shape[0] // 16
    copies = place_copies(
        spot, pieces, (wq, wk, wv), (0, depth, 2 * depth), (0, 0, 0), (width,) * 3, sems, True
    )
    for copy in copies:
        copy.start()
    states = states_ref[...]
    scale = lax.rsqrt(jnp.mean(states * states, axis=1, keepdims=True) + EPSILON)
    for copy in copies:
        copy.wait()
    grad = (
        dot_nt(dq_ref[...], wq[...]) + dot_nt(dk_ref[...], wk[...]) + dot_nt(dv_ref[...], wv[...])
    )
    first = jnp.sum(grad * states * scale, axis=0, keepdims=True)
    parts = features // 128
    lane = lax.broadcasted_iota(jnp.int32, (1, 128), 1)
    losses = [jnp.sum(sums_ref[n : n + 1], axis=1, keepdims=True) for n in (1, 2)]
    for n in range(parts):
        at = slice(n * 128, (n + 1) * 128)
        small_ref[n : n + 1] = first[:, at]
        small_ref[parts + n : parts + n + 1] = sums_ref[:1, at]
    small_ref[2 * parts :] = mix_ref[:HEADS]
    small_ref[2 * parts : 2 * parts + 1] += jnp.where(
        lane == 32, losses[0], jnp.where(lane == 33, losses[1], 0.0)
    )
    term = gain_ref[...] * grad
    inner = jnp.mean(term * states, axis=1, keepdims=True)
    out_ref[...] = mid_ref[...] + scale * term - states * (scale * scale * scale) * inner


def input_block(spot, pieces, dq, dk, dv, states, mid_grad, gain, sums, mix):
    seq, width = dq.shape
    return pl.pallas_call(
        functools.partial(input_kernel, len(pieces)),
        in_specs=[SMEM] + [ANY] * len(pieces) + [VMEM] * 8,
        out_specs=[VMEM] * 2,
        out_shape=[
            jax.ShapeDtypeStruct((seq, width), F32),
            jax.ShapeDtypeStruct((2 * width // 128 + HEADS, 128), F32),
        ],
        scratch_shapes=[pltpu.VMEM((width, width), BF16)] * 3 + [pltpu.SemaphoreType.DMA((96,))],
        compiler_params=PARAMS,
        name="input_grad",
        cost_estimate=cost(9),
    )(spot, *pieces, dq, dk, dv, states, mid_grad, gain, sums, mix)


def exchange(value, mask, total):
    return lax.ppermute(value, AXES, [(i, i ^ mask) for i in range(total)])


def after(value, *others):
    return lax.optimization_barrier((value, *others))[0]


def over_lines(blocks):
    return lax.all_to_all(blocks, "row", 0, 0, axis_index_groups=LINES, tiled=True)


def late(value, rank):
    return 0.0 * value[(0,) * (value.ndim - rank)][(slice(1),) * rank].astype(F32)


def gather_line(packet):
    return over_lines(jnp.broadcast_to(packet, (4, *packet.shape)))


def gather_near(packet, total):
    return [packet, *[exchange(packet, m * Z_BIT, total) for m in (1, 2, 3)]]


def gather_sides(line, total):
    return exchange(line, X_BIT, total), exchange(line, Y_BIT, total)


def gather_halves(over_x, over_y, total):
    return exchange(over_x, Y_BIT, total), exchange(over_y, X_BIT, total)


def add_low(*terms):
    return functools.reduce(jnp.add, [t.astype(F32) for t in terms])


def core_sum(terms, *index):
    return add_low(*[term[index] for term in terms])


def reduce_core(terms):
    low, high = slice(0, 2), slice(2, 4)
    planes = slice(2, 4), slice(1, 4, 2)
    return [core_sum(terms, p, z).astype(BF16) for p, z in zip(planes, (low, high))]


def reduce_first(over_y, over_x, total):
    return exchange(over_y, Y_BIT, total), exchange(over_x, X_BIT, total)


def reduce_sides(terms, over_y, over_x, cols=slice(None)):
    every = slice(None)
    return [
        (core_sum(terms, plane, z, every, cols) + over[1, :, :, cols]).astype(BF16)
        for plane, z, over in ((1, slice(0, 2), over_y), (2, slice(2, 4), over_x))
    ]


def reduce_second(side_x, side_y, total):
    return exchange(side_x, X_BIT, total), exchange(side_y, Y_BIT, total)


def reduce_own(terms, over_y, over_x):
    return [
        core_sum(terms, 0, z) + over[0]
        for z, over in ((slice(0, 2), over_y), (slice(2, 4), over_x))
    ]


def reduce_line(head, tail, side_x, side_y):
    return jnp.concatenate([add_low(head, side_x), add_low(tail, side_y)])


def reduce_far(line, total):
    return [exchange(line[m].astype(BF16), m * Z_BIT, total) for m in (1, 2, 3)]


def gather_whole(block):
    rows, cols = lax.axis_size("row"), lax.axis_size("col")
    depth, width = block.shape
    every = lax.all_gather(block[None], AXES, axis=0, tiled=True)
    every = every.reshape(rows, cols, depth, width).transpose(0, 2, 1, 3)
    return every.reshape(rows * depth, cols * width)


def scatter_whole(grad):
    rows, cols = lax.axis_size("row"), lax.axis_size("col")
    depth, width = grad.shape[0] // rows, grad.shape[1] // cols
    parts = grad.reshape(rows, depth, cols, width).transpose(0, 2, 1, 3)
    parts = parts.reshape(rows * cols, depth, width).astype(F32)
    return lax.psum_scatter(parts, AXES, scatter_dimension=0, tiled=True)[0]


def shards(
    states,
    upstream,
    teacher,
    validity,
    picture_start,
    first_gain,
    query_weight,
    key_weight,
    value_weight,
    premix,
    postmix,
    output_weight,
    second_gain,
    up_weight,
    down_weight,
):
    row_total = lax.axis_size("row")
    col_total = lax.axis_size("col")
    total = row_total * col_total
    seq_len, features = states.shape
    depth, width = query_weight.shape
    units = up_weight.shape[1] * col_total
    blocked = (row_total, col_total) == (16, 2)
    row = lax.axis_index("row")
    spot = jnp.stack([row // 4, (row // 2) % 2, row % 2, lax.axis_index("col")]).astype(jnp.int32)
    down_turned = down_weight.T
    if blocked:
        packet = jnp.concatenate([query_weight, key_weight, value_weight], axis=0)
        qkv_near = gather_near(packet, total)
        qkv_line = jnp.stack(qkv_near)
        qkv_sides = gather_sides(qkv_line, total)
        marks = jnp.sum(validity.reshape(-1, EXTRA), axis=0).astype(F32)
        marks = jnp.broadcast_to(marks, (depth, EXTRA)).astype(BF16)
        packet = jnp.concatenate(
            [up_weight, output_weight, marks, down_turned], axis=1
        )
        line = gather_line(packet)
        *halves, qkv_line, side_x, side_y = lax.optimization_barrier(
            (qkv_sides[0][:2], qkv_sides[1][2:], qkv_line, *qkv_sides)
        )
        qkv = [jnp.stack([qkv_line, side_x, side_y]), jnp.stack(gather_halves(*halves, total))]
        qkv += [exchange(part, CORE_BIT, total) for part in qkv]
        line, *qkv = lax.optimization_barrier((line, *qkv))
        sides = gather_sides(line, total)
        total_valid = jnp.zeros((), F32)
    else:
        qkv = [gather_whole(w) for w in (query_weight, key_weight, value_weight)]
        rest = [gather_whole(w) for w in (output_weight, up_weight, down_turned)]
        total_valid = lax.psum(jnp.sum(validity).astype(F32), AXES)
    first_scale = lax.rsqrt(jnp.mean(states * states, axis=-1, keepdims=True) + EPSILON)
    normed = (states * first_scale * first_gain).astype(BF16)
    pms = premix.T * (HEAD_DIM**-0.5)
    pos = postmix
    pm = jnp.repeat(pms, HEAD_DIM, axis=1)[:, None]
    po = jnp.repeat(pos, HEAD_DIM, axis=1)[:, None]
    queries, keys, values, attended, probs = attend(spot, picture_start, normed, qkv, pm, po)
    if blocked:
        *sides, attended = lax.optimization_barrier((*sides, attended))
        *halves, line, side_x, side_y = lax.optimization_barrier(
            (sides[0][:2], sides[1][2:], line, *sides)
        )
        rest = [line, side_x, side_y, *gather_halves(*halves, total)]
        rest += [exchange(part, CORE_BIT, total) for part in rest]
    layer_out, mid_grad, attended_grad, sums, *grads = middle_block(
        blocked,
        spot,
        total_valid.reshape(1, 1),
        seq_len * total,
        rest,
        attended,
        states,
        upstream,
        teacher,
        validity[:, None],
        second_gain[None],
        units,
    )
    nt = normed.T
    if blocked:
        ffn_mine = grads[0], exchange(grads[1], CORE_BIT, total)
        *first, attended_grad = lax.optimization_barrier((*reduce_core(ffn_mine), attended_grad))
        ffn_first = reduce_first(*first, total)
    else:
        up_grad, down_grad, output_grad = (scatter_whole(g) for g in grads)
        down_grad = down_grad.T
    dq, dk, dv, mix, *grads = attend_back(
        spot, blocked, nt, queries, keys, values, attended_grad, probs, pm, po, pms, pos
    )
    if blocked:
        *ffn_first, dq, dk, dv, mix, keep, send = lax.optimization_barrier(
            (*ffn_first, dq, dk, dv, mix, *grads)
        )
        other = exchange(send, CORE_BIT, total)
        half = units // col_total
        ahead = half + width
        down_sides = reduce_sides(ffn_mine, *ffn_first, slice(ahead, None))
        ffn_sides = reduce_sides(ffn_mine, *ffn_first, slice(ahead))
        down_sides = reduce_second(*down_sides, total)
        ffn_sides = reduce_second(*ffn_sides, total)
        mine = keep, other
        *first, dq, dk, dv = lax.optimization_barrier((*reduce_core(mine), dq, dk, dv))
        first = reduce_first(*first, total)
        input_grad, small = input_block(
            spot, qkv, dq, dk, dv, states, mid_grad, first_gain[None], sums, mix
        )
        *down_sides, small, input_grad = lax.optimization_barrier((*down_sides, small, input_grad))
        own = reduce_own(ffn_mine, *ffn_first)
        down_line = reduce_line(*[o[..., ahead:] for o in own], *down_sides)
        down = reduce_far(down_line, total)
        *ffn_sides, small, tie = lax.optimization_barrier((*ffn_sides, small, down_line[:1, :1, :1]))
        ffn_line = reduce_line(*[o[..., :ahead] for o in own], *ffn_sides) + late(tie, 3)
        small += exchange(small, CORE_BIT, total)
        near = lax.reduce_precision(small, 8, 7)
        small = jnp.broadcast_to(jnp.concatenate([near, small - near]), (4, depth, 128))
        ffn_line = jnp.concatenate([ffn_line, small], axis=2)
        blocks = [ffn_line[m].astype(BF16) for m in (1, 2, 3)]
        ffn_far = [exchange(block, m * Z_BIT, total) for m, block in enumerate(blocks, 1)]
        *first, _, _, _ = lax.optimization_barrier((*first, *blocks))
        sides = reduce_sides(mine, *first)
        sides = reduce_second(*sides, total)
        ffn = add_low(ffn_line[0], *ffn_far) + late(sides[0], 2)
        ffn = with_layout_constraint(ffn, Layout((0, 1)))
        head, tail, ffn = lax.optimization_barrier((*reduce_own(mine, *first), ffn))
        line = reduce_line(head, tail, *sides)
        total_valid = sums[3, 0] + late(line, 0)
        attn = add_low(line[0], *reduce_far(line, total))
        up_grad, output_grad, small = jnp.split(ffn, [half, ahead], axis=1)
        down_grad = add_low(down_line[0], *down)
        small = small[: depth // 2] + small[depth // 2 :] + late(line, 2)
        for bit in (X_BIT, Y_BIT):
            small += exchange(small, bit, total)
        down_grad = down_grad.T
        query_grad, key_grad, value_grad = (attn[n * depth : (n + 1) * depth] for n in range(3))
    else:
        query_grad, key_grad, value_grad = (scatter_whole(g) for g in grads)
        input_grad, small = input_block(
            spot, qkv, dq, dk, dv, states, mid_grad, first_gain[None], sums, mix
        )
        small = lax.psum(small, AXES)
        total_valid = sums[3, 0]
    parts = features // 128
    first_grad = small[:parts].reshape(-1)
    second_grad = small[parts : 2 * parts].reshape(-1)
    small = small[2 * parts :]
    premix_grad = small[:, :HEADS] * (HEAD_DIM**-0.5)
    postmix_grad = small[:, 16 : 16 + HEADS]
    losses = small[0, 32:34]
    return (
        layer_out,
        losses[0] / (total_valid * features),
        losses[1] / total_valid,
        input_grad,
        first_grad,
        query_grad,
        key_grad,
        value_grad,
        premix_grad,
        postmix_grad,
        output_grad,
        second_grad,
        up_grad,
        down_grad,
    )


def solution(mesh):
    tokens, block = P(AXES, None), P("row", "col")
    return jax.shard_map(
        shards,
        mesh=mesh,
        in_specs=(
            tokens, tokens, tokens, P(AXES), tokens, P(), block, block, block, P(), P(), block,
            P(), block, P("col", "row"),
        ),
        out_specs=(
            tokens, P(), P(), tokens, P(), block, block, block, P(), P(), block, P(), block,
            P("col", "row"),
        ),
        check_vma=False,
    )
```
